32 devices in a mesh: gx: 8 (over z, y), gy: 4 (over x, core).
Axes of the slice: x: 2, y: 2, z: 4, core: 2. Of those that a mesh axis runs over, the one named last changes fastest.
Arguments:
- point_feats: bfloat16 [32, 262144], P(None, ('gx', 'gy')), may hold values from -1 to 1
- point_targets: bfloat16 [262144], P(('gx', 'gy')), may hold values from -6 to 6
- point_lists: int32 [32768, 8], P(('gx', 'gy')), may hold values from -1 to 8191, as said below
- brick_adjacency: int32 [1024, 4], P(('gx', 'gy')), may hold values from -1 to 1023, as said below
- voxel_feats: float32 [1024, 32, 512], P(('gx', 'gy')), may hold values from -0.25 to 0.25
- voxel_reg: float32 [1024, 512], P(('gx', 'gy')), may hold values from 0.25 to 2
Outputs:
- solution: float32 [1024, 512], P(('gx', 'gy'))
- residual: float32 [1024, 512], P(('gx', 'gy'))
The draws below stay inside these ranges and needn't reach their ends.
Inputs may be any that keep to these rules, and one draw needn't show every extreme that they name: `point_lists`: row s * 1024 + b lists, in its first slots, distinct indices of the points of source device s in brick b, all within that device's rows b * 8 to b * 8 + 7, then -1 in the remaining slots. Point rows named by no list are unused. `brick_adjacency`: entry k of brick b is the lattice neighbour of b in direction k (minus along the road, plus along the road, minus across, plus across) or -1; the relation is symmetric and -1 wherever the neighbour lies outside the lattice.
All inputs are finite; a program needn't handle non-finite values.
Results may differ from the reference program's by a relative error of at most 0.0003.
Values may be sent and summed in bfloat16 or wider, within the bound.
A program may use at most 64 MiB of HBM per device.

```python
import math
import jax
import jax.numpy as jnp
from jax import lax

FEAT = 32
VOX = 512
BX = 8
BY = 4
CAPB = 8
ITERS = 3
BR_DEV = 32
NB = 1024
P_DEV = 8192
POINTS = 262144
LX = 64
LY = 16
N_GX = 8
N_GY = 4
DEVICES = 32


def draw_point_lists(key, part):
    devices = NB // BR_DEV
    key_counts, key_own, key_shared, key_perm = jax.random.split(jax.random.fold_in(key, 11), 4)
    owner = jnp.arange(NB, dtype=jnp.int32) // BR_DEV
    hottest = 4 + 20 * owner // max(devices - 1, 1)
    raw = jax.random.randint(key_counts, (devices, NB), 0, 1 << 20) % hottest[None, :]
    counts = jnp.minimum(raw, CAPB)
    own_pick = jax.random.randint(key_own, (devices,), 0, NB)
    counts = counts.at[jnp.arange(devices), own_pick].set(CAPB)
    shared = jax.random.randint(key_shared, (), 0, NB)
    counts = counts.at[:, shared].set(CAPB)
    counts = counts.at[:, NB - 1].set(CAPB)
    slot = jnp.arange(CAPB, dtype=jnp.int32)
    scores = jax.random.randint(key_perm, (devices, NB, CAPB), 0, 1 << 20) * CAPB + slot[None, None, :]
    order = jnp.argsort(scores, axis=-1).astype(jnp.int32)
    brick = jnp.arange(NB, dtype=jnp.int32)[None, :, None]
    listed = jnp.where(slot[None, None, :] < counts[:, :, None], brick * CAPB + order, -1)
    return listed.reshape(devices * NB, CAPB).astype(jnp.int32)


def draw_brick_adjacency(key, part):
    key_x, key_y = jax.random.split(jax.random.fold_in(key, 7))
    keep_x = jax.random.randint(key_x, (LX - 1, LY), 0, 4) > 0
    keep_y = jax.random.randint(key_y, (LX, LY - 1), 0, 4) > 0
    place_x = jnp.arange(LX, dtype=jnp.int32)[:, None]
    place_y = jnp.arange(LY, dtype=jnp.int32)[None, :]
    ident = (place_x // BX * (LY // BY) + place_y // BY) * BR_DEV + place_x % BX * BY + place_y % BY
    minus_x = jnp.where(jnp.pad(keep_x, ((1, 0), (0, 0))), jnp.pad(ident[:-1], ((1, 0), (0, 0))), -1)
    plus_x = jnp.where(jnp.pad(keep_x, ((0, 1), (0, 0))), jnp.pad(ident[1:], ((0, 1), (0, 0))), -1)
    minus_y = jnp.where(jnp.pad(keep_y, ((0, 0), (1, 0))), jnp.pad(ident[:, :-1], ((0, 0), (1, 0))), -1)
    plus_y = jnp.where(jnp.pad(keep_y, ((0, 0), (0, 1))), jnp.pad(ident[:, 1:], ((0, 0), (0, 1))), -1)
    lattice = jnp.stack([minus_x, plus_x, minus_y, plus_y], axis=-1)
    shaped = lattice.reshape(LX // BX, BX, LY // BY, BY, 4).transpose(0, 2, 1, 3, 4)
    return shaped.reshape(NB, 4).astype(jnp.int32)


def shard_levels(rng, extent, cuts, low, high):
    level = 1.0
    for position, parts in cuts:
        draws = jax.random.uniform(jax.random.fold_in(jax.random.fold_in(rng, 6), position), (parts,), jnp.float32, low / len(cuts), high / len(cuts))
        level = level * jnp.repeat(jnp.exp(draws), extent[position] // parts).reshape((-1,) + (1,) * (len(extent) - 1 - position))
    return level


def scatter_about(rng, extent, scale, limit, cuts=(), held_as=jnp.bfloat16):
    values = scale * jax.random.normal(rng, extent, jnp.float32)
    if cuts:
        values = values * shard_levels(rng, extent, cuts, -0.22, 0.18)
    return jnp.clip(values, -limit, limit).astype(held_as)


def setup_inputs(seed: int = 0) -> dict:
    arg_keys = jax.random.split(jax.random.key(seed), 7)
    return {
        "point_feats": scatter_about(arg_keys[0], (FEAT, POINTS), (DEVICES ** -0.5), 1.0, ((1, 32),)),
        "point_targets": scatter_about(arg_keys[1], (POINTS,), 1.0, 6.0, ((0, 32),)),
        "point_lists": draw_point_lists(jax.random.fold_in(arg_keys[6], 71), 0),
        "brick_adjacency": draw_brick_adjacency(jax.random.fold_in(arg_keys[6], 71), 0),
        "voxel_feats": scatter_about(arg_keys[4], (NB, FEAT, VOX), VOX ** -0.5, 0.25, ((0, 32),), jnp.float32),
        "voxel_reg": jnp.clip(jnp.exp(math.log(2.0) - 2.0794415 * jax.random.uniform(arg_keys[5], (NB, VOX), jnp.float32) ** shard_levels(arg_keys[5], (NB, VOX), ((0, 32),), -0.2, 0.2)), 0.25, 2.0),
    }


coupling_weight = 1.0


def to_lattice(values):
    width = values.shape[-1]
    shaped = values.reshape(N_GX, N_GY, BX, BY, width).transpose(0, 2, 1, 3, 4)
    return shaped.reshape(BX * N_GX, BY * N_GY, width)


def from_lattice(values):
    width = values.shape[-1]
    shaped = values.reshape(N_GX, BX, N_GY, BY, width).transpose(0, 2, 1, 3, 4)
    return shaped.reshape(BR_DEV * N_GX * N_GY, width)


def neighbour_sum(lattice, mask):
    padded = jnp.pad(lattice, ((1, 1), (1, 1), (0, 0)))
    total = mask[..., 0:1] * padded[:-2, 1:-1] + mask[..., 1:2] * padded[2:, 1:-1]
    return total + mask[..., 2:3] * padded[1:-1, :-2] + mask[..., 3:4] * padded[1:-1, 2:]


def reference(point_feats, point_targets, point_lists, brick_adjacency, voxel_feats, voxel_reg):
    devices = N_GX * N_GY
    lists = point_lists.reshape(devices, NB, CAPB)
    base = (jnp.arange(devices, dtype=jnp.int32) * P_DEV)[:, None, None]

    def one_owner(owner):
        rows = lax.dynamic_slice_in_dim(lists, (owner * BR_DEV).astype(jnp.int32), BR_DEV, 1)
        live = rows >= 0
        index = (jnp.where(live, rows, 0) + base).reshape(-1)
        feats = jnp.take(point_feats, index, axis=1).astype(jnp.float32).reshape(FEAT, devices, BR_DEV, CAPB)
        feats = jnp.where(live[None], feats, jnp.zeros((), jnp.float32))
        target = jnp.take(point_targets, index).astype(jnp.float32).reshape(live.shape)
        target = jnp.where(live, target, jnp.zeros((), jnp.float32))
        moment = jnp.einsum("isbc,jsbc->bij", feats, feats, precision=lax.Precision.HIGHEST)
        gathered = jnp.einsum("sbc,isbc->bi", target, feats, precision=lax.Precision.HIGHEST)
        return moment, gathered

    moments, gathered = lax.map(one_owner, jnp.arange(devices, dtype=jnp.int32))
    moments = moments.reshape(NB, FEAT, FEAT)
    gathered = gathered.reshape(NB, FEAT)
    mask = to_lattice((brick_adjacency >= 0).astype(jnp.float32))
    degree = jnp.sum(mask, axis=-1, keepdims=True)

    def operate(vector):
        projected = jnp.einsum("bik,bk->bi", voxel_feats, vector, precision=lax.Precision.HIGHEST)
        lattice = to_lattice(projected)
        coupled = from_lattice(degree * lattice - neighbour_sum(lattice, mask))
        middle = jnp.einsum("bij,bj->bi", moments, projected, precision=lax.Precision.HIGHEST)
        middle = middle + coupling_weight * coupled
        back = jnp.einsum("bik,bi->bk", voxel_feats, middle, precision=lax.Precision.HIGHEST)
        return back + voxel_reg * vector

    rhs = jnp.einsum("bik,bi->bk", voxel_feats, gathered, precision=lax.Precision.HIGHEST)
    solution = jnp.zeros_like(rhs)
    residual, direction = rhs, rhs
    norm_now = jnp.sum(residual * residual)
    for iteration in range(ITERS):
        image = operate(direction)
        alpha = norm_now / jnp.sum(direction * image)
        solution = solution + alpha * direction
        residual = residual - alpha * image
        norm_next = jnp.sum(residual * residual)
        direction = residual + (norm_next / norm_now) * direction
        norm_now = norm_next
    return solution, residual
```

```python
import functools
import math

import jax
import jax.numpy as jnp
from jax import lax
from jax.experimental import pallas as pl
from jax.experimental.pallas import tpu as pltpu
from jax.sharding import PartitionSpec as P

BX = 8
BY = 4
ITERS = 3
LANES = 128
CHUNK = 8
MESH = pl.DeviceIdType.MESH
STRIDE = 11
SCALE = 2.0**-8
SHIFTS = (8.0, 1.0, 4.0)

coupling_weight = 1.0


def kernel(
    gx,
    gy,
    feats_hbm,
    target_hbm,
    lists_hbm,
    adjacency_hbm,
    voxel_hbm,
    reg_hbm,
    answer_ref,
    res_ref,
    direction_ref,
    image_ref,
    alpha_ref,
    got,
    got_extra,
    extra,
    flat,
    voxel,
    acc,
    square,
    basis,
    z_ref,
    q_ref,
    my_ref,
    mid_ref,
    ym_ref,
    yp_ref,
    y_send,
    halo,
    part,
    parts,
    target_ref,
    lists_ref,
    adjacency_ref,
    reg_ref,
    voxel_sem,
    input_sem,
    feat_send,
    feat_recv,
    extra_send,
    extra_recv,
    halo_send,
    halo_recv,
    part_send,
    part_recv,
):
    count = gx * gy
    ix, iy = lax.axis_index("gx"), lax.axis_index("gy")
    me = ix * gy + iy
    feat, cols = got.shape[1], got.shape[2]
    bricks = reg_ref.shape[0]
    slots = cols // bricks
    halves = cols // LANES
    per_half = LANES // slots

    step_by = STRIDE if math.gcd(STRIDE, count) == 1 else 1

    def place(index):
        return (index // gy, index % gy)

    barrier = pltpu.get_barrier_semaphore()

    def greet(j, _):
        pl.semaphore_signal(
            barrier, inc=1, device_id=place((me + j * step_by) % count), device_id_type=MESH
        )
        return 0

    lax.fori_loop(1, count, greet, 0, unroll=True)
    inputs = [
        pltpu.make_async_copy(source, target, input_sem.at[e])
        for e, (source, target) in enumerate(
            [
                (lists_hbm, lists_ref),
                (target_hbm, target_ref),
                (reg_hbm, reg_ref),
                (adjacency_hbm, adjacency_ref),
            ]
        )
    ]
    for copy in inputs:
        copy.start()
    voxel_copy = pltpu.make_async_copy(voxel_hbm, voxel, voxel_sem)
    voxel_copy.start()
    halo[...] = jnp.zeros_like(halo)
    acc[...] = jnp.zeros_like(acc)
    own_feat = pltpu.make_async_copy(
        feats_hbm.at[:, pl.ds(pl.multiple_of(me * cols, cols), cols)], got.at[me], feat_recv.at[me]
    )
    own_extra = pltpu.make_async_copy(extra.at[me], got_extra.at[me], extra_recv.at[me])
    own_feat.start()

    total_bricks = lists_ref.shape[1]
    groups = total_bricks // LANES
    wide = slots * LANES
    inputs[0].wait()
    listed = lists_ref[...]
    offset = listed - slots * lax.broadcasted_iota(jnp.int32, listed.shape, 1)
    offset = jnp.where(listed >= 0, offset, -1)
    hits = jnp.concatenate(
        [
            jnp.max(jnp.where(offset == d, 1.0, 0.0), axis=0, keepdims=True)
            for d in range(slots)
        ],
        axis=0,
    )
    hits = jnp.concatenate(
        [hits[:, g * LANES : (g + 1) * LANES] for g in range(groups)], axis=0
    ).astype(jnp.bfloat16)
    spread = jnp.where(
        lax.broadcasted_iota(jnp.int32, (LANES, wide), 1) // slots
        == lax.broadcasted_iota(jnp.int32, (LANES, wide), 0),
        1.0,
        0.0,
    ).astype(jnp.bfloat16)
    spread_hits = jnp.dot(hits, spread, preferred_element_type=jnp.float32)
    same = (
        lax.broadcasted_iota(jnp.int32, (slots, wide), 1) % slots
        == lax.broadcasted_iota(jnp.int32, (slots, wide), 0)
    )
    live_rows = jnp.sum(
        jnp.where(same[None], spread_hits.reshape(groups, slots, wide), 0.0), axis=1
    )
    for l in range(slots):
        flat[pl.ds(l, groups, stride=slots), :] = live_rows[:, l * LANES : (l + 1) * LANES]
    inputs[1].wait()
    targets = target_ref[...].astype(jnp.float32)
    for k in range(count):
        rows = slice(k * halves, (k + 1) * halves)
        extra[k] = jnp.concatenate([flat[rows, :], targets[rows]], axis=0).astype(jnp.bfloat16)
    own_extra.start()
    pl.semaphore_wait(barrier, count - 1)

    def feat_copy(to, frm):
        return pltpu.make_async_remote_copy(
            src_ref=feats_hbm.at[:, pl.ds(pl.multiple_of(to * cols, cols), cols)],
            dst_ref=got.at[frm],
            send_sem=feat_send.at[to],
            recv_sem=feat_recv.at[frm],
            device_id=place(to),
            device_id_type=MESH,
        )

    def extra_copy(to, frm):
        return pltpu.make_async_remote_copy(
            src_ref=extra.at[to],
            dst_ref=got_extra.at[frm],
            send_sem=extra_send.at[to],
            recv_sem=extra_recv.at[frm],
            device_id=place(to),
            device_id_type=MESH,
        )

    def send(j, _):
        to = (me + j * step_by) % count
        feat_copy(to, me).start()
        extra_copy(to, me).start()
        return 0

    lax.fori_loop(1, count, send, 0)
    voxel_copy.wait()
    inputs[2].wait()
    inputs[3].wait()
    square[...] = jnp.zeros_like(square)

    def squares(t, _):
        for u in range(4):
            b = t * 4 + u
            rows = pl.ds(pl.multiple_of(b * feat, feat), feat)
            square[rows, 0:feat] = lax.dot_general(
                voxel[b],
                voxel[b],
                (((1,), (1,)), ((), ())),
                precision=lax.Precision.HIGHEST,
                preferred_element_type=jnp.float32,
            )
        return 0

    lax.fori_loop(0, bricks // 4, squares, 0)
    own_feat.wait()
    own_extra.wait()

    group = 4
    while count % group:
        group //= 2
    lane = lax.broadcasted_iota(jnp.int32, (1, group * LANES), 1)
    owner = (lane // slots) % per_half

    def absorb(g, _):
        sources = []
        for u in range(group):
            j = g * group + u
            source = (me + (count - j) * step_by) % count
            sources.append(source)
            if u:
                feat_copy(source, source).wait_recv()
                extra_copy(source, source).wait_recv()
            else:

                @pl.when(g > 0)
                def _():
                    feat_copy(source, source).wait_recv()
                    extra_copy(source, source).wait_recv()

        for h in range(halves):
            span = slice(h * LANES, (h + 1) * LANES)
            x = jnp.concatenate([got[s, :, span] for s in sources], axis=1)
            more = jnp.concatenate(
                [got_extra[s].astype(jnp.float32) for s in sources], axis=1
            )
            live = more[h : h + 1]
            target = more[halves + h : halves + h + 1].astype(jnp.bfloat16)
            left = jnp.concatenate(
                [x * jnp.where(owner == b, live, 0.0).astype(jnp.bfloat16) for b in range(per_half)],
                axis=0,
            )
            right = jnp.concatenate(
                [
                    x,
                    jnp.broadcast_to(target, (16, group * LANES)),
                    jnp.zeros((LANES - feat - 16, group * LANES), jnp.bfloat16),
                ],
                axis=0,
            )
            rows = slice(h * per_half * feat, (h + 1) * per_half * feat)
            acc[rows, :] += lax.dot_general(
                left, right, (((1,), (1,)), ((), ())), preferred_element_type=jnp.float32
            )
        return 0

    lax.fori_loop(0, count // group, absorb, 0)

    eye = lax.broadcasted_iota(jnp.int32, (1, feat, LANES), 1) == lax.broadcasted_iota(
        jnp.int32, (1, feat, LANES), 2
    )
    chunks = bricks // CHUNK
    in_feat = lax.broadcasted_iota(jnp.int32, (bricks, LANES), 1) < feat

    def at(t):
        return pl.ds(pl.multiple_of(t * CHUNK, CHUNK), CHUNK)

    def block(ref, t):
        rows = pl.ds(pl.multiple_of(t * CHUNK * feat, CHUNK * feat), CHUNK * feat)
        return ref[rows, :].reshape(CHUNK, feat, LANES)

    def as_column(rows):
        return jnp.sum(jnp.where(eye, rows[:, None, :], 0.0), axis=2, keepdims=True)

    def gathered(t):
        return block(acc, t)[:, :, feat : feat + 1]

    def begin(t, _):
        z_ref[0, at(t), :] = jnp.sum(block(square, t) * gathered(t), axis=1)
        return 0

    lax.fori_loop(0, chunks, begin, 0, unroll=True)

    linked = jnp.where(adjacency_ref[...] >= 0, 1.0, 0.0)
    same_brick = lax.broadcasted_iota(jnp.int32, (bricks, bricks), 0) == lax.broadcasted_iota(
        jnp.int32, (bricks, bricks), 1
    )
    weights = [
        jnp.sum(jnp.where(same_brick, linked[k : k + 1], 0.0), axis=1, keepdims=True)
        for k in range(4)
    ]
    masks = [w > 0.0 for w in weights]
    degree = weights[0] + weights[1] + weights[2] + weights[3]
    here = [ix > 0, ix < gx - 1, iy > 0, iy < gy - 1]
    beside = [(ix - 1, iy), (ix + 1, iy), (ix, iy - 1), (ix, iy + 1)]

    def halo_copy(step, k):
        if k < 2:
            source = z_ref.at[step, pl.ds(k * (bricks - 8), 8)]
        else:
            source = y_send.at[step, k - 2]
        return pltpu.make_async_remote_copy(
            src_ref=source,
            dst_ref=halo.at[step, k ^ 1],
            send_sem=halo_send.at[step, k],
            recv_sem=halo_recv.at[step, k ^ 1],
            device_id=beside[k],
            device_id_type=MESH,
        )

    def halo_arrived(step, k):
        return pltpu.make_async_remote_copy(
            src_ref=y_send.at[step, 0],
            dst_ref=halo.at[step, k],
            send_sem=halo_send.at[step, k],
            recv_sem=halo_recv.at[step, k],
            device_id=beside[k],
            device_id_type=MESH,
        )

    def part_copy(to, frm):
        return pltpu.make_async_remote_copy(
            src_ref=part,
            dst_ref=parts.at[frm],
            send_sem=part_send.at[to],
            recv_sem=part_recv.at[frm],
            device_id=place(to),
            device_id_type=MESH,
        )

    def fold(values):
        total = jnp.sum(values, axis=0, keepdims=True)
        width = total.shape[1]
        return sum(total[:, c : c + LANES] for c in range(0, width, LANES))

    def next_basis(step, t):
        if step == 0:
            return jnp.sum(voxel[at(t)] * gathered(t), axis=1)
        back = jnp.sum(voxel[at(t)] * as_column(mid_ref[at(t), :]), axis=1)
        shifted = (reg_ref[at(t), :] - SHIFTS[step - 1]) * basis[step - 1, at(t), :]
        return SCALE * (back + shifted)

    def operate(step):
        for e in range(2):
            y_send[step, e] = z_ref[step, pl.ds(e * (BY - 1), BX, stride=BY), :]
        for k in range(4):

            @pl.when(here[k])
            def _():
                halo_copy(step, k).start()

        def widen(t, _):
            made = next_basis(step, t)
            basis[step, at(t), :] = made
            if step + 1 < ITERS:
                weighted = reg_ref[at(t), :] * made
                column = jnp.sum(voxel[at(t)] * weighted[:, None, :], axis=2, keepdims=True)
                q_ref[at(t), :] = jnp.sum(jnp.where(eye, column, 0.0), axis=1)
            my_ref[at(t), :] = jnp.sum(block(acc, t) * as_column(z_ref[step, at(t), :]), axis=1)
            return 0

        lax.fori_loop(0, chunks, widen, 0)
        z = z_ref[step]
        ym_ref[1:bricks, :] = z[: bricks - 1]
        yp_ref[0 : bricks - 1, :] = z[1:]
        found = []
        if step + 1 == ITERS:
            found = [fold(basis[a] * basis[b]) for a, b in early]
            final = (reg_ref[...] - SHIFTS[step]) * basis[step]
            found = found + [fold(basis[a] * final) for a, b in late]
        for k in range(4):

            @pl.when(here[k])
            def _():
                halo_arrived(step, k).wait_recv()

        xm = jnp.concatenate([halo[step, 0][8 - BY :], z[: bricks - BY]], axis=0)
        xp = jnp.concatenate([z[BY:], halo[step, 1][:BY]], axis=0)
        ym_ref[pl.ds(0, BX, stride=BY), :] = halo[step, 2]
        yp_ref[pl.ds(BY - 1, BX, stride=BY), :] = halo[step, 3]
        near = jnp.where(masks[0], xm, 0.0) + jnp.where(masks[1], xp, 0.0)
        near = near + jnp.where(masks[2], ym_ref[...], 0.0) + jnp.where(masks[3], yp_ref[...], 0.0)
        mid = jnp.where(in_feat, my_ref[...] + coupling_weight * (degree * z - near), 0.0)
        mid_ref[...] = mid

        if step + 1 < ITERS:

            def advance(t, _):
                back = jnp.sum(block(square, t) * as_column(mid_ref[at(t), :]), axis=1)
                shifted = q_ref[at(t), :] - SHIFTS[step] * z_ref[step, at(t), :]
                z_ref[step + 1, at(t), :] = SCALE * (back + shifted)
                return 0

            lax.fori_loop(0, chunks, advance, 0, unroll=True)
        else:
            for e, (a, b) in enumerate(late):
                e += len(early)
                found[e] = SCALE * (found[e] + fold(z_ref[a] * mid))
        return found

    early = [(a, b) for a in range(ITERS) for b in range(a, ITERS)]
    late = [(a, ITERS) for a in range(ITERS)]
    pairs = early + late
    rows = []
    for step in range(ITERS):
        rows = operate(step)
    rows = rows + [jnp.zeros_like(rows[0])] * (-len(rows) % 8)
    sums = jnp.sum(jnp.concatenate(rows, axis=0), axis=1, keepdims=True)
    entry = lax.broadcasted_iota(jnp.int32, (len(rows), LANES), 1)
    diagonal = entry == lax.broadcasted_iota(jnp.int32, (len(rows), LANES), 0)
    mine = jnp.sum(jnp.where(diagonal, sums, 0.0), axis=0, keepdims=True)
    part[...] = mine
    parts[me] = mine

    def start(j, _):
        part_copy((me + j * step_by) % count, me).start()
        return 0

    lax.fori_loop(1, count, start, 0, unroll=True)

    def last(t, _):
        basis[ITERS, at(t), :] = next_basis(ITERS, t)
        return 0

    lax.fori_loop(0, chunks, last, 0)

    def finish(j, _):
        source = (me + (count - j) * step_by) % count
        part_copy(source, source).wait_recv()
        return 0

    lax.fori_loop(1, count, finish, 0)
    total = jnp.sum(parts[...], axis=0)
    spread_total = jnp.sum(
        jnp.where(diagonal, jnp.broadcast_to(total, diagonal.shape), 0.0), axis=1, keepdims=True
    )
    gram = {}
    for e, (a, b) in enumerate(pairs):
        gram[a, b] = gram[b, a] = spread_total[e : e + 1]

    def inner(left, right):
        terms = [
            left[a] * right[b] * gram[a, b] for a in range(len(left)) for b in range(len(right))
        ]
        return functools.reduce(lambda p, q: p + q, terms)

    def apply(coefficients):
        size = len(coefficients)
        out = [SHIFTS[k] * coefficients[k] for k in range(size)]
        out.append(coefficients[-1] * (1.0 / SCALE))
        for k in range(1, size):
            out[k] = out[k] + coefficients[k - 1] * (1.0 / SCALE)
        return out

    one = jnp.ones((1, 1), jnp.float32)
    res, direction, answer = [one], [one], []
    norm_now = gram[0, 0]
    for step in range(ITERS):
        before_answer, before_res = answer, res
        image = apply(direction)
        alpha = norm_now / inner(direction, image)
        padded = answer + [jnp.zeros_like(one)] * (len(direction) - len(answer))
        answer = [p + alpha * d for p, d in zip(padded, direction)]
        res = [p - alpha * w for p, w in zip(res + [jnp.zeros_like(one)], image)]
        if step + 1 < ITERS:
            norm_next = inner(res, res)
            ratio = norm_next / norm_now
            direction = [
                p + ratio * d for p, d in zip(res, direction + [jnp.zeros_like(one)])
            ]
            norm_now = norm_next
    def combine(coefficients):
        return functools.reduce(
            lambda p, q: p + q, [c * basis[k] for k, c in enumerate(coefficients)]
        )

    answer_ref[...] = combine(before_answer)
    res_ref[...] = combine(before_res)
    direction_ref[...] = combine(direction)
    image_ref[...] = combine(image)
    alpha_ref[...] = jnp.broadcast_to(alpha, alpha_ref.shape)

    def drain(j, _):
        to = (me + j * step_by) % count
        feat_copy(to, me).wait_send()
        extra_copy(to, me).wait_send()
        part_copy(to, me).wait_send()
        return 0

    lax.fori_loop(1, count, drain, 0)
    for step in range(ITERS):
        for k in range(4):

            @pl.when(here[k])
            def _():
                halo_copy(step, k).wait_send()


def shards(gx, gy, point_feats, point_targets, point_lists, brick_adjacency, voxel_feats, voxel_reg):
    feat = point_feats.shape[0]
    brick_total, slots = point_lists.shape
    bricks, _, vox = voxel_feats.shape
    count = gx * gy
    cols = bricks * slots
    vmem = pl.BlockSpec(memory_space=pltpu.VMEM)
    hbm = pl.BlockSpec(memory_space=pltpu.HBM)
    f32 = jnp.float32
    answer, res, direction, image, alpha = pl.pallas_call(
        functools.partial(kernel, gx, gy),
        out_shape=(pltpu.VMEM((bricks, vox), f32),) * 4 + (pltpu.VMEM((1, vox), f32),),
        in_specs=[hbm] * 6,
        out_specs=(vmem,) * 5,
        scratch_shapes=[
            pltpu.VMEM((count, feat, cols), jnp.bfloat16),
            pltpu.VMEM((count, 2 * cols // LANES, LANES), jnp.bfloat16),
            pltpu.VMEM((count, 2 * cols // LANES, LANES), jnp.bfloat16),
            pltpu.VMEM((count * cols // LANES, LANES), f32),
            pltpu.VMEM((bricks, feat, vox), f32),
            pltpu.VMEM((bricks * feat, LANES), f32),
            pltpu.VMEM((bricks * feat, LANES), f32),
            pltpu.VMEM((ITERS + 1, bricks, vox), f32),
            pltpu.VMEM((ITERS, bricks, LANES), f32),
            pltpu.VMEM((bricks, LANES), f32),
            pltpu.VMEM((bricks, LANES), f32),
            pltpu.VMEM((bricks, LANES), f32),
            pltpu.VMEM((bricks, LANES), f32),
            pltpu.VMEM((bricks, LANES), f32),
            pltpu.VMEM((ITERS, 2, BX, LANES), f32),
            pltpu.VMEM((ITERS, 4, 8, LANES), f32),
            pltpu.VMEM((1, LANES), f32),
            pltpu.VMEM((count, 1, LANES), f32),
            pltpu.VMEM((count * cols // LANES, LANES), point_targets.dtype),
            pltpu.VMEM((slots, brick_total), jnp.int32),
            pltpu.VMEM((4, bricks), jnp.int32),
            pltpu.VMEM((bricks, vox), f32),
            pltpu.SemaphoreType.DMA,
            pltpu.SemaphoreType.DMA((4,)),
            pltpu.SemaphoreType.DMA((count,)),
            pltpu.SemaphoreType.DMA((count,)),
            pltpu.SemaphoreType.DMA((count,)),
            pltpu.SemaphoreType.DMA((count,)),
            pltpu.SemaphoreType.DMA((ITERS, 4)),
            pltpu.SemaphoreType.DMA((ITERS, 4)),
            pltpu.SemaphoreType.DMA((count,)),
            pltpu.SemaphoreType.DMA((count,)),
        ],
        compiler_params=pltpu.CompilerParams(collective_id=0, has_side_effects=True, vmem_limit_bytes=16 * 1024 * 1024),
    )(
        *(
            pltpu.with_memory_space_constraint(x, pltpu.HBM)
            for x in (
                point_feats,
                point_targets.reshape(-1, LANES),
                point_lists.T,
                brick_adjacency.T,
                voxel_feats,
                voxel_reg,
            )
        )
    )
    return answer + alpha * direction, res - alpha * image


def solution(mesh):
    placed = (
        P(None, ("gx", "gy")),
        P(("gx", "gy")),
        P(("gx", "gy"), None),
        P(("gx", "gy"), None),
        P(("gx", "gy"), None, None),
        P(("gx", "gy"), None),
    )
    return jax.shard_map(
        functools.partial(shards, mesh.shape["gx"], mesh.shape["gy"]),
        mesh=mesh,
        in_specs=placed,
        out_specs=(P(("gx", "gy"), None), P(("gx", "gy"), None)),
        check_vma=False,
    )
```

```python
import functools
import math

import jax
import jax.numpy as jnp
from jax import lax
from jax.experimental import pallas as pl
from jax.experimental.pallas import tpu as pltpu
from jax.sharding import PartitionSpec as P

BX = 8
BY = 4
ITERS = 3
LANES = 128
CHUNK = 8
MESH = pl.DeviceIdType.MESH
STRIDE = 11
SCALE = 2.0**-8
AHEAD = 8
SHIFTS = (8.0, 1.0, 4.0)

coupling_weight = 1.0


def kernel(
    gx,
    gy,
    feats_hbm,
    target_hbm,
    lists_hbm,
    adjacency_hbm,
    voxel_hbm,
    reg_hbm,
    answer_ref,
    res_ref,
    direction_ref,
    image_ref,
    alpha_ref,
    got,
    got_extra,
    extra,
    flat,
    voxel,
    acc,
    gather,
    mz_ref,
    g_ref,
    square,
    basis,
    z_ref,
    q_ref,
    my_ref,
    mid_ref,
    ym_ref,
    yp_ref,
    y_send,
    halo,
    part,
    parts,
    target_ref,
    lists_ref,
    adjacency_ref,
    reg_ref,
    voxel_sem,
    input_sem,
    feat_send,
    feat_recv,
    extra_send,
    extra_recv,
    halo_send,
    halo_recv,
    part_send,
    part_recv,
):
    count = gx * gy
    ix, iy = lax.axis_index("gx"), lax.axis_index("gy")
    me = ix * gy + iy
    feat, cols = got.shape[1], got.shape[2]
    bricks = reg_ref.shape[0]
    slots = cols // bricks
    halves = cols // LANES
    per_half = LANES // slots
    side = LANES // feat
    tall = per_half // side

    step_by = STRIDE if math.gcd(STRIDE, count) == 1 else 1

    def place(index):
        return (index // gy, index % gy)

    def at_offset(j):
        return (me + j * step_by) % count

    def columns(index):
        return pl.ds(pl.multiple_of(index * cols, cols), cols)

    barrier = pltpu.get_barrier_semaphore()

    def greet(j, _):
        pl.semaphore_signal(barrier, inc=1, device_id=place(at_offset(j)), device_id_type=MESH)
        return 0

    lax.fori_loop(1, count, greet, 0, unroll=True)
    inputs = [
        pltpu.make_async_copy(source, target, input_sem.at[e])
        for e, (source, target) in enumerate(
            [
                (lists_hbm, lists_ref),
                (target_hbm, target_ref),
                (reg_hbm, reg_ref),
                (adjacency_hbm, adjacency_ref),
            ]
        )
    ]
    for copy in inputs:
        copy.start()
    voxel_copy = pltpu.make_async_copy(voxel_hbm, voxel, voxel_sem)
    voxel_copy.start()
    own_feat = pltpu.make_async_copy(feats_hbm.at[:, columns(me)], got.at[0], feat_recv.at[0])
    own_feat.start()
    halo[...] = jnp.zeros_like(halo)
    acc[...] = jnp.zeros_like(acc)
    gather[...] = jnp.zeros_like(gather)

    def feat_copy(j):
        to = at_offset(j)
        return pltpu.make_async_remote_copy(
            src_ref=feats_hbm.at[:, columns(to)],
            dst_ref=got.at[j],
            send_sem=feat_send.at[0],
            recv_sem=feat_recv.at[j // group],
            device_id=place(to),
            device_id_type=MESH,
        )

    def extra_copy(j):
        to = at_offset(j)
        return pltpu.make_async_remote_copy(
            src_ref=extra.at[to],
            dst_ref=got_extra.at[j],
            send_sem=extra_send.at[0],
            recv_sem=extra_recv.at[j // group],
            device_id=place(to),
            device_id_type=MESH,
        )

    group = count // feat_recv.shape[0]
    ahead = min(AHEAD, count)
    pl.semaphore_wait(barrier, count - 1)
    for j in range(1, ahead):
        feat_copy(j).start()

    total_bricks = lists_ref.shape[1]
    groups = total_bricks // LANES
    wide = slots * LANES
    inputs[0].wait()
    listed = lists_ref[...]
    offset = listed - slots * lax.broadcasted_iota(jnp.int32, listed.shape, 1)
    offset = jnp.where(listed >= 0, offset, -1)
    hits = jnp.concatenate(
        [
            jnp.max(jnp.where(offset == d, 1.0, 0.0), axis=0, keepdims=True)
            for d in range(slots)
        ],
        axis=0,
    )
    hits = jnp.concatenate(
        [hits[:, g * LANES : (g + 1) * LANES] for g in range(groups)], axis=0
    ).astype(jnp.bfloat16)
    spread = jnp.where(
        lax.broadcasted_iota(jnp.int32, (LANES, wide), 1) // slots
        == lax.broadcasted_iota(jnp.int32, (LANES, wide), 0),
        1.0,
        0.0,
    ).astype(jnp.bfloat16)
    spread_hits = jnp.dot(hits, spread, preferred_element_type=jnp.float32)
    same = (
        lax.broadcasted_iota(jnp.int32, (slots, wide), 1) % slots
        == lax.broadcasted_iota(jnp.int32, (slots, wide), 0)
    )
    live_rows = jnp.sum(
        jnp.where(same[None], spread_hits.reshape(groups, slots, wide), 0.0), axis=1
    )
    for l in range(slots):
        flat[pl.ds(l, groups, stride=slots), :] = live_rows[:, l * LANES : (l + 1) * LANES]
    inputs[1].wait()
    targets = target_ref[...].astype(jnp.float32)
    for k in range(count):
        rows = slice(k * halves, (k + 1) * halves)
        extra[k] = jnp.concatenate([flat[rows, :], targets[rows]], axis=0).astype(jnp.bfloat16)
    own_extra = pltpu.make_async_copy(extra.at[me], got_extra.at[0], extra_recv.at[0])
    own_extra.start()
    for j in range(1, ahead):
        extra_copy(j).start()

    def send(j, _):
        feat_copy(j).start()
        extra_copy(j).start()
        return 0

    lax.fori_loop(ahead, count, send, 0, unroll=True)
    voxel_copy.wait()
    inputs[2].wait()
    inputs[3].wait()
    square[...] = jnp.zeros_like(square)

    def squares(t, _):
        for u in range(4):
            b = t * 4 + u
            rows = pl.ds(pl.multiple_of(b * feat, feat), feat)
            square[rows, 0:feat] = lax.dot_general(
                voxel[b],
                voxel[b],
                (((1,), (1,)), ((), ())),
                precision=lax.Precision.HIGHEST,
                preferred_element_type=jnp.float32,
            )
        return 0

    lax.fori_loop(0, bricks // 4, squares, 0)

    span_all = group * LANES
    owner = (lax.broadcasted_iota(jnp.int32, (1, span_all), 1) // slots) % per_half
    across = [jnp.where(owner % side == j, 1.0, 0.0).astype(jnp.bfloat16) for j in range(side)]
    along = owner // side == lax.broadcasted_iota(jnp.int32, (16, span_all), 0)

    def arrived(ref, sems, g):
        part_of = ref.at[pl.ds(g * group, group)]
        return pltpu.make_async_remote_copy(
            src_ref=part_of,
            dst_ref=part_of,
            send_sem=feat_send.at[0],
            recv_sem=sems.at[g],
            device_id=place(at_offset(1)),
            device_id_type=MESH,
        )

    def absorb(g, _):
        arrived(got, feat_recv, g).wait_recv()
        arrived(got_extra, extra_recv, g).wait_recv()
        more = jnp.concatenate(
            [got_extra[g * group + u].astype(jnp.float32) for u in range(group)], axis=1
        )
        for h in range(halves):
            span = slice(h * LANES, (h + 1) * LANES)
            x = jnp.concatenate([got[g * group + u, :, span] for u in range(group)], axis=1)
            live = jnp.where(along, more[h : h + 1], 0.0)
            marked = live * more[halves + h : halves + h + 1]
            left = jnp.concatenate(
                [x * live[i : i + 1].astype(jnp.bfloat16) for i in range(tall)]
                + [marked.astype(jnp.bfloat16)],
                axis=0,
            )
            right = jnp.concatenate([x * mask for mask in across], axis=0)
            found = lax.dot_general(
                left, right, (((1,), (1,)), ((), ())), preferred_element_type=jnp.float32
            )
            acc[h * LANES : (h + 1) * LANES, :] += found[:LANES]
            gather[h * tall : (h + 1) * tall, :] += found[LANES : LANES + tall]
        return 0

    lax.fori_loop(0, count // group, absorb, 0)

    def unpack(ref, rows):
        for e in range(side):
            turned = rows if e == 0 else pltpu.roll(rows, LANES - e * feat, 1)
            ref[pl.ds(e, bricks // side, stride=side), :] = turned

    unpack(g_ref, gather[...])

    eye = lax.broadcasted_iota(jnp.int32, (1, feat, LANES), 1) == lax.broadcasted_iota(
        jnp.int32, (1, feat, LANES), 2
    )
    chunks = bricks // CHUNK
    in_feat = lax.broadcasted_iota(jnp.int32, (bricks, LANES), 1) < feat

    def at(t):
        return pl.ds(pl.multiple_of(t * CHUNK, CHUNK), CHUNK)

    def block(ref, t):
        rows = pl.ds(pl.multiple_of(t * CHUNK * feat, CHUNK * feat), CHUNK * feat)
        return ref[rows, :].reshape(CHUNK, feat, LANES)

    def as_column(rows):
        return jnp.sum(jnp.where(eye, rows[:, None, :], 0.0), axis=2, keepdims=True)

    def gathered(t):
        return as_column(g_ref[at(t), :])

    lane_block = lax.broadcasted_iota(jnp.int32, (1, 1, LANES), 2) // feat

    def moments_times(step):
        for t in range(chunks):
            z_column = as_column(z_ref[step, at(t), :]).reshape(CHUNK // side, side, feat, 1)
            spread_column = z_column[:, 0]
            for e in range(1, side):
                spread_column = jnp.where(lane_block == e, z_column[:, e], spread_column)
            rows = CHUNK // side * feat
            packed = acc[t * rows : (t + 1) * rows, :].reshape(CHUNK // side, feat, LANES)
            mz_ref[t * (CHUNK // side) : (t + 1) * (CHUNK // side), :] = jnp.sum(
                packed * spread_column, axis=1
            )
        unpack(my_ref, mz_ref[...])

    def begin(t, _):
        z_ref[0, at(t), :] = jnp.sum(block(square, t) * gathered(t), axis=1)
        return 0

    lax.fori_loop(0, chunks, begin, 0, unroll=True)

    linked = jnp.where(adjacency_ref[...] >= 0, 1.0, 0.0)
    same_brick = lax.broadcasted_iota(jnp.int32, (bricks, bricks), 0) == lax.broadcasted_iota(
        jnp.int32, (bricks, bricks), 1
    )
    weights = [
        jnp.sum(jnp.where(same_brick, linked[k : k + 1], 0.0), axis=1, keepdims=True)
        for k in range(4)
    ]
    masks = [w > 0.0 for w in weights]
    degree = weights[0] + weights[1] + weights[2] + weights[3]
    here = [ix > 0, ix < gx - 1, iy > 0, iy < gy - 1]
    beside = [(ix - 1, iy), (ix + 1, iy), (ix, iy - 1), (ix, iy + 1)]

    def halo_copy(step, k):
        if k < 2:
            source = z_ref.at[step, pl.ds(k * (bricks - 8), 8)]
        else:
            source = y_send.at[step, k - 2]
        return pltpu.make_async_remote_copy(
            src_ref=source,
            dst_ref=halo.at[step, k ^ 1],
            send_sem=halo_send.at[k],
            recv_sem=halo_recv.at[step % 2, k ^ 1],
            device_id=beside[k],
            device_id_type=MESH,
        )

    def halo_arrived(step, k):
        return pltpu.make_async_remote_copy(
            src_ref=y_send.at[step, 0],
            dst_ref=halo.at[step, k],
            send_sem=halo_send.at[k],
            recv_sem=halo_recv.at[step % 2, k],
            device_id=beside[k],
            device_id_type=MESH,
        )

    def part_copy(j):
        return pltpu.make_async_remote_copy(
            src_ref=part,
            dst_ref=parts.at[j],
            send_sem=part_send.at[0],
            recv_sem=part_recv.at[0],
            device_id=place(at_offset(j)),
            device_id_type=MESH,
        )

    def all_of(ref, send_sem, recv_sem):
        whole = ref.at[pl.ds(1, count - 1)]
        return pltpu.make_async_remote_copy(
            src_ref=whole,
            dst_ref=whole,
            send_sem=send_sem.at[0],
            recv_sem=recv_sem.at[0],
            device_id=place(at_offset(1)),
            device_id_type=MESH,
        )

    def fold(values):
        total = jnp.sum(values, axis=0, keepdims=True)
        width = total.shape[1]
        return sum(total[:, c : c + LANES] for c in range(0, width, LANES))

    def next_basis(step, t):
        if step == 0:
            return jnp.sum(voxel[at(t)] * gathered(t), axis=1)
        back = jnp.sum(voxel[at(t)] * as_column(mid_ref[at(t), :]), axis=1)
        shifted = (reg_ref[at(t), :] - SHIFTS[step - 1]) * basis[step - 1, at(t), :]
        return SCALE * (back + shifted)

    def operate(step):
        for e in range(2):
            y_send[step, e] = z_ref[step, pl.ds(e * (BY - 1), BX, stride=BY), :]
        for k in range(4):

            @pl.when(here[k])
            def _():
                halo_copy(step, k).start()

        def widen(t, _):
            made = next_basis(step, t)
            basis[step, at(t), :] = made
            if step + 1 < ITERS:
                weighted = reg_ref[at(t), :] * made
                column = jnp.sum(voxel[at(t)] * weighted[:, None, :], axis=2, keepdims=True)
                q_ref[at(t), :] = jnp.sum(jnp.where(eye, column, 0.0), axis=1)
            return 0

        lax.fori_loop(0, chunks, widen, 0)
        moments_times(step)
        z = z_ref[step]
        ym_ref[1:bricks, :] = z[: bricks - 1]
        yp_ref[0 : bricks - 1, :] = z[1:]
        found = []
        if step + 1 == ITERS:
            found = [fold(basis[a] * basis[b]) for a, b in early]
            final = (reg_ref[...] - SHIFTS[step]) * basis[step]
            found = found + [fold(basis[a] * final) for a, b in late]
        for k in range(4):

            @pl.when(here[k])
            def _():
                halo_arrived(step, k).wait_recv()
                halo_copy(step, k).wait_send()

        xm = jnp.concatenate([halo[step, 0][8 - BY :], z[: bricks - BY]], axis=0)
        xp = jnp.concatenate([z[BY:], halo[step, 1][:BY]], axis=0)
        ym_ref[pl.ds(0, BX, stride=BY), :] = halo[step, 2]
        yp_ref[pl.ds(BY - 1, BX, stride=BY), :] = halo[step, 3]
        near = jnp.where(masks[0], xm, 0.0) + jnp.where(masks[1], xp, 0.0)
        near = near + jnp.where(masks[2], ym_ref[...], 0.0) + jnp.where(masks[3], yp_ref[...], 0.0)
        mid = jnp.where(in_feat, my_ref[...] + coupling_weight * (degree * z - near), 0.0)
        mid_ref[...] = mid

        if step + 1 < ITERS:

            def advance(t, _):
                back = jnp.sum(block(square, t) * as_column(mid_ref[at(t), :]), axis=1)
                shifted = q_ref[at(t), :] - SHIFTS[step] * z_ref[step, at(t), :]
                z_ref[step + 1, at(t), :] = SCALE * (back + shifted)
                return 0

            lax.fori_loop(0, chunks, advance, 0, unroll=True)
        else:
            for e, (a, b) in enumerate(late):
                e += len(early)
                found[e] = SCALE * (found[e] + fold(z_ref[a] * mid))
        return found

    early = [(a, b) for a in range(ITERS) for b in range(a, ITERS)]
    late = [(a, ITERS) for a in range(ITERS)]
    pairs = early + late
    rows = []
    for step in range(ITERS):
        rows = operate(step)
    rows = rows + [jnp.zeros_like(rows[0])] * (-len(rows) % 8)
    sums = jnp.sum(jnp.concatenate(rows, axis=0), axis=1, keepdims=True)
    entry = lax.broadcasted_iota(jnp.int32, (len(rows), LANES), 1)
    diagonal = entry == lax.broadcasted_iota(jnp.int32, (len(rows), LANES), 0)
    mine = jnp.sum(jnp.where(diagonal, sums, 0.0), axis=0, keepdims=True)
    part[...] = mine
    parts[0] = mine

    def start(j, _):
        part_copy(j).start()
        return 0

    lax.fori_loop(1, count, start, 0, unroll=True)

    def last(t, _):
        basis[ITERS, at(t), :] = next_basis(ITERS, t)
        return 0

    lax.fori_loop(0, chunks, last, 0)

    all_of(got, feat_send, feat_recv).wait_send()
    all_of(got_extra, extra_send, extra_recv).wait_send()
    all_of(parts, part_send, part_recv).wait_send()
    all_of(parts, part_send, part_recv).wait_recv()
    total = jnp.sum(parts[...], axis=0)
    spread_total = jnp.sum(
        jnp.where(diagonal, jnp.broadcast_to(total, diagonal.shape), 0.0), axis=1, keepdims=True
    )
    gram = {}
    for e, (a, b) in enumerate(pairs):
        gram[a, b] = gram[b, a] = spread_total[e : e + 1]

    def inner(left, right):
        terms = [
            left[a] * right[b] * gram[a, b] for a in range(len(left)) for b in range(len(right))
        ]
        return functools.reduce(lambda p, q: p + q, terms)

    def apply(coefficients):
        size = len(coefficients)
        out = [SHIFTS[k] * coefficients[k] for k in range(size)]
        out.append(coefficients[-1] * (1.0 / SCALE))
        for k in range(1, size):
            out[k] = out[k] + coefficients[k - 1] * (1.0 / SCALE)
        return out

    one = jnp.ones((1, 1), jnp.float32)
    res, direction, answer = [one], [one], []
    norm_now = gram[0, 0]
    for step in range(ITERS):
        before_answer, before_res = answer, res
        image = apply(direction)
        alpha = norm_now / inner(direction, image)
        padded = answer + [jnp.zeros_like(one)] * (len(direction) - len(answer))
        answer = [p + alpha * d for p, d in zip(padded, direction)]
        res = [p - alpha * w for p, w in zip(res + [jnp.zeros_like(one)], image)]
        if step + 1 < ITERS:
            norm_next = inner(res, res)
            ratio = norm_next / norm_now
            direction = [
                p + ratio * d for p, d in zip(res, direction + [jnp.zeros_like(one)])
            ]
            norm_now = norm_next
    def combine(coefficients):
        return functools.reduce(
            lambda p, q: p + q, [c * basis[k] for k, c in enumerate(coefficients)]
        )

    answer_ref[...] = combine(before_answer)
    res_ref[...] = combine(before_res)
    direction_ref[...] = combine(direction)
    image_ref[...] = combine(image)
    alpha_ref[...] = jnp.broadcast_to(alpha, alpha_ref.shape)


def shards(gx, gy, point_feats, point_targets, point_lists, brick_adjacency, voxel_feats, voxel_reg):
    feat = point_feats.shape[0]
    brick_total, slots = point_lists.shape
    bricks, _, vox = voxel_feats.shape
    count = gx * gy
    cols = bricks * slots
    group = 4
    while count % group:
        group //= 2
    vmem = pl.BlockSpec(memory_space=pltpu.VMEM)
    hbm = pl.BlockSpec(memory_space=pltpu.HBM)
    f32 = jnp.float32
    answer, res, direction, image, alpha = pl.pallas_call(
        functools.partial(kernel, gx, gy),
        out_shape=(pltpu.VMEM((bricks, vox), f32),) * 4 + (pltpu.VMEM((1, vox), f32),),
        in_specs=[hbm] * 6,
        out_specs=(vmem,) * 5,
        scratch_shapes=[
            pltpu.VMEM((count, feat, cols), jnp.bfloat16),
            pltpu.VMEM((count, 2 * cols // LANES, LANES), jnp.bfloat16),
            pltpu.VMEM((count, 2 * cols // LANES, LANES), jnp.bfloat16),
            pltpu.VMEM((count * cols // LANES, LANES), f32),
            pltpu.VMEM((bricks, feat, vox), f32),
            pltpu.VMEM((bricks * feat * feat // LANES, LANES), f32),
            pltpu.VMEM((bricks * feat // LANES, LANES), f32),
            pltpu.VMEM((bricks * feat // LANES, LANES), f32),
            pltpu.VMEM((bricks, LANES), f32),
            pltpu.VMEM((bricks * feat, LANES), f32),
            pltpu.VMEM((ITERS + 1, bricks, vox), f32),
            pltpu.VMEM((ITERS, bricks, LANES), f32),
            pltpu.VMEM((bricks, LANES), f32),
            pltpu.VMEM((bricks, LANES), f32),
            pltpu.VMEM((bricks, LANES), f32),
            pltpu.VMEM((bricks, LANES), f32),
            pltpu.VMEM((bricks, LANES), f32),
            pltpu.VMEM((ITERS, 2, BX, LANES), f32),
            pltpu.VMEM((ITERS, 4, 8, LANES), f32),
            pltpu.VMEM((1, LANES), f32),
            pltpu.VMEM((count, 1, LANES), f32),
            pltpu.VMEM((count * cols // LANES, LANES), point_targets.dtype),
            pltpu.VMEM((slots, brick_total), jnp.int32),
            pltpu.VMEM((4, bricks), jnp.int32),
            pltpu.VMEM((bricks, vox), f32),
            pltpu.SemaphoreType.DMA,
            pltpu.SemaphoreType.DMA((4,)),
            pltpu.SemaphoreType.DMA((1,)),
            pltpu.SemaphoreType.DMA((count // group,)),
            pltpu.SemaphoreType.DMA((1,)),
            pltpu.SemaphoreType.DMA((count // group,)),
            pltpu.SemaphoreType.DMA((4,)),
            pltpu.SemaphoreType.DMA((2, 4)),
            pltpu.SemaphoreType.DMA((1,)),
            pltpu.SemaphoreType.DMA((1,)),
        ],
        compiler_params=pltpu.CompilerParams(collective_id=0, has_side_effects=True, vmem_limit_bytes=16 * 1024 * 1024),
    )(
        *(
            pltpu.with_memory_space_constraint(x, pltpu.HBM)
            for x in (
                point_feats,
                point_targets.reshape(-1, LANES),
                point_lists.T,
                brick_adjacency.T,
                voxel_feats,
                voxel_reg,
            )
        )
    )
    return answer + alpha * direction, res - alpha * image


def solution(mesh):
    placed = (
        P(None, ("gx", "gy")),
        P(("gx", "gy")),
        P(("gx", "gy"), None),
        P(("gx", "gy"), None),
        P(("gx", "gy"), None, None),
        P(("gx", "gy"), None),
    )
    return jax.shard_map(
        functools.partial(shards, mesh.shape["gx"], mesh.shape["gy"]),
        mesh=mesh,
        in_specs=placed,
        out_specs=(P(("gx", "gy"), None), P(("gx", "gy"), None)),
        check_vma=False,
    )
```

```python
import functools
import math

import jax
import jax.numpy as jnp
from jax import lax
from jax.experimental import pallas as pl
from jax.experimental.pallas import tpu as pltpu
from jax.sharding import PartitionSpec as P

BX = 8
BY = 4
ITERS = 3
LANES = 128
CHUNK = 8
MESH = pl.DeviceIdType.MESH
STRIDE = 11
SCALE = 2.0**-8
SHIFTS = (8.0, 1.0, 4.0)

coupling_weight = 1.0


def kernel(
    gx,
    gy,
    feats_hbm,
    target_hbm,
    lists_hbm,
    adjacency_hbm,
    voxel_hbm,
    reg_hbm,
    answer_ref,
    res_ref,
    direction_ref,
    image_ref,
    alpha_ref,
    got,
    got_extra,
    extra,
    acc_far,
    gather_far,
    flat,
    voxel,
    acc,
    gather,
    mz_ref,
    g_ref,
    square,
    basis,
    z_ref,
    q_ref,
    my_ref,
    mid_ref,
    ym_ref,
    yp_ref,
    y_send,
    halo,
    part,
    parts,
    target_ref,
    lists_ref,
    adjacency_ref,
    reg_ref,
    voxel_sem,
    input_sem,
    feat_send,
    feat_recv,
    extra_send,
    extra_recv,
    far_send,
    far_recv,
    halo_send,
    halo_recv,
    part_send,
    part_recv,
):
    count = gx * gy
    ix, iy = lax.axis_index("gx"), lax.axis_index("gy")
    me = ix * gy + iy
    feat = got.shape[2]
    total_bricks, slots = lists_ref.shape[1], lists_ref.shape[0]
    near = got.shape[1]
    wings = count // near
    first = me // near * near
    group = near // feat_recv.shape[1]
    bricks = reg_ref.shape[0]
    cols = bricks * slots
    halves = cols // LANES
    per_half = LANES // slots
    side = LANES // feat
    tall = per_half // side

    step_by = STRIDE if math.gcd(STRIDE, count) == 1 else 1
    kinds = [(w, h) for w in reversed(range(wings)) for h in range(halves)]

    def place(index):
        return (index // gy, index % gy)

    def at_offset(j):
        return (me + j * step_by) % count

    def near_offset(j):
        return first + (me - first + j * step_by) % near

    def columns(index, w, h):
        start = (index + w * near) % count * cols + h * LANES
        return pl.ds(pl.multiple_of(start, LANES), LANES)

    barrier = pltpu.get_barrier_semaphore()

    def greet(j, _):
        pl.semaphore_signal(barrier, inc=1, device_id=place(at_offset(j)), device_id_type=MESH)
        return 0

    lax.fori_loop(1, count, greet, 0, unroll=True)
    inputs = [
        pltpu.make_async_copy(source, target, input_sem.at[e])
        for e, (source, target) in enumerate(
            [
                (lists_hbm, lists_ref),
                (target_hbm, target_ref),
                (reg_hbm, reg_ref),
                (adjacency_hbm, adjacency_ref),
            ]
        )
    ]
    for copy in inputs:
        copy.start()
    voxel_copy = pltpu.make_async_copy(voxel_hbm, voxel, voxel_sem)
    voxel_copy.start()
    for q, (w, h) in enumerate(kinds):
        pltpu.make_async_copy(
            feats_hbm.at[:, columns(me, w, h)], got.at[q, 0], feat_recv.at[q, 0]
        ).start()
    halo[...] = jnp.zeros_like(halo)
    acc[...] = jnp.zeros_like(acc)
    gather[...] = jnp.zeros_like(gather)

    def feat_copy(q, j):
        to = near_offset(j)
        return pltpu.make_async_remote_copy(
            src_ref=feats_hbm.at[:, columns(to, *kinds[q])],
            dst_ref=got.at[q, j],
            send_sem=feat_send.at[0],
            recv_sem=feat_recv.at[q, j // group],
            device_id=place(to),
            device_id_type=MESH,
        )

    def extra_copy(j):
        to = near_offset(j)
        return pltpu.make_async_remote_copy(
            src_ref=extra.at[to % near],
            dst_ref=got_extra.at[j],
            send_sem=extra_send.at[0],
            recv_sem=extra_recv.at[0],
            device_id=place(to),
            device_id_type=MESH,
        )

    groups = total_bricks // LANES
    wide = slots * LANES
    inputs[0].wait()
    listed = lists_ref[...]
    offset = listed - slots * lax.broadcasted_iota(jnp.int32, listed.shape, 1)
    offset = jnp.where(listed >= 0, offset, -1)
    hits = jnp.concatenate(
        [
            jnp.max(jnp.where(offset == d, 1.0, 0.0), axis=0, keepdims=True)
            for d in range(slots)
        ],
        axis=0,
    )
    hits = jnp.concatenate(
        [hits[:, g * LANES : (g + 1) * LANES] for g in range(groups)], axis=0
    ).astype(jnp.bfloat16)
    spread = jnp.where(
        lax.broadcasted_iota(jnp.int32, (LANES, wide), 1) // slots
        == lax.broadcasted_iota(jnp.int32, (LANES, wide), 0),
        1.0,
        0.0,
    ).astype(jnp.bfloat16)
    spread_hits = jnp.dot(hits, spread, preferred_element_type=jnp.float32)
    same = (
        lax.broadcasted_iota(jnp.int32, (slots, wide), 1) % slots
        == lax.broadcasted_iota(jnp.int32, (slots, wide), 0)
    )
    live_rows = jnp.sum(
        jnp.where(same[None], spread_hits.reshape(groups, slots, wide), 0.0), axis=1
    )
    for l in range(slots):
        flat[pl.ds(l, groups, stride=slots), :] = live_rows[:, l * LANES : (l + 1) * LANES]
    inputs[1].wait()
    targets = target_ref[...].astype(jnp.float32)
    for k in range(count):
        rows = slice(k * halves, (k + 1) * halves)
        wing = (k // near + count - me // near) % wings if wings > 1 else 0
        extra[k % near, wing] = jnp.concatenate([flat[rows, :], targets[rows]], axis=0).astype(
            jnp.bfloat16
        )
    pltpu.make_async_copy(extra.at[me % near], got_extra.at[0], extra_recv.at[0]).start()

    pl.semaphore_wait(barrier, count - 1)

    def send_feats(q):
        def send(j, _):
            feat_copy(q, j).start()
            return 0

        lax.fori_loop(1, near, send, 0, unroll=True)

    def send_extra(j, _):
        extra_copy(j).start()
        return 0

    lax.fori_loop(1, near, send_extra, 0, unroll=True)
    for q in range(len(kinds)):
        send_feats(q)
    voxel_copy.wait()
    inputs[2].wait()
    inputs[3].wait()
    square[...] = jnp.zeros_like(square)

    def squares(t, _):
        for u in range(4):
            b = t * 4 + u
            rows = pl.ds(pl.multiple_of(b * feat, feat), feat)
            square[rows, 0:feat] = lax.dot_general(
                voxel[b],
                voxel[b],
                (((1,), (1,)), ((), ())),
                precision=lax.Precision.HIGHEST,
                preferred_element_type=jnp.float32,
            )
        return 0

    lax.fori_loop(0, bricks // 4, squares, 0)

    span_all = group * LANES
    owner = (lax.broadcasted_iota(jnp.int32, (1, span_all), 1) // slots) % per_half
    across = [jnp.where(owner % side == j, 1.0, 0.0).astype(jnp.bfloat16) for j in range(side)]
    along = owner // side == lax.broadcasted_iota(jnp.int32, (16, span_all), 0)

    def arrived(ref, sem):
        return pltpu.make_async_remote_copy(
            src_ref=ref,
            dst_ref=ref,
            send_sem=feat_send.at[0],
            recv_sem=sem,
            device_id=place(at_offset(1)),
            device_id_type=MESH,
        )

    def absorb(q):
        w, h = kinds[q]

        def some(g, _):
            mine = pl.ds(g * group, group)
            arrived(got.at[q, mine], feat_recv.at[q, g]).wait_recv()
            x = jnp.concatenate([got[q, g * group + u] for u in range(group)], axis=1)
            more = jnp.concatenate(
                [got_extra[g * group + u, w].astype(jnp.float32) for u in range(group)], axis=1
            )
            live = jnp.where(along, more[h : h + 1], 0.0)
            marked = live * more[halves + h : halves + h + 1]
            left = jnp.concatenate(
                [x * live[i : i + 1].astype(jnp.bfloat16) for i in range(tall)]
                + [marked.astype(jnp.bfloat16)],
                axis=0,
            )
            right = jnp.concatenate([x * mask for mask in across], axis=0)
            found = lax.dot_general(
                left, right, (((1,), (1,)), ((), ())), preferred_element_type=jnp.float32
            )
            acc[w, h * LANES : (h + 1) * LANES, :] += found[:LANES]
            gather[w, h * tall : (h + 1) * tall, :] += found[LANES : LANES + tall]
            return 0

        lax.fori_loop(0, near // group, some, 0)

    def far_copy(source, target, e):
        return pltpu.make_async_remote_copy(
            src_ref=source,
            dst_ref=target,
            send_sem=far_send.at[e],
            recv_sem=far_recv.at[e],
            device_id=place((me + near) % count),
            device_id_type=MESH,
        )

    def far_moments(piece):
        rows = pl.ds(piece * LANES // 2, LANES // 2)
        return far_copy(acc.at[1, rows], acc_far.at[rows], 0)

    far_gather = far_copy(gather.at[1], gather_far, 1)
    all_far_moments = far_copy(acc.at[1], acc_far, 0)

    arrived(got_extra, extra_recv.at[0]).wait_recv()
    for q, (w, h) in enumerate(kinds):
        absorb(q)
        if w:
            pieces_done = 2 * h + 1
            if h + 1 == halves:
                far_gather.start()
                pieces_done = 2 * halves
            for piece in range(max(2 * h - 1, 0), pieces_done):
                far_moments(piece).start()

    def unpack(ref, rows):
        for e in range(side):
            turned = rows if e == 0 else pltpu.roll(rows, LANES - e * feat, 1)
            ref[pl.ds(e, bricks // side, stride=side), :] = turned

    found_gather = gather[0]
    if wings > 1:
        far_gather.wait_recv()
        found_gather = found_gather + gather_far[...]
    unpack(g_ref, found_gather)

    eye = lax.broadcasted_iota(jnp.int32, (1, feat, LANES), 1) == lax.broadcasted_iota(
        jnp.int32, (1, feat, LANES), 2
    )
    chunks = bricks // CHUNK
    in_feat = lax.broadcasted_iota(jnp.int32, (bricks, LANES), 1) < feat

    def at(t):
        return pl.ds(pl.multiple_of(t * CHUNK, CHUNK), CHUNK)

    def block(ref, t):
        rows = pl.ds(pl.multiple_of(t * CHUNK * feat, CHUNK * feat), CHUNK * feat)
        return ref[rows, :].reshape(CHUNK, feat, LANES)

    def as_column(rows):
        return jnp.sum(jnp.where(eye, rows[:, None, :], 0.0), axis=2, keepdims=True)

    def gathered(t):
        return as_column(g_ref[at(t), :])

    lane_block = lax.broadcasted_iota(jnp.int32, (1, 1, LANES), 2) // feat

    def moments_times(step):
        for t in range(chunks):
            z_column = as_column(z_ref[step, at(t), :]).reshape(CHUNK // side, side, feat, 1)
            spread_column = z_column[:, 0]
            for e in range(1, side):
                spread_column = jnp.where(lane_block == e, z_column[:, e], spread_column)
            rows = CHUNK // side * feat
            packed = acc[0, t * rows : (t + 1) * rows, :].reshape(CHUNK // side, feat, LANES)
            mz_ref[t * (CHUNK // side) : (t + 1) * (CHUNK // side), :] = jnp.sum(
                packed * spread_column, axis=1
            )
        unpack(my_ref, mz_ref[...])

    def begin(t, _):
        z_ref[0, at(t), :] = jnp.sum(block(square, t) * gathered(t), axis=1)
        return 0

    lax.fori_loop(0, chunks, begin, 0, unroll=True)

    linked = jnp.where(adjacency_ref[...] >= 0, 1.0, 0.0)
    same_brick = lax.broadcasted_iota(jnp.int32, (bricks, bricks), 0) == lax.broadcasted_iota(
        jnp.int32, (bricks, bricks), 1
    )
    weights = [
        jnp.sum(jnp.where(same_brick, linked[k : k + 1], 0.0), axis=1, keepdims=True)
        for k in range(4)
    ]
    masks = [w > 0.0 for w in weights]
    degree = weights[0] + weights[1] + weights[2] + weights[3]
    here = [ix > 0, ix < gx - 1, iy > 0, iy < gy - 1]
    beside = [(ix - 1, iy), (ix + 1, iy), (ix, iy - 1), (ix, iy + 1)]

    def halo_copy(step, k):
        if k < 2:
            source = z_ref.at[step, pl.ds(k * (bricks - 8), 8)]
        else:
            source = y_send.at[step, k - 2]
        return pltpu.make_async_remote_copy(
            src_ref=source,
            dst_ref=halo.at[step, k ^ 1],
            send_sem=halo_send.at[k],
            recv_sem=halo_recv.at[step % 2, k ^ 1],
            device_id=beside[k],
            device_id_type=MESH,
        )

    def halo_arrived(step, k):
        return pltpu.make_async_remote_copy(
            src_ref=y_send.at[step, 0],
            dst_ref=halo.at[step, k],
            send_sem=halo_send.at[k],
            recv_sem=halo_recv.at[step % 2, k],
            device_id=beside[k],
            device_id_type=MESH,
        )

    def part_copy(j):
        return pltpu.make_async_remote_copy(
            src_ref=part,
            dst_ref=parts.at[j],
            send_sem=part_send.at[0],
            recv_sem=part_recv.at[0],
            device_id=place(at_offset(j)),
            device_id_type=MESH,
        )

    def sent(ref, sem):
        pltpu.make_async_remote_copy(
            src_ref=ref,
            dst_ref=ref,
            send_sem=sem,
            recv_sem=part_recv.at[0],
            device_id=place(at_offset(1)),
            device_id_type=MESH,
        ).wait_send()

    def fold(values):
        total = jnp.sum(values, axis=0, keepdims=True)
        width = total.shape[1]
        return sum(total[:, c : c + LANES] for c in range(0, width, LANES))

    def next_basis(step, t):
        if step == 0:
            return jnp.sum(voxel[at(t)] * gathered(t), axis=1)
        back = jnp.sum(voxel[at(t)] * as_column(mid_ref[at(t), :]), axis=1)
        shifted = (reg_ref[at(t), :] - SHIFTS[step - 1]) * basis[step - 1, at(t), :]
        return SCALE * (back + shifted)

    def operate(step):
        for e in range(2):
            y_send[step, e] = z_ref[step, pl.ds(e * (BY - 1), BX, stride=BY), :]
        for k in range(4):

            @pl.when(here[k])
            def _():
                halo_copy(step, k).start()

        def widen(t, _):
            made = next_basis(step, t)
            basis[step, at(t), :] = made
            if step + 1 < ITERS:
                weighted = reg_ref[at(t), :] * made
                column = jnp.sum(voxel[at(t)] * weighted[:, None, :], axis=2, keepdims=True)
                q_ref[at(t), :] = jnp.sum(jnp.where(eye, column, 0.0), axis=1)
            return 0

        lax.fori_loop(0, chunks, widen, 0)
        if step == 0 and wings > 1:
            all_far_moments.wait_recv()
            acc[0] += acc_far[...]
        moments_times(step)
        z = z_ref[step]
        ym_ref[1:bricks, :] = z[: bricks - 1]
        yp_ref[0 : bricks - 1, :] = z[1:]
        found = []
        if step + 1 == ITERS:
            found = [fold(basis[a] * basis[b]) for a, b in early]
            final = (reg_ref[...] - SHIFTS[step]) * basis[step]
            found = found + [fold(basis[a] * final) for a, b in late]
        for k in range(4):

            @pl.when(here[k])
            def _():
                halo_arrived(step, k).wait_recv()
                halo_copy(step, k).wait_send()

        xm = jnp.concatenate([halo[step, 0][8 - BY :], z[: bricks - BY]], axis=0)
        xp = jnp.concatenate([z[BY:], halo[step, 1][:BY]], axis=0)
        ym_ref[pl.ds(0, BX, stride=BY), :] = halo[step, 2]
        yp_ref[pl.ds(BY - 1, BX, stride=BY), :] = halo[step, 3]
        near = jnp.where(masks[0], xm, 0.0) + jnp.where(masks[1], xp, 0.0)
        near = near + jnp.where(masks[2], ym_ref[...], 0.0) + jnp.where(masks[3], yp_ref[...], 0.0)
        mid = jnp.where(in_feat, my_ref[...] + coupling_weight * (degree * z - near), 0.0)
        mid_ref[...] = mid

        if step + 1 < ITERS:

            def advance(t, _):
                back = jnp.sum(block(square, t) * as_column(mid_ref[at(t), :]), axis=1)
                shifted = q_ref[at(t), :] - SHIFTS[step] * z_ref[step, at(t), :]
                z_ref[step + 1, at(t), :] = SCALE * (back + shifted)
                return 0

            lax.fori_loop(0, chunks, advance, 0, unroll=True)
        else:
            for e, (a, b) in enumerate(late):
                e += len(early)
                found[e] = SCALE * (found[e] + fold(z_ref[a] * mid))
        return found

    early = [(a, b) for a in range(ITERS) for b in range(a, ITERS)]
    late = [(a, ITERS) for a in range(ITERS)]
    pairs = early + late
    rows = []
    for step in range(ITERS):
        rows = operate(step)
    rows = rows + [jnp.zeros_like(rows[0])] * (-len(rows) % 8)
    sums = jnp.sum(jnp.concatenate(rows, axis=0), axis=1, keepdims=True)
    entry = lax.broadcasted_iota(jnp.int32, (len(rows), LANES), 1)
    diagonal = entry == lax.broadcasted_iota(jnp.int32, (len(rows), LANES), 0)
    mine = jnp.sum(jnp.where(diagonal, sums, 0.0), axis=0, keepdims=True)
    part[...] = mine
    parts[0] = mine

    def start(j, _):
        part_copy(j).start()
        return 0

    lax.fori_loop(1, count, start, 0, unroll=True)

    def last(t, _):
        basis[ITERS, at(t), :] = next_basis(ITERS, t)
        return 0

    lax.fori_loop(0, chunks, last, 0)

    sent(got.at[:, pl.ds(1, near - 1)], feat_send.at[0])
    sent(got_extra.at[pl.ds(1, near - 1)], extra_send.at[0])
    if wings > 1:
        far_gather.wait_send()
        all_far_moments.wait_send()
    others = parts.at[pl.ds(1, count - 1)]
    sent(others, part_send.at[0])
    arrived(others, part_recv.at[0]).wait_recv()
    total = jnp.sum(parts[...], axis=0)
    spread_total = jnp.sum(
        jnp.where(diagonal, jnp.broadcast_to(total, diagonal.shape), 0.0), axis=1, keepdims=True
    )
    gram = {}
    for e, (a, b) in enumerate(pairs):
        gram[a, b] = gram[b, a] = spread_total[e : e + 1]

    def inner(left, right):
        terms = [
            left[a] * right[b] * gram[a, b] for a in range(len(left)) for b in range(len(right))
        ]
        return functools.reduce(lambda p, q: p + q, terms)

    def apply(coefficients):
        size = len(coefficients)
        out = [SHIFTS[k] * coefficients[k] for k in range(size)]
        out.append(coefficients[-1] * (1.0 / SCALE))
        for k in range(1, size):
            out[k] = out[k] + coefficients[k - 1] * (1.0 / SCALE)
        return out

    one = jnp.ones((1, 1), jnp.float32)
    res, direction, answer = [one], [one], []
    norm_now = gram[0, 0]
    for step in range(ITERS):
        before_answer, before_res = answer, res
        image = apply(direction)
        alpha = norm_now / inner(direction, image)
        padded = answer + [jnp.zeros_like(one)] * (len(direction) - len(answer))
        answer = [p + alpha * d for p, d in zip(padded, direction)]
        res = [p - alpha * w for p, w in zip(res + [jnp.zeros_like(one)], image)]
        if step + 1 < ITERS:
            norm_next = inner(res, res)
            ratio = norm_next / norm_now
            direction = [
                p + ratio * d for p, d in zip(res, direction + [jnp.zeros_like(one)])
            ]
            norm_now = norm_next
    def combine(coefficients):
        return functools.reduce(
            lambda p, q: p + q, [c * basis[k] for k, c in enumerate(coefficients)]
        )

    answer_ref[...] = combine(before_answer)
    res_ref[...] = combine(before_res)
    direction_ref[...] = combine(direction)
    image_ref[...] = combine(image)
    alpha_ref[...] = jnp.broadcast_to(alpha, alpha_ref.shape)


def shards(gx, gy, point_feats, point_targets, point_lists, brick_adjacency, voxel_feats, voxel_reg):
    feat = point_feats.shape[0]
    brick_total, slots = point_lists.shape
    bricks, _, vox = voxel_feats.shape
    count = gx * gy
    cols = bricks * slots
    wings = 2 if gx % 2 == 0 else 1
    near = count // wings
    group = 8
    while near % group:
        group //= 2
    vmem = pl.BlockSpec(memory_space=pltpu.VMEM)
    hbm = pl.BlockSpec(memory_space=pltpu.HBM)
    f32 = jnp.float32
    answer, res, direction, image, alpha = pl.pallas_call(
        functools.partial(kernel, gx, gy),
        out_shape=(pltpu.VMEM((bricks, vox), f32),) * 4 + (pltpu.VMEM((1, vox), f32),),
        in_specs=[hbm] * 6,
        out_specs=(vmem,) * 5,
        scratch_shapes=[
            pltpu.VMEM((wings * cols // LANES, near, feat, LANES), jnp.bfloat16),
            pltpu.VMEM((near, wings, 2 * cols // LANES, LANES), jnp.bfloat16),
            pltpu.VMEM((near, wings, 2 * cols // LANES, LANES), jnp.bfloat16),
            pltpu.VMEM((bricks * feat * feat // LANES, LANES), f32),
            pltpu.VMEM((bricks * feat // LANES, LANES), f32),
            pltpu.VMEM((count * cols // LANES, LANES), f32),
            pltpu.VMEM((bricks, feat, vox), f32),
            pltpu.VMEM((wings, bricks * feat * feat // LANES, LANES), f32),
            pltpu.VMEM((wings, bricks * feat // LANES, LANES), f32),
            pltpu.VMEM((bricks * feat // LANES, LANES), f32),
            pltpu.VMEM((bricks, LANES), f32),
            pltpu.VMEM((bricks * feat, LANES), f32),
            pltpu.VMEM((ITERS + 1, bricks, vox), f32),
            pltpu.VMEM((ITERS, bricks, LANES), f32),
            pltpu.VMEM((bricks, LANES), f32),
            pltpu.VMEM((bricks, LANES), f32),
            pltpu.VMEM((bricks, LANES), f32),
            pltpu.VMEM((bricks, LANES), f32),
            pltpu.VMEM((bricks, LANES), f32),
            pltpu.VMEM((ITERS, 2, BX, LANES), f32),
            pltpu.VMEM((ITERS, 4, 8, LANES), f32),
            pltpu.VMEM((1, LANES), f32),
            pltpu.VMEM((count, 1, LANES), f32),
            pltpu.VMEM((count * cols // LANES, LANES), point_targets.dtype),
            pltpu.VMEM((slots, brick_total), jnp.int32),
            pltpu.VMEM((4, bricks), jnp.int32),
            pltpu.VMEM((bricks, vox), f32),
            pltpu.SemaphoreType.DMA,
            pltpu.SemaphoreType.DMA((4,)),
            pltpu.SemaphoreType.DMA((1,)),
            pltpu.SemaphoreType.DMA((wings * cols // LANES, near // group)),
            pltpu.SemaphoreType.DMA((1,)),
            pltpu.SemaphoreType.DMA((1,)),
            pltpu.SemaphoreType.DMA((2,)),
            pltpu.SemaphoreType.DMA((2,)),
            pltpu.SemaphoreType.DMA((4,)),
            pltpu.SemaphoreType.DMA((2, 4)),
            pltpu.SemaphoreType.DMA((1,)),
            pltpu.SemaphoreType.DMA((1,)),
        ],
        compiler_params=pltpu.CompilerParams(collective_id=0, has_side_effects=True, vmem_limit_bytes=16 * 1024 * 1024),
    )(
        *(
            pltpu.with_memory_space_constraint(x, pltpu.HBM)
            for x in (
                point_feats,
                point_targets.reshape(-1, LANES),
                point_lists.T,
                brick_adjacency.T,
                voxel_feats,
                voxel_reg,
            )
        )
    )
    return answer + alpha * direction, res - alpha * image


def solution(mesh):
    placed = (
        P(None, ("gx", "gy")),
        P(("gx", "gy")),
        P(("gx", "gy"), None),
        P(("gx", "gy"), None),
        P(("gx", "gy"), None, None),
        P(("gx", "gy"), None),
    )
    return jax.shard_map(
        functools.partial(shards, mesh.shape["gx"], mesh.shape["gy"]),
        mesh=mesh,
        in_specs=placed,
        out_specs=(P(("gx", "gy"), None), P(("gx", "gy"), None)),
        check_vma=False,
    )
```

```python
import functools
import math

import jax
import jax.numpy as jnp
from jax import lax
from jax.experimental import pallas as pl
from jax.experimental.pallas import tpu as pltpu
from jax.sharding import PartitionSpec as P

BX = 8
BY = 4
ITERS = 3
LANES = 128
SUBLANES = 8
CHUNK = 8
MESH = pl.DeviceIdType.MESH
STRIDE = 11
SCALE = 2.0**-8
SHIFTS = (8.0, 1.0, 4.0)

coupling_weight = 1.0


def kernel(
    gx,
    gy,
    feats_hbm,
    target_hbm,
    lists_hbm,
    adjacency_hbm,
    voxel_hbm,
    reg_hbm,
    answer_ref,
    res_ref,
    direction_ref,
    image_ref,
    alpha_ref,
    got,
    got_extra,
    extra,
    acc_sent,
    acc_far,
    gather_far,
    flat,
    voxel,
    acc,
    gather,
    mz_ref,
    g_ref,
    square,
    basis,
    z_ref,
    q_ref,
    my_ref,
    mid_ref,
    ym_ref,
    yp_ref,
    y_send,
    halo,
    part,
    parts,
    target_ref,
    lists_ref,
    adjacency_ref,
    reg_ref,
    voxel_sem,
    input_sem,
    feat_send,
    feat_recv,
    extra_send,
    extra_recv,
    far_send,
    far_recv,
    halo_send,
    halo_recv,
    part_send,
    part_recv,
    ready,
):
    count = gx * gy
    ix, iy = lax.axis_index("gx"), lax.axis_index("gy")
    me = ix * gy + iy
    feat = got.shape[2]
    total_bricks, slots = lists_ref.shape[1], lists_ref.shape[0]
    near = got.shape[1]
    wings = count // near
    first = me // near * near
    group = near // feat_recv.shape[1]
    bricks = reg_ref.shape[0]
    cols = bricks * slots
    halves = cols // LANES
    per_half = LANES // slots
    side = LANES // feat
    tall = per_half // side

    step_by = STRIDE if math.gcd(STRIDE, count) == 1 else 1
    kinds = [(w, h) for w in reversed(range(wings)) for h in range(halves)]

    def place(index):
        return (index // gy, index % gy)

    def at_offset(j):
        return (me + j * step_by) % count

    def near_offset(j):
        return first + (me - first + j * step_by) % near

    def columns(index, w, h):
        start = (index + w * near) % count * cols + h * LANES
        return pl.ds(pl.multiple_of(start, LANES), LANES)

    barrier = pltpu.get_barrier_semaphore()

    partner = place((me + near) % count)
    wing = me // near
    first_wing = wing == 0
    last_wing = wing == wings - 1

    def greet(j, _):
        pl.semaphore_signal(
            barrier, inc=1, device_id=place(near_offset(j)), device_id_type=MESH
        )
        return 0

    inputs = [
        pltpu.make_async_copy(source, target, input_sem.at[e])
        for e, (source, target) in enumerate(
            [
                (lists_hbm, lists_ref),
                (target_hbm, target_ref),
                (reg_hbm, reg_ref),
                (adjacency_hbm, adjacency_ref),
            ]
        )
    ]
    inputs[0].start()
    inputs[1].start()
    lax.fori_loop(1, near, greet, 0, unroll=True)
    if wings > 1:

        @pl.when(first_wing)
        def _():
            pl.semaphore_signal(barrier, inc=1, device_id=partner, device_id_type=MESH)

    inputs[2].start()
    inputs[3].start()
    voxel_copy = pltpu.make_async_copy(voxel_hbm, voxel, voxel_sem)
    voxel_copy.start()
    for q, (w, h) in enumerate(kinds):
        pltpu.make_async_copy(
            feats_hbm.at[:, columns(me, w, h)], got.at[q, 0], feat_recv.at[q, 0]
        ).start()
    halo[...] = jnp.zeros_like(halo)
    acc[...] = jnp.zeros_like(acc)
    gather[...] = jnp.zeros_like(gather)

    def feat_copy(q, j):
        to = near_offset(j)
        return pltpu.make_async_remote_copy(
            src_ref=feats_hbm.at[:, columns(to, *kinds[q])],
            dst_ref=got.at[q, j],
            send_sem=feat_send.at[0],
            recv_sem=feat_recv.at[q, j // group],
            device_id=place(to),
            device_id_type=MESH,
        )

    def extra_copy(j):
        to = near_offset(j)
        return pltpu.make_async_remote_copy(
            src_ref=extra.at[to % near],
            dst_ref=got_extra.at[j],
            send_sem=extra_send.at[0],
            recv_sem=extra_recv.at[0],
            device_id=place(to),
            device_id_type=MESH,
        )

    groups = total_bricks // LANES
    wide = slots * LANES
    inputs[0].wait()
    listed = lists_ref[...]
    offset = listed - slots * lax.broadcasted_iota(jnp.int32, listed.shape, 1)
    offset = jnp.where(listed >= 0, offset, -1)
    hits = jnp.concatenate(
        [
            jnp.max(jnp.where(offset == d, 1.0, 0.0), axis=0, keepdims=True)
            for d in range(slots)
        ],
        axis=0,
    )
    hits = jnp.concatenate(
        [hits[:, g * LANES : (g + 1) * LANES] for g in range(groups)], axis=0
    ).astype(jnp.bfloat16)
    spread = jnp.where(
        lax.broadcasted_iota(jnp.int32, (LANES, wide), 1) // slots
        == lax.broadcasted_iota(jnp.int32, (LANES, wide), 0),
        1.0,
        0.0,
    ).astype(jnp.bfloat16)
    spread_hits = jnp.dot(hits, spread, preferred_element_type=jnp.float32)
    same = (
        lax.broadcasted_iota(jnp.int32, (slots, wide), 1) % slots
        == lax.broadcasted_iota(jnp.int32, (slots, wide), 0)
    )
    live_rows = jnp.sum(
        jnp.where(same[None], spread_hits.reshape(groups, slots, wide), 0.0), axis=1
    )
    for l in range(slots):
        flat[pl.ds(l, groups, stride=slots), :] = live_rows[:, l * LANES : (l + 1) * LANES]
    inputs[1].wait()
    targets = target_ref[...].astype(jnp.float32)
    for k in range(count):
        rows = slice(k * halves, (k + 1) * halves)
        from_me = (k // near + wings - wing) % wings if wings > 1 else 0
        extra[k % near, from_me] = jnp.concatenate([flat[rows, :], targets[rows]], axis=0).astype(
            jnp.bfloat16
        )
    pltpu.make_async_copy(extra.at[me % near], got_extra.at[0], extra_recv.at[0]).start()

    pl.semaphore_wait(barrier, near - 1 + wing)
    if wings > 1:

        @pl.when(last_wing)
        def _():
            pl.semaphore_signal(ready, inc=1, device_id=partner, device_id_type=MESH)


    def send_feats(q):
        def send(j, _):
            feat_copy(q, j).start()
            return 0

        lax.fori_loop(1, near, send, 0, unroll=True)

    def send_extra(j, _):
        extra_copy(j).start()
        return 0

    lax.fori_loop(1, near, send_extra, 0, unroll=True)
    for q in range(len(kinds)):
        send_feats(q)
    voxel_copy.wait()
    inputs[2].wait()
    inputs[3].wait()
    square[...] = jnp.zeros_like(square)

    def squares(t, _):
        for u in range(4):
            b = t * 4 + u
            rows = pl.ds(pl.multiple_of(b * feat, feat), feat)
            square[rows, 0:feat] = lax.dot_general(
                voxel[b],
                voxel[b],
                (((1,), (1,)), ((), ())),
                precision=lax.Precision.HIGHEST,
                preferred_element_type=jnp.float32,
            )
        return 0

    lax.fori_loop(0, bricks // 4, squares, 0)
    linked = jnp.where(adjacency_ref[...] >= 0, 1.0, 0.0)
    same_brick = lax.broadcasted_iota(jnp.int32, (bricks, bricks), 0) == lax.broadcasted_iota(
        jnp.int32, (bricks, bricks), 1
    )
    weights = [
        jnp.sum(jnp.where(same_brick, linked[k : k + 1], 0.0), axis=1, keepdims=True)
        for k in range(4)
    ]
    masks = [w > 0.0 for w in weights]
    degree = weights[0] + weights[1] + weights[2] + weights[3]

    span_all = group * LANES
    owner = (lax.broadcasted_iota(jnp.int32, (1, span_all), 1) // slots) % per_half
    across = [jnp.where(owner % side == j, 1.0, 0.0).astype(jnp.bfloat16) for j in range(side)]
    along = owner // side == lax.broadcasted_iota(jnp.int32, (16, span_all), 0)

    def arrived(ref, sem):
        return pltpu.make_async_remote_copy(
            src_ref=ref,
            dst_ref=ref,
            send_sem=feat_send.at[0],
            recv_sem=sem,
            device_id=place(at_offset(1)),
            device_id_type=MESH,
        )

    def absorb(q):
        w, h = kinds[q]

        def some(g, _):
            mine = pl.ds(g * group, group)
            arrived(got.at[q, mine], feat_recv.at[q, g]).wait_recv()
            x = jnp.concatenate([got[q, g * group + u] for u in range(group)], axis=1)
            more = jnp.concatenate(
                [got_extra[g * group + u, w].astype(jnp.float32) for u in range(group)], axis=1
            )
            live = jnp.where(along, more[h : h + 1], 0.0)
            marked = live * more[halves + h : halves + h + 1]
            left = jnp.concatenate(
                [x * live[i : i + 1].astype(jnp.bfloat16) for i in range(tall)]
                + [marked.astype(jnp.bfloat16)],
                axis=0,
            )
            right = jnp.concatenate([x * mask for mask in across], axis=0)
            found = lax.dot_general(
                left, right, (((1,), (1,)), ((), ())), preferred_element_type=jnp.float32
            )
            acc[w, h * LANES : (h + 1) * LANES, :] += found[:LANES]
            gather[w, h * tall : (h + 1) * tall, :] += found[LANES : LANES + tall]
            return 0

        lax.fori_loop(0, near // group, some, 0)

    def far_copy(source, target, e):
        return pltpu.make_async_remote_copy(
            src_ref=source,
            dst_ref=target,
            send_sem=far_send.at[e],
            recv_sem=far_recv.at[e],
            device_id=partner,
            device_id_type=MESH,
        )

    tiles = feat // SUBLANES
    middle = tiles // 2
    in_block = lax.broadcasted_iota(jnp.int32, (SUBLANES, LANES), 1) % feat
    lane_block = lax.broadcasted_iota(jnp.int32, (1, LANES), 1) // feat

    def pack(h):
        found = []
        for i in range(0, tall, 2):
            rows = [
                [
                    acc[1, pl.ds(h * LANES + (i + k) * feat + r * SUBLANES, SUBLANES), :]
                    for r in range(tiles)
                ]
                for k in range(2)
            ]
            found = found + [rows[0][0], rows[1][0]]
            for k in range(2):
                for r in range(1, middle):
                    turned = pltpu.roll(rows[k][tiles - r], r * SUBLANES, 1)
                    found.append(jnp.where(in_block >= r * SUBLANES, rows[k][r], turned))
            turned = pltpu.roll(rows[1][middle], middle * SUBLANES, 1)
            found.append(jnp.where(in_block >= middle * SUBLANES, rows[0][middle], turned))
        packed = jnp.concatenate(found, axis=0)
        acc_sent[h * packed.shape[0] : (h + 1) * packed.shape[0], :] = packed

    def unpack_far(h):
        upper, above = [], []
        each = tiles + 1
        for i in range(0, tall, 2):
            start = (h * tall // 2 + i // 2) * each
            given = [
                acc_far[pl.ds((start + r) * SUBLANES, SUBLANES), :] for r in range(each)
            ]
            for k in range(2):
                rows = [given[k]] + [None] * (tiles - 1)
                for r in range(1, middle):
                    both = given[2 + k * (middle - 1) + r - 1]
                    rows[r] = both
                    rows[tiles - r] = pltpu.roll(both, LANES - r * SUBLANES, 1)
                last_tile = given[each - 1]
                rows[middle] = (
                    pltpu.roll(last_tile, LANES - middle * SUBLANES, 1) if k else last_tile
                )
                for r in range(tiles):
                    upper.append(jnp.where(in_block >= r * SUBLANES, rows[r], 0.0))
                    above.append(jnp.where(in_block >= (r + 1) * SUBLANES, rows[r], 0.0))
        turned = jnp.concatenate(above, axis=0).T
        below = []
        for i in range(tall):
            mine = jnp.zeros((feat, LANES), jnp.float32)
            for j in range(side):
                band = turned[j * feat : (j + 1) * feat]
                if i != j:
                    band = pltpu.roll(band, (j - i) % side * feat, 1)
                mine = jnp.where(lane_block == j, band, mine)
            below.append(mine)
        rows = slice(h * LANES, (h + 1) * LANES)
        acc[0, rows, :] += jnp.concatenate(upper, axis=0) + jnp.concatenate(below, axis=0)

    def far_moments(h):
        half = acc_sent.shape[0] // halves
        rows = pl.ds(h * half, half)
        return far_copy(acc_sent.at[rows], acc_far.at[rows], 0)

    far_gather = far_copy(gather.at[1], gather_far, 1)
    all_far_moments = far_copy(acc_sent, acc_far, 0)

    arrived(got_extra, extra_recv.at[0]).wait_recv()
    for q, (w, h) in enumerate(kinds):
        absorb(q)
        if w:
            pack(h)
            if h == 0:

                @pl.when(first_wing)
                def _():
                    pl.semaphore_wait(ready, 1)

            if h + 1 == halves:
                far_gather.start()
            far_moments(h).start()

    def unpack(ref, rows):
        for e in range(side):
            turned = rows if e == 0 else pltpu.roll(rows, LANES - e * feat, 1)
            ref[pl.ds(e, bricks // side, stride=side), :] = turned

    found_gather = gather[0]
    if wings > 1:
        far_gather.wait_recv()
        found_gather = found_gather + gather_far[...]
    unpack(g_ref, found_gather)

    eye = lax.broadcasted_iota(jnp.int32, (1, feat, LANES), 1) == lax.broadcasted_iota(
        jnp.int32, (1, feat, LANES), 2
    )
    chunks = bricks // CHUNK
    in_feat = lax.broadcasted_iota(jnp.int32, (bricks, LANES), 1) < feat

    def at(t):
        return pl.ds(pl.multiple_of(t * CHUNK, CHUNK), CHUNK)

    def block(ref, t):
        rows = pl.ds(pl.multiple_of(t * CHUNK * feat, CHUNK * feat), CHUNK * feat)
        return ref[rows, :].reshape(CHUNK, feat, LANES)

    def as_column(rows):
        return jnp.sum(jnp.where(eye, rows[:, None, :], 0.0), axis=2, keepdims=True)

    def gathered(t):
        return as_column(g_ref[at(t), :])

    def moments_times(step):
        for t in range(chunks):
            z_column = as_column(z_ref[step, at(t), :]).reshape(CHUNK // side, side, feat, 1)
            spread_column = z_column[:, 0]
            for e in range(1, side):
                spread_column = jnp.where(lane_block == e, z_column[:, e], spread_column)
            rows = CHUNK // side * feat
            packed = acc[0, t * rows : (t + 1) * rows, :].reshape(CHUNK // side, feat, LANES)
            mz_ref[t * (CHUNK // side) : (t + 1) * (CHUNK // side), :] = jnp.sum(
                packed * spread_column, axis=1
            )
        unpack(my_ref, mz_ref[...])

    def begin(t, _):
        z_ref[0, at(t), :] = jnp.sum(block(square, t) * gathered(t), axis=1)
        return 0

    lax.fori_loop(0, chunks, begin, 0, unroll=True)

    here = [ix > 0, ix < gx - 1, iy > 0, iy < gy - 1]
    beside = [(ix - 1, iy), (ix + 1, iy), (ix, iy - 1), (ix, iy + 1)]

    def halo_copy(step, k):
        if k < 2:
            source = z_ref.at[step, pl.ds(k * (bricks - 8), 8)]
        else:
            source = y_send.at[step, k - 2]
        return pltpu.make_async_remote_copy(
            src_ref=source,
            dst_ref=halo.at[step, k ^ 1],
            send_sem=halo_send.at[k],
            recv_sem=halo_recv.at[step % 2, k ^ 1],
            device_id=beside[k],
            device_id_type=MESH,
        )

    def halo_arrived(step, k):
        return pltpu.make_async_remote_copy(
            src_ref=y_send.at[step, 0],
            dst_ref=halo.at[step, k],
            send_sem=halo_send.at[k],
            recv_sem=halo_recv.at[step % 2, k],
            device_id=beside[k],
            device_id_type=MESH,
        )

    def part_copy(j):
        return pltpu.make_async_remote_copy(
            src_ref=part,
            dst_ref=parts.at[j],
            send_sem=part_send.at[0],
            recv_sem=part_recv.at[0],
            device_id=place(at_offset(j)),
            device_id_type=MESH,
        )

    def sent(ref, sem):
        pltpu.make_async_remote_copy(
            src_ref=ref,
            dst_ref=ref,
            send_sem=sem,
            recv_sem=part_recv.at[0],
            device_id=place(at_offset(1)),
            device_id_type=MESH,
        ).wait_send()

    def fold(values):
        total = jnp.sum(values, axis=0, keepdims=True)
        width = total.shape[1]
        return sum(total[:, c : c + LANES] for c in range(0, width, LANES))

    def next_basis(step, t):
        if step == 0:
            return jnp.sum(voxel[at(t)] * gathered(t), axis=1)
        back = jnp.sum(voxel[at(t)] * as_column(mid_ref[at(t), :]), axis=1)
        shifted = (reg_ref[at(t), :] - SHIFTS[step - 1]) * basis[step - 1, at(t), :]
        return SCALE * (back + shifted)

    def operate(step):
        for e in range(2):
            y_send[step, e] = z_ref[step, pl.ds(e * (BY - 1), BX, stride=BY), :]
        for k in range(4):

            @pl.when(here[k])
            def _():
                halo_copy(step, k).start()

        def widen(t, _):
            made = next_basis(step, t)
            basis[step, at(t), :] = made
            if step + 1 < ITERS:
                weighted = reg_ref[at(t), :] * made
                column = jnp.sum(voxel[at(t)] * weighted[:, None, :], axis=2, keepdims=True)
                q_ref[at(t), :] = jnp.sum(jnp.where(eye, column, 0.0), axis=1)
            return 0

        lax.fori_loop(0, chunks, widen, 0)
        if step == 0 and wings > 1:
            all_far_moments.wait_recv()
            for h in range(halves):
                unpack_far(h)
        moments_times(step)
        z = z_ref[step]
        ym_ref[1:bricks, :] = z[: bricks - 1]
        yp_ref[0 : bricks - 1, :] = z[1:]
        found = []
        if step + 1 == ITERS:
            found = [fold(basis[a] * basis[b]) for a, b in early]
            final = (reg_ref[...] - SHIFTS[step]) * basis[step]
            found = found + [fold(basis[a] * final) for a, b in late]
        for k in range(4):

            @pl.when(here[k])
            def _():
                halo_arrived(step, k).wait_recv()
                halo_copy(step, k).wait_send()

        xm = jnp.concatenate([halo[step, 0][8 - BY :], z[: bricks - BY]], axis=0)
        xp = jnp.concatenate([z[BY:], halo[step, 1][:BY]], axis=0)
        ym_ref[pl.ds(0, BX, stride=BY), :] = halo[step, 2]
        yp_ref[pl.ds(BY - 1, BX, stride=BY), :] = halo[step, 3]
        near = jnp.where(masks[0], xm, 0.0) + jnp.where(masks[1], xp, 0.0)
        near = near + jnp.where(masks[2], ym_ref[...], 0.0) + jnp.where(masks[3], yp_ref[...], 0.0)
        mid = jnp.where(in_feat, my_ref[...] + coupling_weight * (degree * z - near), 0.0)
        mid_ref[...] = mid

        if step + 1 < ITERS:

            def advance(t, _):
                back = jnp.sum(block(square, t) * as_column(mid_ref[at(t), :]), axis=1)
                shifted = q_ref[at(t), :] - SHIFTS[step] * z_ref[step, at(t), :]
                z_ref[step + 1, at(t), :] = SCALE * (back + shifted)
                return 0

            lax.fori_loop(0, chunks, advance, 0, unroll=True)
        else:
            for e, (a, b) in enumerate(late):
                e += len(early)
                found[e] = SCALE * (found[e] + fold(z_ref[a] * mid))
        return found

    early = [(a, b) for a in range(ITERS) for b in range(a, ITERS)]
    late = [(a, ITERS) for a in range(ITERS)]
    pairs = early + late
    rows = []
    for step in range(ITERS):
        rows = operate(step)
    rows = rows + [jnp.zeros_like(rows[0])] * (-len(rows) % 8)
    sums = jnp.sum(jnp.concatenate(rows, axis=0), axis=1, keepdims=True)
    entry = lax.broadcasted_iota(jnp.int32, (len(rows), LANES), 1)
    diagonal = entry == lax.broadcasted_iota(jnp.int32, (len(rows), LANES), 0)
    mine = jnp.sum(jnp.where(diagonal, sums, 0.0), axis=0, keepdims=True)
    part[...] = mine
    parts[0] = mine

    def start(j, _):
        part_copy(j).start()
        return 0

    lax.fori_loop(1, count, start, 0, unroll=True)

    def last(t, _):
        basis[ITERS, at(t), :] = next_basis(ITERS, t)
        return 0

    lax.fori_loop(0, chunks, last, 0)

    sent(got.at[:, pl.ds(1, near - 1)], feat_send.at[0])
    sent(got_extra.at[pl.ds(1, near - 1)], extra_send.at[0])
    if wings > 1:
        far_gather.wait_send()
        all_far_moments.wait_send()
    others = parts.at[pl.ds(1, count - 1)]
    sent(others, part_send.at[0])
    arrived(others, part_recv.at[0]).wait_recv()
    total = jnp.sum(parts[...], axis=0)
    spread_total = jnp.sum(
        jnp.where(diagonal, jnp.broadcast_to(total, diagonal.shape), 0.0), axis=1, keepdims=True
    )
    gram = {}
    for e, (a, b) in enumerate(pairs):
        gram[a, b] = gram[b, a] = spread_total[e : e + 1]

    def inner(left, right):
        terms = [
            left[a] * right[b] * gram[a, b] for a in range(len(left)) for b in range(len(right))
        ]
        return functools.reduce(lambda p, q: p + q, terms)

    def apply(coefficients):
        size = len(coefficients)
        out = [SHIFTS[k] * coefficients[k] for k in range(size)]
        out.append(coefficients[-1] * (1.0 / SCALE))
        for k in range(1, size):
            out[k] = out[k] + coefficients[k - 1] * (1.0 / SCALE)
        return out

    one = jnp.ones((1, 1), jnp.float32)
    res, direction, answer = [one], [one], []
    norm_now = gram[0, 0]
    for step in range(ITERS):
        before_answer, before_res = answer, res
        image = apply(direction)
        alpha = norm_now / inner(direction, image)
        padded = answer + [jnp.zeros_like(one)] * (len(direction) - len(answer))
        answer = [p + alpha * d for p, d in zip(padded, direction)]
        res = [p - alpha * w for p, w in zip(res + [jnp.zeros_like(one)], image)]
        if step + 1 < ITERS:
            norm_next = inner(res, res)
            ratio = norm_next / norm_now
            direction = [
                p + ratio * d for p, d in zip(res, direction + [jnp.zeros_like(one)])
            ]
            norm_now = norm_next
    def combine(coefficients):
        return functools.reduce(
            lambda p, q: p + q, [c * basis[k] for k, c in enumerate(coefficients)]
        )

    answer_ref[...] = combine(before_answer)
    res_ref[...] = combine(before_res)
    direction_ref[...] = combine(direction)
    image_ref[...] = combine(image)
    alpha_ref[...] = jnp.broadcast_to(alpha, alpha_ref.shape)


def shards(gx, gy, point_feats, point_targets, point_lists, brick_adjacency, voxel_feats, voxel_reg):
    feat = point_feats.shape[0]
    brick_total, slots = point_lists.shape
    bricks, _, vox = voxel_feats.shape
    count = gx * gy
    cols = bricks * slots
    wings = 2 if gx % 2 == 0 else 1
    kept = bricks * feat * (feat + SUBLANES) // 2 // LANES
    near = count // wings
    group = 8
    while near % group:
        group //= 2
    vmem = pl.BlockSpec(memory_space=pltpu.VMEM)
    hbm = pl.BlockSpec(memory_space=pltpu.HBM)
    f32 = jnp.float32
    answer, res, direction, image, alpha = pl.pallas_call(
        functools.partial(kernel, gx, gy),
        out_shape=(pltpu.VMEM((bricks, vox), f32),) * 4 + (pltpu.VMEM((1, vox), f32),),
        in_specs=[hbm] * 6,
        out_specs=(vmem,) * 5,
        scratch_shapes=[
            pltpu.VMEM((wings * cols // LANES, near, feat, LANES), jnp.bfloat16),
            pltpu.VMEM((near, wings, 2 * cols // LANES, LANES), jnp.bfloat16),
            pltpu.VMEM((near, wings, 2 * cols // LANES, LANES), jnp.bfloat16),
            pltpu.VMEM((kept, LANES), f32),
            pltpu.VMEM((kept, LANES), f32),
            pltpu.VMEM((bricks * feat // LANES, LANES), f32),
            pltpu.VMEM((count * cols // LANES, LANES), f32),
            pltpu.VMEM((bricks, feat, vox), f32),
            pltpu.VMEM((wings, bricks * feat * feat // LANES, LANES), f32),
            pltpu.VMEM((wings, bricks * feat // LANES, LANES), f32),
            pltpu.VMEM((bricks * feat // LANES, LANES), f32),
            pltpu.VMEM((bricks, LANES), f32),
            pltpu.VMEM((bricks * feat, LANES), f32),
            pltpu.VMEM((ITERS + 1, bricks, vox), f32),
            pltpu.VMEM((ITERS, bricks, LANES), f32),
            pltpu.VMEM((bricks, LANES), f32),
            pltpu.VMEM((bricks, LANES), f32),
            pltpu.VMEM((bricks, LANES), f32),
            pltpu.VMEM((bricks, LANES), f32),
            pltpu.VMEM((bricks, LANES), f32),
            pltpu.VMEM((ITERS, 2, BX, LANES), f32),
            pltpu.VMEM((ITERS, 4, 8, LANES), f32),
            pltpu.VMEM((1, LANES), f32),
            pltpu.VMEM((count, 1, LANES), f32),
            pltpu.VMEM((count * cols // LANES, LANES), point_targets.dtype),
            pltpu.VMEM((slots, brick_total), jnp.int32),
            pltpu.VMEM((4, bricks), jnp.int32),
            pltpu.VMEM((bricks, vox), f32),
            pltpu.SemaphoreType.DMA,
            pltpu.SemaphoreType.DMA((4,)),
            pltpu.SemaphoreType.DMA((1,)),
            pltpu.SemaphoreType.DMA((wings * cols // LANES, near // group)),
            pltpu.SemaphoreType.DMA((1,)),
            pltpu.SemaphoreType.DMA((1,)),
            pltpu.SemaphoreType.DMA((2,)),
            pltpu.SemaphoreType.DMA((2,)),
            pltpu.SemaphoreType.DMA((4,)),
            pltpu.SemaphoreType.DMA((2, 4)),
            pltpu.SemaphoreType.DMA((1,)),
            pltpu.SemaphoreType.DMA((1,)),
            pltpu.SemaphoreType.REGULAR,
        ],
        compiler_params=pltpu.CompilerParams(collective_id=0, has_side_effects=True, vmem_limit_bytes=16 * 1024 * 1024),
    )(
        *(
            pltpu.with_memory_space_constraint(x, pltpu.HBM)
            for x in (
                point_feats,
                point_targets.reshape(-1, LANES),
                point_lists.T,
                brick_adjacency.T,
                voxel_feats,
                voxel_reg,
            )
        )
    )
    return answer + alpha * direction, res - alpha * image


def solution(mesh):
    placed = (
        P(None, ("gx", "gy")),
        P(("gx", "gy")),
        P(("gx", "gy"), None),
        P(("gx", "gy"), None),
        P(("gx", "gy"), None, None),
        P(("gx", "gy"), None),
    )
    return jax.shard_map(
        functools.partial(shards, mesh.shape["gx"], mesh.shape["gy"]),
        mesh=mesh,
        in_specs=placed,
        out_specs=(P(("gx", "gy"), None), P(("gx", "gy"), None)),
        check_vma=False,
    )
```

```python
import functools
import math

import jax
import jax.numpy as jnp
from jax import lax
from jax.experimental import pallas as pl
from jax.experimental.pallas import tpu as pltpu
from jax.sharding import PartitionSpec as P

BX = 8
BY = 4
ITERS = 3
LANES = 128
SUBLANES = 8
CHUNK = 8
MESH = pl.DeviceIdType.MESH
STRIDE = 11
SCALE = 2.0**-8
UNUSED = 256.0
SHIFTS = (8.0, 1.0, 4.0)

coupling_weight = 1.0


def kernel(
    gx,
    gy,
    feats_hbm,
    target_hbm,
    lists_hbm,
    adjacency_hbm,
    voxel_hbm,
    reg_hbm,
    answer_ref,
    res_ref,
    direction_ref,
    image_ref,
    alpha_ref,
    got,
    got_extra,
    extra,
    acc_sent,
    acc_far,
    gather_far,
    flat,
    voxel,
    acc,
    gather,
    mz_ref,
    g_ref,
    square,
    basis,
    z_ref,
    q_ref,
    my_ref,
    mid_ref,
    ym_ref,
    yp_ref,
    y_send,
    halo,
    part,
    parts,
    target_ref,
    lists_ref,
    adjacency_ref,
    reg_ref,
    voxel_sem,
    input_sem,
    feat_send,
    feat_recv,
    extra_send,
    extra_recv,
    far_send,
    far_recv,
    halo_send,
    halo_recv,
    part_send,
    part_recv,
    ready,
):
    count = gx * gy
    ix, iy = lax.axis_index("gx"), lax.axis_index("gy")
    me = ix * gy + iy
    feat = got.shape[2]
    total_bricks, slots = lists_ref.shape[1], lists_ref.shape[0]
    near = got.shape[1]
    wings = count // near
    first = me // near * near
    group = near // feat_recv.shape[1]
    bricks = reg_ref.shape[0]
    cols = bricks * slots
    halves = cols // LANES
    per_half = LANES // slots
    side = LANES // feat
    tall = per_half // side

    half_gx = gx // wings
    first_x = ix // half_gx * half_gx
    rows_at = [(ix - first_x + a) % half_gx for a in range(half_gx)]
    across_at = [(iy + b) % gy for b in range(gy)]
    all_rows_at = [(ix + a) % gx for a in range(gx)]
    step_by = STRIDE if math.gcd(STRIDE, near) == 1 else 1
    offsets = [divmod(j * step_by % near, gy) for j in range(near)]
    part_order = list(range(count - 1, 0, -1))
    kinds = [(w, h) for w in reversed(range(wings)) for h in range(halves)]

    def near_index(j):
        a, b = offsets[j]
        return rows_at[a] * gy + across_at[b]

    def near_place(j):
        a, b = offsets[j]
        return (first_x + rows_at[a], across_at[b])

    def columns(j, w, h):
        start = ((first_x + w * half_gx) % gx * gy + near_index(j)) * cols + h * LANES
        return pl.ds(pl.multiple_of(start, LANES), LANES)

    barrier = pltpu.get_barrier_semaphore()

    partner = ((ix + half_gx) % gx, iy)
    wing = me // near
    first_wing = wing == 0
    last_wing = wing == wings - 1

    def greet(j):
        pl.semaphore_signal(barrier, inc=1, device_id=near_place(j), device_id_type=MESH)

    inputs = [
        pltpu.make_async_copy(source, target, input_sem.at[e])
        for e, (source, target) in enumerate(
            [
                (lists_hbm, lists_ref),
                (target_hbm, target_ref),
                (reg_hbm, reg_ref),
                (adjacency_hbm, adjacency_ref),
            ]
        )
    ]
    inputs[0].start()
    inputs[1].start()
    for j in range(1, near):
        greet(j)
    if wings > 1:

        @pl.when(first_wing)
        def _():
            pl.semaphore_signal(barrier, inc=1, device_id=partner, device_id_type=MESH)

    inputs[2].start()
    inputs[3].start()
    voxel_copy = pltpu.make_async_copy(voxel_hbm, voxel, voxel_sem)
    voxel_copy.start()
    for q, (w, h) in enumerate(kinds):
        pltpu.make_async_copy(
            feats_hbm.at[:, columns(0, w, h)], got.at[q, 0], feat_recv.at[q, 0]
        ).start()
    halo[...] = jnp.zeros_like(halo)
    acc[...] = jnp.zeros_like(acc)
    gather[...] = jnp.zeros_like(gather)

    def feat_copy(q, j):
        return pltpu.make_async_remote_copy(
            src_ref=feats_hbm.at[:, columns(j, *kinds[q])],
            dst_ref=got.at[q, j],
            send_sem=feat_send.at[0],
            recv_sem=feat_recv.at[q, j // group],
            device_id=near_place(j),
            device_id_type=MESH,
        )

    def extra_copy(j):
        return pltpu.make_async_remote_copy(
            src_ref=extra.at[near_index(j)],
            dst_ref=got_extra.at[j],
            send_sem=extra_send.at[0],
            recv_sem=extra_recv.at[0],
            device_id=near_place(j),
            device_id_type=MESH,
        )

    groups = total_bricks // LANES
    wide = slots * LANES
    inputs[0].wait()
    listed = lists_ref[...]
    offset = listed - slots * lax.broadcasted_iota(jnp.int32, listed.shape, 1)
    offset = jnp.where(listed >= 0, offset, -1)
    hits = jnp.concatenate(
        [
            jnp.max(jnp.where(offset == d, 1.0, 0.0), axis=0, keepdims=True)
            for d in range(slots)
        ],
        axis=0,
    )
    hits = jnp.concatenate(
        [hits[:, g * LANES : (g + 1) * LANES] for g in range(groups)], axis=0
    ).astype(jnp.bfloat16)
    spread = jnp.where(
        lax.broadcasted_iota(jnp.int32, (LANES, wide), 1) // slots
        == lax.broadcasted_iota(jnp.int32, (LANES, wide), 0),
        1.0,
        0.0,
    ).astype(jnp.bfloat16)
    spread_hits = jnp.dot(hits, spread, preferred_element_type=jnp.float32)
    same = (
        lax.broadcasted_iota(jnp.int32, (slots, wide), 1) % slots
        == lax.broadcasted_iota(jnp.int32, (slots, wide), 0)
    )
    live_rows = jnp.sum(
        jnp.where(same[None], spread_hits.reshape(groups, slots, wide), 0.0), axis=1
    )
    for l in range(slots):
        flat[pl.ds(l, groups, stride=slots), :] = live_rows[:, l * LANES : (l + 1) * LANES]
    inputs[1].wait()
    marked_targets = jnp.where(flat[...] > 0.0, target_ref[...].astype(jnp.float32), UNUSED)
    for k in range(count):
        from_me = (k // near + wings - wing) % wings if wings > 1 else 0
        for h in range(halves):
            row = k * halves + h
            extra[k % near, from_me, h : h + 1] = marked_targets[row : row + 1].astype(jnp.bfloat16)
    pltpu.make_async_copy(extra.at[me % near], got_extra.at[0], extra_recv.at[0]).start()

    pl.semaphore_wait(barrier, near - 1 + wing)
    if wings > 1:

        @pl.when(last_wing)
        def _():
            pl.semaphore_signal(ready, inc=1, device_id=partner, device_id_type=MESH)


    for j in range(1, near):
        extra_copy(j).start()
    for q in range(len(kinds)):
        for j in range(1, near):
            feat_copy(q, j).start()
    voxel_copy.wait()
    inputs[2].wait()
    inputs[3].wait()
    square[...] = jnp.zeros_like(square)

    def squares(t, _):
        for u in range(4):
            b = t * 4 + u
            rows = pl.ds(pl.multiple_of(b * feat, feat), feat)
            square[rows, 0:feat] = lax.dot_general(
                voxel[b],
                voxel[b],
                (((1,), (1,)), ((), ())),
                precision=lax.Precision.HIGHEST,
                preferred_element_type=jnp.float32,
            )
        return 0

    lax.fori_loop(0, bricks // 4, squares, 0)
    linked = jnp.where(adjacency_ref[...] >= 0, 1.0, 0.0)
    same_brick = lax.broadcasted_iota(jnp.int32, (bricks, bricks), 0) == lax.broadcasted_iota(
        jnp.int32, (bricks, bricks), 1
    )
    weights = [
        jnp.sum(jnp.where(same_brick, linked[k : k + 1], 0.0), axis=1, keepdims=True)
        for k in range(4)
    ]
    masks = [w > 0.0 for w in weights]
    degree = weights[0] + weights[1] + weights[2] + weights[3]

    span_all = group * LANES
    owner = (lax.broadcasted_iota(jnp.int32, (1, span_all), 1) // slots) % per_half
    across = [jnp.where(owner % side == j, 1.0, 0.0).astype(jnp.bfloat16) for j in range(side)]
    along = owner // side == lax.broadcasted_iota(jnp.int32, (16, span_all), 0)

    def arrived(ref, sem):
        return pltpu.make_async_remote_copy(
            src_ref=ref,
            dst_ref=ref,
            send_sem=feat_send.at[0],
            recv_sem=sem,
            device_id=near_place(1),
            device_id_type=MESH,
        )

    def absorb(q):
        w, h = kinds[q]

        def some(g, _):
            mine = pl.ds(g * group, group)
            arrived(got.at[q, mine], feat_recv.at[q, g]).wait_recv()
            x = jnp.concatenate([got[q, g * group + u] for u in range(group)], axis=1)
            more = jnp.concatenate(
                [got_extra[g * group + u, w].astype(jnp.float32) for u in range(group)], axis=1
            )
            target = more[h : h + 1]
            live = jnp.where(along & (target < UNUSED), 1.0, 0.0)
            marked = live * target
            left = jnp.concatenate(
                [x * live[i : i + 1].astype(jnp.bfloat16) for i in range(tall)]
                + [marked.astype(jnp.bfloat16)],
                axis=0,
            )
            right = jnp.concatenate([x * mask for mask in across], axis=0)
            found = lax.dot_general(
                left, right, (((1,), (1,)), ((), ())), preferred_element_type=jnp.float32
            )
            acc[w, h * LANES : (h + 1) * LANES, :] += found[:LANES]
            gather[w, h * tall : (h + 1) * tall, :] += found[LANES : LANES + tall]
            return 0

        lax.fori_loop(0, near // group, some, 0)

    def far_copy(source, target, e):
        return pltpu.make_async_remote_copy(
            src_ref=source,
            dst_ref=target,
            send_sem=far_send.at[e],
            recv_sem=far_recv.at[e],
            device_id=partner,
            device_id_type=MESH,
        )

    tiles = feat // SUBLANES
    middle = tiles // 2
    in_block = lax.broadcasted_iota(jnp.int32, (SUBLANES, LANES), 1) % feat
    lane_block = lax.broadcasted_iota(jnp.int32, (1, LANES), 1) // feat

    def pack(h):
        found = []
        for i in range(0, tall, 2):
            rows = [
                [
                    acc[1, pl.ds(h * LANES + (i + k) * feat + r * SUBLANES, SUBLANES), :]
                    for r in range(tiles)
                ]
                for k in range(2)
            ]
            found = found + [rows[0][0], rows[1][0]]
            for k in range(2):
                for r in range(1, middle):
                    turned = pltpu.roll(rows[k][tiles - r], r * SUBLANES, 1)
                    found.append(jnp.where(in_block >= r * SUBLANES, rows[k][r], turned))
            turned = pltpu.roll(rows[1][middle], middle * SUBLANES, 1)
            found.append(jnp.where(in_block >= middle * SUBLANES, rows[0][middle], turned))
        packed = jnp.concatenate(found, axis=0)
        acc_sent[h * packed.shape[0] : (h + 1) * packed.shape[0], :] = packed

    def unpack_far(h):
        upper, above = [], []
        each = tiles + 1
        for i in range(0, tall, 2):
            start = (h * tall // 2 + i // 2) * each
            given = [
                acc_far[pl.ds((start + r) * SUBLANES, SUBLANES), :] for r in range(each)
            ]
            for k in range(2):
                rows = [given[k]] + [None] * (tiles - 1)
                for r in range(1, middle):
                    both = given[2 + k * (middle - 1) + r - 1]
                    rows[r] = both
                    rows[tiles - r] = pltpu.roll(both, LANES - r * SUBLANES, 1)
                last_tile = given[each - 1]
                rows[middle] = (
                    pltpu.roll(last_tile, LANES - middle * SUBLANES, 1) if k else last_tile
                )
                for r in range(tiles):
                    upper.append(jnp.where(in_block >= r * SUBLANES, rows[r], 0.0))
                    above.append(jnp.where(in_block >= (r + 1) * SUBLANES, rows[r], 0.0))
        turned = jnp.concatenate(above, axis=0).T
        below = []
        for i in range(tall):
            mine = jnp.zeros((feat, LANES), jnp.float32)
            for j in range(side):
                band = turned[j * feat : (j + 1) * feat]
                if i != j:
                    band = pltpu.roll(band, (j - i) % side * feat, 1)
                mine = jnp.where(lane_block == j, band, mine)
            below.append(mine)
        rows = slice(h * LANES, (h + 1) * LANES)
        acc[0, rows, :] += jnp.concatenate(upper, axis=0) + jnp.concatenate(below, axis=0)

    def far_moments(h):
        half = acc_sent.shape[0] // halves
        rows = pl.ds(h * half, half)
        return far_copy(acc_sent.at[rows], acc_far.at[rows], 0)

    far_gather = far_copy(gather.at[1], gather_far, 1)
    all_far_moments = far_copy(acc_sent, acc_far, 0)

    arrived(got_extra, extra_recv.at[0]).wait_recv()
    for q, (w, h) in enumerate(kinds):
        absorb(q)
        if w:
            pack(h)
            if h == 0:

                @pl.when(first_wing)
                def _():
                    pl.semaphore_wait(ready, 1)

            if h + 1 == halves:
                far_gather.start()

            @pl.when(last_wing)
            def _():
                far_moments(h).start()

            if h in [0]:

                @pl.when(first_wing)
                def _():
                    far_moments(h).start()

        elif wings > 1 and h in {1: [1]}:

            @pl.when(first_wing)
            def _():
                for e in {1: [1]}[h]:
                    far_moments(e).start()

    def unpack(ref, rows):
        for e in range(side):
            turned = rows if e == 0 else pltpu.roll(rows, LANES - e * feat, 1)
            ref[pl.ds(e, bricks // side, stride=side), :] = turned

    found_gather = gather[0]
    if wings > 1:
        far_gather.wait_recv()
        found_gather = found_gather + gather_far[...]
    unpack(g_ref, found_gather)

    eye = lax.broadcasted_iota(jnp.int32, (1, feat, LANES), 1) == lax.broadcasted_iota(
        jnp.int32, (1, feat, LANES), 2
    )
    chunks = bricks // CHUNK
    in_feat = lax.broadcasted_iota(jnp.int32, (bricks, LANES), 1) < feat

    def at(t):
        return pl.ds(pl.multiple_of(t * CHUNK, CHUNK), CHUNK)

    def block(ref, t):
        rows = pl.ds(pl.multiple_of(t * CHUNK * feat, CHUNK * feat), CHUNK * feat)
        return ref[rows, :].reshape(CHUNK, feat, LANES)

    def as_column(rows):
        return jnp.sum(jnp.where(eye, rows[:, None, :], 0.0), axis=2, keepdims=True)

    def gathered(t):
        return as_column(g_ref[at(t), :])

    def moments_times(step):
        for t in range(chunks):
            z_column = as_column(z_ref[step, at(t), :]).reshape(CHUNK // side, side, feat, 1)
            spread_column = z_column[:, 0]
            for e in range(1, side):
                spread_column = jnp.where(lane_block == e, z_column[:, e], spread_column)
            rows = CHUNK // side * feat
            packed = acc[0, t * rows : (t + 1) * rows, :].reshape(CHUNK // side, feat, LANES)
            mz_ref[t * (CHUNK // side) : (t + 1) * (CHUNK // side), :] = jnp.sum(
                packed * spread_column, axis=1
            )
        unpack(my_ref, mz_ref[...])

    here = [ix > 0, ix < gx - 1, iy > 0, iy < gy - 1]
    beside = [(ix - 1, iy), (ix + 1, iy), (ix, iy - 1), (ix, iy + 1)]

    def halo_copy(step, k):
        if k < 2:
            source = z_ref.at[step, pl.ds(k * (bricks - BY), BY)]
            target = halo.at[step, k ^ 1, pl.ds(0, BY)]
        else:
            source = y_send.at[step, k - 2]
            target = halo.at[step, k ^ 1]
        return pltpu.make_async_remote_copy(
            src_ref=source,
            dst_ref=target,
            send_sem=halo_send.at[k],
            recv_sem=halo_recv.at[step % 2, k ^ 1],
            device_id=beside[k],
            device_id_type=MESH,
        )

    def halo_arrived(step, k):
        return pltpu.make_async_remote_copy(
            src_ref=halo.at[step, k, pl.ds(0, BY if k < 2 else BX)],
            dst_ref=halo.at[step, k, pl.ds(0, BY if k < 2 else BX)],
            send_sem=halo_send.at[k],
            recv_sem=halo_recv.at[step % 2, k],
            device_id=beside[k],
            device_id_type=MESH,
        )

    def send_halos(step, ks):
        for k in ks:

            @pl.when(here[k])
            def _():
                halo_copy(step, k).start()

    def produce(step, make):
        for t in (0, chunks - 1):
            z_ref[step, at(t), :] = make(t)
        send_halos(step, (0, 1))
        for t in range(1, chunks - 1):
            z_ref[step, at(t), :] = make(t)
        for e in range(2):
            y_send[step, e] = z_ref[step, pl.ds(e * (BY - 1), BX, stride=BY), :]
        send_halos(step, (2, 3))

    produce(0, lambda t: jnp.sum(block(square, t) * gathered(t), axis=1))

    def part_copy(j):
        a, b = divmod(j, gy)
        return pltpu.make_async_remote_copy(
            src_ref=part,
            dst_ref=parts.at[j],
            send_sem=part_send.at[0],
            recv_sem=part_recv.at[0],
            device_id=(all_rows_at[a], across_at[b]),
            device_id_type=MESH,
        )

    def sent(ref, sem):
        pltpu.make_async_remote_copy(
            src_ref=ref,
            dst_ref=ref,
            send_sem=sem,
            recv_sem=part_recv.at[0],
            device_id=near_place(1),
            device_id_type=MESH,
        ).wait_send()

    def fold(values):
        total = jnp.sum(values, axis=0, keepdims=True)
        width = total.shape[1]
        return sum(total[:, c : c + LANES] for c in range(0, width, LANES))

    def next_basis(step, t):
        if step == 0:
            return jnp.sum(voxel[at(t)] * gathered(t), axis=1)
        back = jnp.sum(voxel[at(t)] * as_column(mid_ref[at(t), :]), axis=1)
        shifted = (reg_ref[at(t), :] - SHIFTS[step - 1]) * basis[step - 1, at(t), :]
        return SCALE * (back + shifted)

    def operate(step):
        def widen(t, _):
            made = next_basis(step, t)
            basis[step, at(t), :] = made
            if step + 1 < ITERS:
                weighted = reg_ref[at(t), :] * made
                column = jnp.sum(voxel[at(t)] * weighted[:, None, :], axis=2, keepdims=True)
                q_ref[at(t), :] = jnp.sum(jnp.where(eye, column, 0.0), axis=1)
            return 0

        lax.fori_loop(0, chunks, widen, 0)
        if step == 0 and wings > 1:
            all_far_moments.wait_recv()
            for h in range(halves):
                unpack_far(h)
        moments_times(step)
        z = z_ref[step]
        ym_ref[1:bricks, :] = z[: bricks - 1]
        yp_ref[0 : bricks - 1, :] = z[1:]
        found = []
        if step + 1 == ITERS:
            found = [fold(basis[a] * basis[b]) for a, b in early]
            final = (reg_ref[...] - SHIFTS[step]) * basis[step]
            found = found + [fold(basis[a] * final) for a, b in late]
        for k in range(4):

            @pl.when(here[k])
            def _():
                halo_arrived(step, k).wait_recv()
                halo_copy(step, k).wait_send()

        xm = jnp.concatenate([halo[step, 0][:BY], z[: bricks - BY]], axis=0)
        xp = jnp.concatenate([z[BY:], halo[step, 1][:BY]], axis=0)
        ym_ref[pl.ds(0, BX, stride=BY), :] = halo[step, 2]
        yp_ref[pl.ds(BY - 1, BX, stride=BY), :] = halo[step, 3]
        near = jnp.where(masks[0], xm, 0.0) + jnp.where(masks[1], xp, 0.0)
        near = near + jnp.where(masks[2], ym_ref[...], 0.0) + jnp.where(masks[3], yp_ref[...], 0.0)
        mid = jnp.where(in_feat, my_ref[...] + coupling_weight * (degree * z - near), 0.0)
        mid_ref[...] = mid

        if step + 1 < ITERS:

            def advance(t):
                back = jnp.sum(block(square, t) * as_column(mid_ref[at(t), :]), axis=1)
                shifted = q_ref[at(t), :] - SHIFTS[step] * z_ref[step, at(t), :]
                return SCALE * (back + shifted)

            produce(step + 1, advance)
        else:
            for e, (a, b) in enumerate(late):
                e += len(early)
                found[e] = SCALE * (found[e] + fold(z_ref[a] * mid))
        return found

    early = [(a, b) for a in range(ITERS) for b in range(a, ITERS)]
    late = [(a, ITERS) for a in range(ITERS)]
    pairs = early + late
    rows = []
    for step in range(ITERS):
        rows = operate(step)
    rows = rows + [jnp.zeros_like(rows[0])] * (-len(rows) % 8)
    sums = jnp.sum(jnp.concatenate(rows, axis=0), axis=1, keepdims=True)
    entry = lax.broadcasted_iota(jnp.int32, (len(rows), LANES), 1)
    diagonal = entry == lax.broadcasted_iota(jnp.int32, (len(rows), LANES), 0)
    mine = jnp.sum(jnp.where(diagonal, sums, 0.0), axis=0, keepdims=True)
    part[...] = mine
    parts[0] = mine

    for j in part_order:
        part_copy(j).start()

    def last(t, _):
        basis[ITERS, at(t), :] = next_basis(ITERS, t)
        return 0

    lax.fori_loop(0, chunks, last, 0)

    sent(got.at[:, pl.ds(1, near - 1)], feat_send.at[0])
    sent(got_extra.at[pl.ds(1, near - 1)], extra_send.at[0])
    if wings > 1:
        far_gather.wait_send()
        all_far_moments.wait_send()
    others = parts.at[pl.ds(1, count - 1)]
    sent(others, part_send.at[0])
    arrived(others, part_recv.at[0]).wait_recv()
    total = jnp.sum(parts[...], axis=0)
    spread_total = jnp.sum(
        jnp.where(diagonal, jnp.broadcast_to(total, diagonal.shape), 0.0), axis=1, keepdims=True
    )
    gram = {}
    for e, (a, b) in enumerate(pairs):
        gram[a, b] = gram[b, a] = spread_total[e : e + 1]

    def inner(left, right):
        terms = [
            left[a] * right[b] * gram[a, b] for a in range(len(left)) for b in range(len(right))
        ]
        return functools.reduce(lambda p, q: p + q, terms)

    def apply(coefficients):
        size = len(coefficients)
        out = [SHIFTS[k] * coefficients[k] for k in range(size)]
        out.append(coefficients[-1] * (1.0 / SCALE))
        for k in range(1, size):
            out[k] = out[k] + coefficients[k - 1] * (1.0 / SCALE)
        return out

    one = jnp.ones((1, 1), jnp.float32)
    res, direction, answer = [one], [one], []
    norm_now = gram[0, 0]
    for step in range(ITERS):
        before_answer, before_res = answer, res
        image = apply(direction)
        alpha = norm_now / inner(direction, image)
        padded = answer + [jnp.zeros_like(one)] * (len(direction) - len(answer))
        answer = [p + alpha * d for p, d in zip(padded, direction)]
        res = [p - alpha * w for p, w in zip(res + [jnp.zeros_like(one)], image)]
        if step + 1 < ITERS:
            norm_next = inner(res, res)
            ratio = norm_next / norm_now
            direction = [
                p + ratio * d for p, d in zip(res, direction + [jnp.zeros_like(one)])
            ]
            norm_now = norm_next
    def combine(coefficients):
        return functools.reduce(
            lambda p, q: p + q, [c * basis[k] for k, c in enumerate(coefficients)]
        )

    answer_ref[...] = combine(before_answer)
    res_ref[...] = combine(before_res)
    direction_ref[...] = combine(direction)
    image_ref[...] = combine(image)
    alpha_ref[...] = jnp.broadcast_to(alpha, alpha_ref.shape)


def shards(gx, gy, point_feats, point_targets, point_lists, brick_adjacency, voxel_feats, voxel_reg):
    feat = point_feats.shape[0]
    brick_total, slots = point_lists.shape
    bricks, _, vox = voxel_feats.shape
    count = gx * gy
    cols = bricks * slots
    wings = 2 if gx % 2 == 0 else 1
    kept = bricks * feat * (feat + SUBLANES) // 2 // LANES
    near = count // wings
    group = 16
    while near % group:
        group //= 2
    vmem = pl.BlockSpec(memory_space=pltpu.VMEM)
    hbm = pl.BlockSpec(memory_space=pltpu.HBM)
    f32 = jnp.float32
    answer, res, direction, image, alpha = pl.pallas_call(
        functools.partial(kernel, gx, gy),
        out_shape=(pltpu.VMEM((bricks, vox), f32),) * 4 + (pltpu.VMEM((1, vox), f32),),
        in_specs=[hbm] * 6,
        out_specs=(vmem,) * 5,
        scratch_shapes=[
            pltpu.VMEM((wings * cols // LANES, near, feat, LANES), jnp.bfloat16),
            pltpu.VMEM((near, wings, cols // LANES, LANES), jnp.bfloat16),
            pltpu.VMEM((near, wings, cols // LANES, LANES), jnp.bfloat16),
            pltpu.VMEM((kept, LANES), f32),
            pltpu.VMEM((kept, LANES), f32),
            pltpu.VMEM((bricks * feat // LANES, LANES), f32),
            pltpu.VMEM((count * cols // LANES, LANES), f32),
            pltpu.VMEM((bricks, feat, vox), f32),
            pltpu.VMEM((wings, bricks * feat * feat // LANES, LANES), f32),
            pltpu.VMEM((wings, bricks * feat // LANES, LANES), f32),
            pltpu.VMEM((bricks * feat // LANES, LANES), f32),
            pltpu.VMEM((bricks, LANES), f32),
            pltpu.VMEM((bricks * feat, LANES), f32),
            pltpu.VMEM((ITERS + 1, bricks, vox), f32),
            pltpu.VMEM((ITERS, bricks, LANES), f32),
            pltpu.VMEM((bricks, LANES), f32),
            pltpu.VMEM((bricks, LANES), f32),
            pltpu.VMEM((bricks, LANES), f32),
            pltpu.VMEM((bricks, LANES), f32),
            pltpu.VMEM((bricks, LANES), f32),
            pltpu.VMEM((ITERS, 2, BX, LANES), f32),
            pltpu.VMEM((ITERS, 4, 8, LANES), f32),
            pltpu.VMEM((1, LANES), f32),
            pltpu.VMEM((count, 1, LANES), f32),
            pltpu.VMEM((count * cols // LANES, LANES), point_targets.dtype),
            pltpu.VMEM((slots, brick_total), jnp.int32),
            pltpu.VMEM((4, bricks), jnp.int32),
            pltpu.VMEM((bricks, vox), f32),
            pltpu.SemaphoreType.DMA,
            pltpu.SemaphoreType.DMA((4,)),
            pltpu.SemaphoreType.DMA((1,)),
            pltpu.SemaphoreType.DMA((wings * cols // LANES, near // group)),
            pltpu.SemaphoreType.DMA((1,)),
            pltpu.SemaphoreType.DMA((1,)),
            pltpu.SemaphoreType.DMA((2,)),
            pltpu.SemaphoreType.DMA((2,)),
            pltpu.SemaphoreType.DMA((4,)),
            pltpu.SemaphoreType.DMA((2, 4)),
            pltpu.SemaphoreType.DMA((1,)),
            pltpu.SemaphoreType.DMA((1,)),
            pltpu.SemaphoreType.REGULAR,
        ],
        compiler_params=pltpu.CompilerParams(collective_id=0, has_side_effects=True, vmem_limit_bytes=16 * 1024 * 1024),
    )(
        *(
            pltpu.with_memory_space_constraint(x, pltpu.HBM)
            for x in (
                point_feats,
                point_targets.reshape(-1, LANES),
                point_lists.T,
                brick_adjacency.T,
                voxel_feats,
                voxel_reg,
            )
        )
    )
    return answer + alpha * direction, res - alpha * image


def solution(mesh):
    placed = (
        P(None, ("gx", "gy")),
        P(("gx", "gy")),
        P(("gx", "gy"), None),
        P(("gx", "gy"), None),
        P(("gx", "gy"), None, None),
        P(("gx", "gy"), None),
    )
    return jax.shard_map(
        functools.partial(shards, mesh.shape["gx"], mesh.shape["gy"]),
        mesh=mesh,
        in_specs=placed,
        out_specs=(P(("gx", "gy"), None), P(("gx", "gy"), None)),
        check_vma=False,
    )
```

```python
import functools
import math

import jax
import jax.numpy as jnp
from jax import lax
from jax.experimental import pallas as pl
from jax.experimental.pallas import tpu as pltpu
from jax.sharding import PartitionSpec as P

BX = 8
BY = 4
ITERS = 3
LANES = 128
SUBLANES = 8
CHUNK = 8
MESH = pl.DeviceIdType.MESH
STRIDE = 11
SCALE = 2.0**-8
WINGS = 2
HOLD_BACK = True
DIRECT_LAST = True
DIRECT = (0,)
UNUSED = 256.0
SHIFTS = (8.0, 1.0, 4.0)

coupling_weight = 1.0


def kernel(
    gx,
    gy,
    feats_hbm,
    target_hbm,
    lists_hbm,
    adjacency_hbm,
    voxel_hbm,
    reg_hbm,
    answer_ref,
    res_ref,
    direction_ref,
    image_ref,
    alpha_ref,
    got,
    got_extra,
    extra,
    acc_sent,
    acc_far,
    gather_far,
    flat,
    voxel,
    acc,
    gather,
    mz_ref,
    g_ref,
    square,
    basis,
    z_ref,
    q_ref,
    my_ref,
    mid_ref,
    ym_ref,
    yp_ref,
    y_send,
    halo,
    part,
    parts,
    target_ref,
    lists_ref,
    adjacency_ref,
    reg_ref,
    voxel_sem,
    input_sem,
    feat_send,
    feat_recv,
    extra_send,
    extra_recv,
    far_send,
    far_recv,
    halo_send,
    halo_recv,
    part_send,
    part_recv,
    ready,
):
    count = gx * gy
    ix, iy = lax.axis_index("gx"), lax.axis_index("gy")
    me = ix * gy + iy
    feat = got.shape[2]
    total_bricks, slots = lists_ref.shape[1], lists_ref.shape[0]
    near = got.shape[1]
    wings = WINGS
    wing = me // near
    plane = near // 2
    chunk = math.gcd(plane, CHUNK)
    bricks = reg_ref.shape[0]
    cols = bricks * slots
    halves = cols // LANES
    per_half = LANES // slots
    side = LANES // feat
    tall = per_half // side

    half_gx = gx // wings
    deep = half_gx // 2
    first_x = wing * half_gx
    layer = ix // deep % 2
    inner = (layer + wing) % 2
    gives = inner * wing
    takes = inner * (1 - wing)
    relays = 1 - wing * (1 - inner)
    rows_at = [
        [first_x + (layer + p) % 2 * deep + (ix % deep + a) % deep for a in range(deep)]
        for p in range(2)
    ]
    across_at = [(iy + b) % gy for b in range(gy)]
    all_rows_at = [(ix + a) % gx for a in range(gx)]
    step_by = STRIDE if math.gcd(STRIDE, plane) == 1 else 1
    offsets = [
        (j // plane,) + divmod(j % plane * step_by % plane, gy) for j in range(near)
    ]
    part_order = list(range(count - 1, 0, -1))

    def near_x(j):
        p, a, _ = offsets[j]
        return rows_at[p][a]

    def near_y(j):
        return across_at[offsets[j][2]]

    def near_index(j):
        return (near_x(j) - first_x) * gy + near_y(j)

    def near_place(j):
        return (near_x(j), near_y(j))

    def far_place(j):
        return ((near_x(j) + half_gx) % gx, near_y(j))

    def columns(j, w, h):
        start = ((near_x(j) + w * half_gx) % gx * gy + near_y(j)) * cols + h * LANES
        return pl.ds(pl.multiple_of(start, LANES), LANES)

    barrier = pltpu.get_barrier_semaphore()

    partner = ((ix + half_gx) % gx, iy)
    first_wing = wing == 0
    last_wing = wing == wings - 1

    def greet(j):
        pl.semaphore_signal(barrier, inc=1, device_id=near_place(j), device_id_type=MESH)

    inputs = [
        pltpu.make_async_copy(source, target, input_sem.at[e])
        for e, (source, target) in enumerate(
            [
                (lists_hbm, lists_ref),
                (target_hbm, target_ref),
                (reg_hbm, reg_ref),
                (adjacency_hbm, adjacency_ref),
            ]
        )
    ]
    inputs[0].start()
    inputs[1].start()
    for j in range(1, near):
        greet(j)
    if wings > 1:

        @pl.when(first_wing)
        def _():
            pl.semaphore_signal(barrier, inc=1, device_id=partner, device_id_type=MESH)

        @pl.when(takes == 1)
        def _():
            for j in range(plane, near):
                pl.semaphore_signal(
                    barrier, inc=1, device_id=far_place(j), device_id_type=MESH
                )

    inputs[2].start()
    inputs[3].start()
    voxel_copy = pltpu.make_async_copy(voxel_hbm, voxel, voxel_sem)
    voxel_copy.start()
    for h in range(halves):
        for w in range(wings):
            kind = h + (1 - w) * halves
            pltpu.make_async_copy(
                feats_hbm.at[:, columns(0, w, h)], got.at[kind, 0], feat_recv.at[2 * kind]
            ).start()
    halo[...] = jnp.zeros_like(halo)
    acc[...] = jnp.zeros_like(acc)
    gather[...] = jnp.zeros_like(gather)

    def feat_copy(w, h, j):
        flip = gives if w and offsets[j][0] and h in DIRECT else 0
        kind = h + (1 - w) * halves
        return pltpu.make_async_remote_copy(
            src_ref=feats_hbm.at[:, columns(j, w, h)],
            dst_ref=got.at[kind + flip * 2 * halves, j],
            send_sem=feat_send.at[0],
            recv_sem=feat_recv.at[2 * kind + offsets[j][0] + flip * (4 * halves - h - 1)],
            device_id=((near_x(j) + flip * half_gx) % gx, near_y(j)),
            device_id_type=MESH,
        )

    def extra_copy(w, j):
        return pltpu.make_async_remote_copy(
            src_ref=extra.at[near_index(j), w],
            dst_ref=got_extra.at[1 - w, j],
            send_sem=extra_send.at[0],
            recv_sem=extra_recv.at[offsets[j][0] if w else 3],
            device_id=near_place(j),
            device_id_type=MESH,
        )

    def direct_extra_copy(j):
        return pltpu.make_async_remote_copy(
            src_ref=extra.at[near_index(j), 1],
            dst_ref=got_extra.at[2, j],
            send_sem=extra_send.at[1],
            recv_sem=extra_recv.at[2],
            device_id=far_place(j),
            device_id_type=MESH,
        )

    groups = total_bricks // LANES
    wide = slots * LANES
    inputs[0].wait()
    listed = lists_ref[...]
    offset = listed - slots * lax.broadcasted_iota(jnp.int32, listed.shape, 1)
    offset = jnp.where(listed >= 0, offset, -1)
    hits = jnp.concatenate(
        [
            jnp.max(jnp.where(offset == d, 1.0, 0.0), axis=0, keepdims=True)
            for d in range(slots)
        ],
        axis=0,
    )
    hits = jnp.concatenate(
        [hits[:, g * LANES : (g + 1) * LANES] for g in range(groups)], axis=0
    ).astype(jnp.bfloat16)
    spread = jnp.where(
        lax.broadcasted_iota(jnp.int32, (LANES, wide), 1) // slots
        == lax.broadcasted_iota(jnp.int32, (LANES, wide), 0),
        1.0,
        0.0,
    ).astype(jnp.bfloat16)
    spread_hits = jnp.dot(hits, spread, preferred_element_type=jnp.float32)
    same = (
        lax.broadcasted_iota(jnp.int32, (slots, wide), 1) % slots
        == lax.broadcasted_iota(jnp.int32, (slots, wide), 0)
    )
    live_rows = jnp.sum(
        jnp.where(same[None], spread_hits.reshape(groups, slots, wide), 0.0), axis=1
    )
    for l in range(slots):
        flat[pl.ds(l, groups, stride=slots), :] = live_rows[:, l * LANES : (l + 1) * LANES]
    inputs[1].wait()
    marked_targets = jnp.where(flat[...] > 0.0, target_ref[...].astype(jnp.float32), UNUSED)
    for k in range(count):
        from_me = (k // near + wings - wing) % wings if wings > 1 else 0
        for h in range(halves):
            row = k * halves + h
            extra[k % near, from_me, h : h + 1] = marked_targets[row : row + 1].astype(jnp.bfloat16)
    for w in range(wings):
        pltpu.make_async_copy(
            extra.at[me % near, w], got_extra.at[1 - w, 0], extra_recv.at[0 if w else 3]
        ).start()

    pl.semaphore_wait(barrier, near - 1 + wing + gives * plane)
    if wings > 1:

        @pl.when(last_wing)
        def _():
            pl.semaphore_signal(ready, inc=1, device_id=partner, device_id_type=MESH)

    for j in range(1, near):
        extra_copy(1, j).start()

    @pl.when(gives == 1)
    def _():
        for j in range(plane, near):
            direct_extra_copy(j).start()

    for h in range(halves):
        for j in range(1, near):
            feat_copy(1, h, j).start()
    for j in range(1, near):
        extra_copy(0, j).start()
    for h in range(halves):
        for j in range(1, near):
            feat_copy(0, h, j).start()
    voxel_copy.wait()
    inputs[2].wait()
    inputs[3].wait()
    square[...] = jnp.zeros_like(square)

    def squares(t, _):
        for u in range(4):
            b = t * 4 + u
            rows = pl.ds(pl.multiple_of(b * feat, feat), feat)
            square[rows, 0:feat] = lax.dot_general(
                voxel[b],
                voxel[b],
                (((1,), (1,)), ((), ())),
                precision=lax.Precision.HIGHEST,
                preferred_element_type=jnp.float32,
            )
        return 0

    lax.fori_loop(0, bricks // 4, squares, 0)

    linked = jnp.where(adjacency_ref[...] >= 0, 1.0, 0.0)
    same_brick = lax.broadcasted_iota(jnp.int32, (bricks, bricks), 0) == lax.broadcasted_iota(
        jnp.int32, (bricks, bricks), 1
    )
    weights = [
        jnp.sum(jnp.where(same_brick, linked[k : k + 1], 0.0), axis=1, keepdims=True)
        for k in range(4)
    ]
    masks = [w > 0.0 for w in weights]
    degree = weights[0] + weights[1] + weights[2] + weights[3]

    span_all = chunk * LANES
    owner = (lax.broadcasted_iota(jnp.int32, (1, span_all), 1) // slots) % per_half
    across = [jnp.where(owner % side == j, 1.0, 0.0).astype(jnp.bfloat16) for j in range(side)]
    along = owner // side == lax.broadcasted_iota(jnp.int32, (16, span_all), 0)

    def arrived(ref, sem):
        return pltpu.make_async_remote_copy(
            src_ref=ref,
            dst_ref=ref,
            send_sem=feat_send.at[0],
            recv_sem=sem,
            device_id=near_place(1),
            device_id_type=MESH,
        )

    def absorb(kind, p, w, h, role):
        first_slot = p * plane
        slots_of = pl.ds(first_slot, plane)
        sem = 8 + h if kind >= 2 * halves else 2 * kind + p
        arrived(got.at[kind, slots_of], feat_recv.at[sem]).wait_recv()

        def some(g, _):
            mine = [first_slot + g * chunk + u for u in range(chunk)]
            x = jnp.concatenate([got[kind, u] for u in mine], axis=1)
            target = jnp.concatenate(
                [got_extra[role, u].astype(jnp.float32)[h : h + 1] for u in mine], axis=1
            )
            live = jnp.where(along & (target < UNUSED), 1.0, 0.0)
            marked = live * target
            left = jnp.concatenate(
                [x * live[i : i + 1].astype(jnp.bfloat16) for i in range(tall)]
                + [marked.astype(jnp.bfloat16)],
                axis=0,
            )
            right = jnp.concatenate([x * mask for mask in across], axis=0)
            found = lax.dot_general(
                left, right, (((1,), (1,)), ((), ())), preferred_element_type=jnp.float32
            )
            acc[w, h * LANES : (h + 1) * LANES, :] += found[:LANES]
            gather[w, h * tall : (h + 1) * tall, :] += found[LANES : LANES + tall]
            return 0

        if plane == chunk:
            some(0, 0)
        else:
            lax.fori_loop(0, plane // chunk, some, 0)

    def far_copy(source, target, e):
        return pltpu.make_async_remote_copy(
            src_ref=source,
            dst_ref=target,
            send_sem=far_send.at[e],
            recv_sem=far_recv.at[e],
            device_id=partner,
            device_id_type=MESH,
        )

    tiles = feat // SUBLANES
    middle = tiles // 2
    in_block = lax.broadcasted_iota(jnp.int32, (SUBLANES, LANES), 1) % feat
    lane_block = lax.broadcasted_iota(jnp.int32, (1, LANES), 1) // feat

    def pack(h):
        found = []
        for i in range(0, tall, 2):
            rows = [
                [
                    acc[1, pl.ds(h * LANES + (i + k) * feat + r * SUBLANES, SUBLANES), :]
                    for r in range(tiles)
                ]
                for k in range(2)
            ]
            found = found + [rows[0][0], rows[1][0]]
            for k in range(2):
                for r in range(1, middle):
                    turned = pltpu.roll(rows[k][tiles - r], r * SUBLANES, 1)
                    found.append(jnp.where(in_block >= r * SUBLANES, rows[k][r], turned))
            turned = pltpu.roll(rows[1][middle], middle * SUBLANES, 1)
            found.append(jnp.where(in_block >= middle * SUBLANES, rows[0][middle], turned))
        packed = jnp.concatenate(found, axis=0)
        acc_sent[h * packed.shape[0] : (h + 1) * packed.shape[0], :] = packed

    def unpack_far(h):
        upper, above = [], []
        each = tiles + 1
        for i in range(0, tall, 2):
            start = (h * tall // 2 + i // 2) * each
            given = [
                acc_far[pl.ds((start + r) * SUBLANES, SUBLANES), :] for r in range(each)
            ]
            for k in range(2):
                rows = [given[k]] + [None] * (tiles - 1)
                for r in range(1, middle):
                    both = given[2 + k * (middle - 1) + r - 1]
                    rows[r] = both
                    rows[tiles - r] = pltpu.roll(both, LANES - r * SUBLANES, 1)
                last_tile = given[each - 1]
                rows[middle] = (
                    pltpu.roll(last_tile, LANES - middle * SUBLANES, 1) if k else last_tile
                )
                for r in range(tiles):
                    upper.append(jnp.where(in_block >= r * SUBLANES, rows[r], 0.0))
                    above.append(jnp.where(in_block >= (r + 1) * SUBLANES, rows[r], 0.0))
        turned = jnp.concatenate(above, axis=0).T
        below = []
        for i in range(tall):
            mine = jnp.zeros((feat, LANES), jnp.float32)
            for j in range(side):
                band = turned[j * feat : (j + 1) * feat]
                if i != j:
                    band = pltpu.roll(band, (j - i) % side * feat, 1)
                mine = jnp.where(lane_block == j, band, mine)
            below.append(mine)
        rows = slice(h * LANES, (h + 1) * LANES)
        acc[0, rows, :] += jnp.concatenate(upper, axis=0) + jnp.concatenate(below, axis=0)

    def far_moments(h):
        half = acc_sent.shape[0] // halves
        rows = pl.ds(h * half, half)
        return far_copy(acc_sent.at[rows], acc_far.at[rows], 0)

    far_gather = far_copy(gather.at[1], gather_far, 1)
    all_far_moments = far_copy(acc_sent, acc_far, 0)

    def extras_arrived(role, p, count_of, e):
        arrived(got_extra.at[role, pl.ds(p * plane, count_of)], extra_recv.at[e]).wait_recv()

    extras_arrived(0, 0, plane, 0)

    extras_arrived(0, 1, plane, 1)

    for h in range(halves):
        absorb(h, 0, 1, h, 0)

        if h in DIRECT:

            @pl.when(relays == 1)
            def _():
                absorb(h, 1, 1, h, 0)

        else:
            absorb(h, 1, 1, h, 0)

        pack(h)
        if h == 0:

            @pl.when(first_wing)
            def _():
                pl.semaphore_wait(ready, 1)

        if h + 1 == halves:
            far_gather.start()

        @pl.when(last_wing)
        def _():
            far_moments(h).start()

        if h + 1 < halves or not HOLD_BACK:

            @pl.when(first_wing)
            def _():
                far_moments(h).start()

    def absorb_direct():
        @pl.when(takes == 1)
        def _():
            extras_arrived(2, 1, plane, 2)
            for h in DIRECT:
                absorb(2 * halves + h, 1, 0, h, 2)

    if not DIRECT_LAST:
        absorb_direct()
    extras_arrived(1, 0, near, 3)
    for h in range(halves):
        for p in range(2):
            absorb(halves + h, p, 0, h, 1)
    if HOLD_BACK:

        @pl.when(first_wing)
        def _():
            far_moments(halves - 1).start()

    if DIRECT_LAST:
        absorb_direct()

    def unpack(ref, rows):
        for e in range(side):
            turned = rows if e == 0 else pltpu.roll(rows, LANES - e * feat, 1)
            ref[pl.ds(e, bricks // side, stride=side), :] = turned

    found_gather = gather[0]
    if wings > 1:
        far_gather.wait_recv()
        found_gather = found_gather + gather_far[...]
    unpack(g_ref, found_gather)

    eye = lax.broadcasted_iota(jnp.int32, (1, feat, LANES), 1) == lax.broadcasted_iota(
        jnp.int32, (1, feat, LANES), 2
    )
    chunks = bricks // CHUNK
    in_feat = lax.broadcasted_iota(jnp.int32, (bricks, LANES), 1) < feat

    def at(t):
        return pl.ds(pl.multiple_of(t * CHUNK, CHUNK), CHUNK)

    def block(ref, t):
        rows = pl.ds(pl.multiple_of(t * CHUNK * feat, CHUNK * feat), CHUNK * feat)
        return ref[rows, :].reshape(CHUNK, feat, LANES)

    def as_column(rows):
        return jnp.sum(jnp.where(eye, rows[:, None, :], 0.0), axis=2, keepdims=True)

    def gathered(t):
        return as_column(g_ref[at(t), :])

    def moments_times(step):
        for t in range(chunks):
            z_column = as_column(z_ref[step, at(t), :]).reshape(CHUNK // side, side, feat, 1)
            spread_column = z_column[:, 0]
            for e in range(1, side):
                spread_column = jnp.where(lane_block == e, z_column[:, e], spread_column)
            rows = CHUNK // side * feat
            packed = acc[0, t * rows : (t + 1) * rows, :].reshape(CHUNK // side, feat, LANES)
            mz_ref[t * (CHUNK // side) : (t + 1) * (CHUNK // side), :] = jnp.sum(
                packed * spread_column, axis=1
            )
        unpack(my_ref, mz_ref[...])

    here = [ix > 0, ix < gx - 1, iy > 0, iy < gy - 1]
    beside = [(ix - 1, iy), (ix + 1, iy), (ix, iy - 1), (ix, iy + 1)]

    def halo_copy(step, k):
        if k < 2:
            source = z_ref.at[step, pl.ds(k * (bricks - BY), BY)]
            target = halo.at[step, k ^ 1, pl.ds(0, BY)]
        else:
            source = y_send.at[step, k - 2]
            target = halo.at[step, k ^ 1]
        return pltpu.make_async_remote_copy(
            src_ref=source,
            dst_ref=target,
            send_sem=halo_send.at[k],
            recv_sem=halo_recv.at[step % 2, k ^ 1],
            device_id=beside[k],
            device_id_type=MESH,
        )

    def halo_arrived(step, k):
        return pltpu.make_async_remote_copy(
            src_ref=halo.at[step, k, pl.ds(0, BY if k < 2 else BX)],
            dst_ref=halo.at[step, k, pl.ds(0, BY if k < 2 else BX)],
            send_sem=halo_send.at[k],
            recv_sem=halo_recv.at[step % 2, k],
            device_id=beside[k],
            device_id_type=MESH,
        )

    def send_halos(step, ks):
        for k in ks:

            @pl.when(here[k])
            def _():
                halo_copy(step, k).start()

    def produce(step, make):
        for t in (0, chunks - 1):
            z_ref[step, at(t), :] = make(t)
        send_halos(step, (0, 1))
        for t in range(1, chunks - 1):
            z_ref[step, at(t), :] = make(t)
        for e in range(2):
            y_send[step, e] = z_ref[step, pl.ds(e * (BY - 1), BX, stride=BY), :]
        send_halos(step, (2, 3))

    produce(0, lambda t: jnp.sum(block(square, t) * gathered(t), axis=1))

    def part_copy(j):
        a, b = divmod(j, gy)
        return pltpu.make_async_remote_copy(
            src_ref=part,
            dst_ref=parts.at[j],
            send_sem=part_send.at[0],
            recv_sem=part_recv.at[0],
            device_id=(all_rows_at[a], across_at[b]),
            device_id_type=MESH,
        )

    def sent(ref, sem):
        pltpu.make_async_remote_copy(
            src_ref=ref,
            dst_ref=ref,
            send_sem=sem,
            recv_sem=part_recv.at[0],
            device_id=near_place(1),
            device_id_type=MESH,
        ).wait_send()

    def fold(values):
        total = jnp.sum(values, axis=0, keepdims=True)
        width = total.shape[1]
        return sum(total[:, c : c + LANES] for c in range(0, width, LANES))

    def next_basis(step, t):
        if step == 0:
            return jnp.sum(voxel[at(t)] * gathered(t), axis=1)
        back = jnp.sum(voxel[at(t)] * as_column(mid_ref[at(t), :]), axis=1)
        shifted = (reg_ref[at(t), :] - SHIFTS[step - 1]) * basis[step - 1, at(t), :]
        return SCALE * (back + shifted)

    def operate(step):
        def widen(t, _):
            made = next_basis(step, t)
            basis[step, at(t), :] = made
            if step + 1 < ITERS:
                weighted = reg_ref[at(t), :] * made
                column = jnp.sum(voxel[at(t)] * weighted[:, None, :], axis=2, keepdims=True)
                q_ref[at(t), :] = jnp.sum(jnp.where(eye, column, 0.0), axis=1)
            return 0

        lax.fori_loop(0, chunks, widen, 0)
        if step == 0 and wings > 1:
            all_far_moments.wait_recv()
            for h in range(halves):
                unpack_far(h)
        moments_times(step)
        z = z_ref[step]
        ym_ref[1:bricks, :] = z[: bricks - 1]
        yp_ref[0 : bricks - 1, :] = z[1:]
        found = []
        if step + 1 == ITERS:
            found = [fold(basis[a] * basis[b]) for a, b in early]
            final = (reg_ref[...] - SHIFTS[step]) * basis[step]
            found = found + [fold(basis[a] * final) for a, b in late]
        for k in range(4):

            @pl.when(here[k])
            def _():
                halo_arrived(step, k).wait_recv()
                halo_copy(step, k).wait_send()

        xm = jnp.concatenate([halo[step, 0][:BY], z[: bricks - BY]], axis=0)
        xp = jnp.concatenate([z[BY:], halo[step, 1][:BY]], axis=0)
        ym_ref[pl.ds(0, BX, stride=BY), :] = halo[step, 2]
        yp_ref[pl.ds(BY - 1, BX, stride=BY), :] = halo[step, 3]
        near = jnp.where(masks[0], xm, 0.0) + jnp.where(masks[1], xp, 0.0)
        near = near + jnp.where(masks[2], ym_ref[...], 0.0) + jnp.where(masks[3], yp_ref[...], 0.0)
        mid = jnp.where(in_feat, my_ref[...] + coupling_weight * (degree * z - near), 0.0)
        mid_ref[...] = mid

        if step + 1 < ITERS:

            def advance(t):
                back = jnp.sum(block(square, t) * as_column(mid_ref[at(t), :]), axis=1)
                shifted = q_ref[at(t), :] - SHIFTS[step] * z_ref[step, at(t), :]
                return SCALE * (back + shifted)

            produce(step + 1, advance)
        else:
            for e, (a, b) in enumerate(late):
                e += len(early)
                found[e] = SCALE * (found[e] + fold(z_ref[a] * mid))
        return found

    early = [(a, b) for a in range(ITERS) for b in range(a, ITERS)]
    late = [(a, ITERS) for a in range(ITERS)]
    pairs = early + late
    rows = []
    for step in range(ITERS):
        rows = operate(step)
    rows = rows + [jnp.zeros_like(rows[0])] * (-len(rows) % 8)
    sums = jnp.sum(jnp.concatenate(rows, axis=0), axis=1, keepdims=True)
    entry = lax.broadcasted_iota(jnp.int32, (len(rows), LANES), 1)
    diagonal = entry == lax.broadcasted_iota(jnp.int32, (len(rows), LANES), 0)
    mine = jnp.sum(jnp.where(diagonal, sums, 0.0), axis=0, keepdims=True)
    part[...] = mine
    parts[0] = mine

    for j in part_order:
        part_copy(j).start()

    def last(t, _):
        basis[ITERS, at(t), :] = next_basis(ITERS, t)
        return 0

    lax.fori_loop(0, chunks, last, 0)

    sent(got.at[pl.ds(0, 2 * halves), pl.ds(1, near - 1)], feat_send.at[0])
    sent(got_extra.at[pl.ds(0, 2), pl.ds(1, near - 1)], extra_send.at[0])

    @pl.when(gives == 1)
    def _():
        sent(got_extra.at[2, pl.ds(plane, plane)], extra_send.at[1])

    if wings > 1:
        far_gather.wait_send()
        all_far_moments.wait_send()
    others = parts.at[pl.ds(1, count - 1)]
    sent(others, part_send.at[0])
    arrived(others, part_recv.at[0]).wait_recv()
    total = jnp.sum(parts[...], axis=0)
    spread_total = jnp.sum(
        jnp.where(diagonal, jnp.broadcast_to(total, diagonal.shape), 0.0), axis=1, keepdims=True
    )
    gram = {}
    for e, (a, b) in enumerate(pairs):
        gram[a, b] = gram[b, a] = spread_total[e : e + 1]

    def inner(left, right):
        terms = [
            left[a] * right[b] * gram[a, b] for a in range(len(left)) for b in range(len(right))
        ]
        return functools.reduce(lambda p, q: p + q, terms)

    def apply(coefficients):
        size = len(coefficients)
        out = [SHIFTS[k] * coefficients[k] for k in range(size)]
        out.append(coefficients[-1] * (1.0 / SCALE))
        for k in range(1, size):
            out[k] = out[k] + coefficients[k - 1] * (1.0 / SCALE)
        return out

    one = jnp.ones((1, 1), jnp.float32)
    res, direction, answer = [one], [one], []
    norm_now = gram[0, 0]
    for step in range(ITERS):
        before_answer, before_res = answer, res
        image = apply(direction)
        alpha = norm_now / inner(direction, image)
        padded = answer + [jnp.zeros_like(one)] * (len(direction) - len(answer))
        answer = [p + alpha * d for p, d in zip(padded, direction)]
        res = [p - alpha * w for p, w in zip(res + [jnp.zeros_like(one)], image)]
        if step + 1 < ITERS:
            norm_next = inner(res, res)
            ratio = norm_next / norm_now
            direction = [
                p + ratio * d for p, d in zip(res, direction + [jnp.zeros_like(one)])
            ]
            norm_now = norm_next
    def combine(coefficients):
        return functools.reduce(
            lambda p, q: p + q, [c * basis[k] for k, c in enumerate(coefficients)]
        )

    answer_ref[...] = combine(before_answer)
    res_ref[...] = combine(before_res)
    direction_ref[...] = combine(direction)
    image_ref[...] = combine(image)
    alpha_ref[...] = jnp.broadcast_to(alpha, alpha_ref.shape)


def shards(gx, gy, point_feats, point_targets, point_lists, brick_adjacency, voxel_feats, voxel_reg):
    feat = point_feats.shape[0]
    brick_total, slots = point_lists.shape
    bricks, _, vox = voxel_feats.shape
    count = gx * gy
    cols = bricks * slots
    wings = WINGS
    halves = cols // LANES
    kept = bricks * feat * (feat + SUBLANES) // 2 // LANES
    near = count // wings
    vmem = pl.BlockSpec(memory_space=pltpu.VMEM)
    hbm = pl.BlockSpec(memory_space=pltpu.HBM)
    f32 = jnp.float32
    answer, res, direction, image, alpha = pl.pallas_call(
        functools.partial(kernel, gx, gy),
        out_shape=(pltpu.VMEM((bricks, vox), f32),) * 4 + (pltpu.VMEM((1, vox), f32),),
        in_specs=[hbm] * 6,
        out_specs=(vmem,) * 5,
        scratch_shapes=[
            pltpu.VMEM((3 * halves, near, feat, LANES), jnp.bfloat16),
            pltpu.VMEM((3, near, halves, LANES), jnp.bfloat16),
            pltpu.VMEM((near, wings, cols // LANES, LANES), jnp.bfloat16),
            pltpu.VMEM((kept, LANES), f32),
            pltpu.VMEM((kept, LANES), f32),
            pltpu.VMEM((bricks * feat // LANES, LANES), f32),
            pltpu.VMEM((count * cols // LANES, LANES), f32),
            pltpu.VMEM((bricks, feat, vox), f32),
            pltpu.VMEM((wings, bricks * feat * feat // LANES, LANES), f32),
            pltpu.VMEM((wings, bricks * feat // LANES, LANES), f32),
            pltpu.VMEM((bricks * feat // LANES, LANES), f32),
            pltpu.VMEM((bricks, LANES), f32),
            pltpu.VMEM((bricks * feat, LANES), f32),
            pltpu.VMEM((ITERS + 1, bricks, vox), f32),
            pltpu.VMEM((ITERS, bricks, LANES), f32),
            pltpu.VMEM((bricks, LANES), f32),
            pltpu.VMEM((bricks, LANES), f32),
            pltpu.VMEM((bricks, LANES), f32),
            pltpu.VMEM((bricks, LANES), f32),
            pltpu.VMEM((bricks, LANES), f32),
            pltpu.VMEM((ITERS, 2, BX, LANES), f32),
            pltpu.VMEM((ITERS, 4, 8, LANES), f32),
            pltpu.VMEM((1, LANES), f32),
            pltpu.VMEM((count, 1, LANES), f32),
            pltpu.VMEM((count * cols // LANES, LANES), point_targets.dtype),
            pltpu.VMEM((slots, brick_total), jnp.int32),
            pltpu.VMEM((4, bricks), jnp.int32),
            pltpu.VMEM((bricks, vox), f32),
            pltpu.SemaphoreType.DMA,
            pltpu.SemaphoreType.DMA((4,)),
            pltpu.SemaphoreType.DMA((1,)),
            pltpu.SemaphoreType.DMA((5 * halves,)),
            pltpu.SemaphoreType.DMA((2,)),
            pltpu.SemaphoreType.DMA((4,)),
            pltpu.SemaphoreType.DMA((2,)),
            pltpu.SemaphoreType.DMA((2,)),
            pltpu.SemaphoreType.DMA((4,)),
            pltpu.SemaphoreType.DMA((2, 4)),
            pltpu.SemaphoreType.DMA((1,)),
            pltpu.SemaphoreType.DMA((1,)),
            pltpu.SemaphoreType.REGULAR,
        ],
        compiler_params=pltpu.CompilerParams(collective_id=0, has_side_effects=True, vmem_limit_bytes=16 * 1024 * 1024),
    )(
        *(
            pltpu.with_memory_space_constraint(x, pltpu.HBM)
            for x in (
                point_feats,
                point_targets.reshape(-1, LANES),
                point_lists.T,
                brick_adjacency.T,
                voxel_feats,
                voxel_reg,
            )
        )
    )
    return answer + alpha * direction, res - alpha * image


def solution(mesh):
    placed = (
        P(None, ("gx", "gy")),
        P(("gx", "gy")),
        P(("gx", "gy"), None),
        P(("gx", "gy"), None),
        P(("gx", "gy"), None, None),
        P(("gx", "gy"), None),
    )
    return jax.shard_map(
        functools.partial(shards, mesh.shape["gx"], mesh.shape["gy"]),
        mesh=mesh,
        in_specs=placed,
        out_specs=(P(("gx", "gy"), None), P(("gx", "gy"), None)),
        check_vma=False,
    )
```

```python
import functools
import math

import jax
import jax.numpy as jnp
from jax import lax
from jax.experimental import pallas as pl
from jax.experimental.pallas import tpu as pltpu
from jax.sharding import PartitionSpec as P

BX = 8
BY = 4
ITERS = 3
LANES = 128
SUBLANES = 8
CHUNK = 8
MESH = pl.DeviceIdType.MESH
STRIDE = 11
SCALE = 2.0**-8
WINGS = 2
HOLD_BACK = True
DIRECT_LAST = True
DIRECT = (0,)
UNUSED = 256.0
SHIFTS = (8.0, 1.0, 4.0)

coupling_weight = 1.0


def kernel(
    gx,
    gy,
    feats_hbm,
    target_hbm,
    lists_hbm,
    adjacency_hbm,
    voxel_hbm,
    reg_hbm,
    answer_ref,
    res_ref,
    direction_ref,
    image_ref,
    alpha_ref,
    got,
    got_extra,
    extra,
    acc_sent,
    acc_far,
    gather_far,
    flat,
    voxel,
    acc,
    gather,
    mz_ref,
    g_ref,
    square,
    basis,
    z_ref,
    q_ref,
    my_ref,
    mid_ref,
    ym_ref,
    yp_ref,
    y_send,
    halo,
    part,
    parts,
    target_ref,
    lists_ref,
    adjacency_ref,
    reg_ref,
    voxel_sem,
    input_sem,
    feat_send,
    feat_recv,
    extra_send,
    extra_recv,
    far_send,
    far_recv,
    halo_send,
    halo_recv,
    part_send,
    part_recv,
    ready,
):
    count = gx * gy
    ix, iy = lax.axis_index("gx"), lax.axis_index("gy")
    me = ix * gy + iy
    feat = got.shape[2]
    total_bricks, slots = lists_ref.shape[1], lists_ref.shape[0]
    near = got.shape[1]
    wings = WINGS
    wing = me // near
    plane = near // 2
    chunk = math.gcd(plane, CHUNK)
    bricks = reg_ref.shape[0]
    cols = bricks * slots
    halves = cols // LANES
    per_half = LANES // slots
    side = LANES // feat
    tall = per_half // side

    half_gx = gx // wings
    deep = half_gx // 2
    first_x = wing * half_gx
    layer = ix // deep % 2
    inner = (layer + wing) % 2
    gives = inner * wing
    takes = inner * (1 - wing)
    relays = 1 - wing * (1 - inner)
    rows_at = [
        [first_x + (layer + p) % 2 * deep + (ix % deep + a) % deep for a in range(deep)]
        for p in range(2)
    ]
    across_at = [(iy + b) % gy for b in range(gy)]
    all_rows_at = [(ix + a) % gx for a in range(gx)]
    step_by = STRIDE if math.gcd(STRIDE, plane) == 1 else 1
    offsets = [
        (j // plane,) + divmod(j % plane * step_by % plane, gy) for j in range(near)
    ]
    part_order = list(range(count - 1, 0, -1))

    def near_x(j):
        p, a, _ = offsets[j]
        return rows_at[p][a]

    def near_y(j):
        return across_at[offsets[j][2]]

    def near_index(j):
        return (near_x(j) - first_x) * gy + near_y(j)

    def near_place(j):
        return (near_x(j), near_y(j))

    def far_place(j):
        return ((near_x(j) + half_gx) % gx, near_y(j))

    def columns(j, w, h):
        start = ((near_x(j) + w * half_gx) % gx * gy + near_y(j)) * cols + h * LANES
        return pl.ds(pl.multiple_of(start, LANES), LANES)

    barrier = pltpu.get_barrier_semaphore()

    partner = ((ix + half_gx) % gx, iy)
    first_wing = wing == 0
    last_wing = wing == wings - 1

    def greet(j):
        pl.semaphore_signal(barrier, inc=1, device_id=near_place(j), device_id_type=MESH)

    inputs = [
        pltpu.make_async_copy(source, target, input_sem.at[e])
        for e, (source, target) in enumerate(
            [
                (lists_hbm, lists_ref),
                (target_hbm, target_ref),
                (reg_hbm, reg_ref),
                (adjacency_hbm, adjacency_ref),
            ]
        )
    ]
    inputs[0].start()
    inputs[1].start()
    for j in range(1, near):
        greet(j)
    if wings > 1:

        @pl.when(first_wing)
        def _():
            pl.semaphore_signal(barrier, inc=1, device_id=partner, device_id_type=MESH)

        @pl.when(takes == 1)
        def _():
            for j in range(plane, near):
                pl.semaphore_signal(
                    barrier, inc=1, device_id=far_place(j), device_id_type=MESH
                )

    inputs[2].start()
    inputs[3].start()
    voxel_copy = pltpu.make_async_copy(voxel_hbm, voxel, voxel_sem)
    voxel_copy.start()
    for h in range(halves):
        for w in range(wings):
            kind = h + (1 - w) * halves
            pltpu.make_async_copy(
                feats_hbm.at[:, columns(0, w, h)], got.at[kind, 0], feat_recv.at[2 * kind]
            ).start()
    halo[...] = jnp.zeros_like(halo)
    acc[...] = jnp.zeros_like(acc)
    gather[...] = jnp.zeros_like(gather)

    def feat_copy(w, h, j):
        flip = gives if w and offsets[j][0] and h in DIRECT else 0
        kind = h + (1 - w) * halves
        return pltpu.make_async_remote_copy(
            src_ref=feats_hbm.at[:, columns(j, w, h)],
            dst_ref=got.at[kind + flip * 2 * halves, j],
            send_sem=feat_send.at[0],
            recv_sem=feat_recv.at[2 * kind + offsets[j][0] + flip * (4 * halves - h - 1)],
            device_id=((near_x(j) + flip * half_gx) % gx, near_y(j)),
            device_id_type=MESH,
        )

    def extra_copy(w, j):
        return pltpu.make_async_remote_copy(
            src_ref=extra.at[near_index(j), w],
            dst_ref=got_extra.at[1 - w, j],
            send_sem=extra_send.at[0],
            recv_sem=extra_recv.at[offsets[j][0] if w else 3],
            device_id=near_place(j),
            device_id_type=MESH,
        )

    def direct_extra_copy(j):
        return pltpu.make_async_remote_copy(
            src_ref=extra.at[near_index(j), 1],
            dst_ref=got_extra.at[2, j],
            send_sem=extra_send.at[1],
            recv_sem=extra_recv.at[2],
            device_id=far_place(j),
            device_id_type=MESH,
        )

    groups = total_bricks // LANES
    wide = slots * LANES
    inputs[0].wait()
    listed = lists_ref[...]
    offset = listed - slots * lax.broadcasted_iota(jnp.int32, listed.shape, 1)
    offset = jnp.where(listed >= 0, offset, -1)
    hits = jnp.concatenate(
        [
            jnp.max(jnp.where(offset == d, 1.0, 0.0), axis=0, keepdims=True)
            for d in range(slots)
        ],
        axis=0,
    )
    hits = jnp.concatenate(
        [hits[:, g * LANES : (g + 1) * LANES] for g in range(groups)], axis=0
    ).astype(jnp.bfloat16)
    spread = jnp.where(
        lax.broadcasted_iota(jnp.int32, (LANES, wide), 1) // slots
        == lax.broadcasted_iota(jnp.int32, (LANES, wide), 0),
        1.0,
        0.0,
    ).astype(jnp.bfloat16)
    spread_hits = jnp.dot(hits, spread, preferred_element_type=jnp.float32)
    same = (
        lax.broadcasted_iota(jnp.int32, (slots, wide), 1) % slots
        == lax.broadcasted_iota(jnp.int32, (slots, wide), 0)
    )
    live_rows = jnp.sum(
        jnp.where(same[None], spread_hits.reshape(groups, slots, wide), 0.0), axis=1
    )
    for l in range(slots):
        flat[pl.ds(l, groups, stride=slots), :] = live_rows[:, l * LANES : (l + 1) * LANES]
    inputs[1].wait()
    marked_targets = jnp.where(flat[...] > 0.0, target_ref[...].astype(jnp.float32), UNUSED)
    for k in range(count):
        from_me = (k // near + wings - wing) % wings if wings > 1 else 0
        for h in range(halves):
            row = k * halves + h
            extra[k % near, from_me, h : h + 1] = marked_targets[row : row + 1].astype(jnp.bfloat16)
    for w in range(wings):
        pltpu.make_async_copy(
            extra.at[me % near, w], got_extra.at[1 - w, 0], extra_recv.at[0 if w else 3]
        ).start()

    pl.semaphore_wait(barrier, near - 1 + wing + gives * plane)
    if wings > 1:

        @pl.when(last_wing)
        def _():
            pl.semaphore_signal(ready, inc=1, device_id=partner, device_id_type=MESH)

    for j in range(1, near):
        extra_copy(1, j).start()

    @pl.when(gives == 1)
    def _():
        for j in range(plane, near):
            direct_extra_copy(j).start()

    for h in range(halves):
        for j in range(1, near):
            feat_copy(1, h, j).start()
    for j in range(1, near):
        extra_copy(0, j).start()
    for h in range(halves):
        for j in range(1, near):
            feat_copy(0, h, j).start()
    voxel_copy.wait()
    inputs[2].wait()
    inputs[3].wait()
    square[...] = jnp.zeros_like(square)

    def squares(t, _):
        for u in range(4):
            b = t * 4 + u
            rows = pl.ds(pl.multiple_of(b * feat, feat), feat)
            square[rows, 0:feat] = lax.dot_general(
                voxel[b],
                voxel[b],
                (((1,), (1,)), ((), ())),
                precision=lax.Precision.HIGHEST,
                preferred_element_type=jnp.float32,
            )
        return 0

    lax.fori_loop(0, bricks // 4, squares, 0)

    linked = jnp.where(adjacency_ref[...] >= 0, 1.0, 0.0)
    same_brick = lax.broadcasted_iota(jnp.int32, (bricks, bricks), 0) == lax.broadcasted_iota(
        jnp.int32, (bricks, bricks), 1
    )
    weights = [
        jnp.sum(jnp.where(same_brick, linked[k : k + 1], 0.0), axis=1, keepdims=True)
        for k in range(4)
    ]
    masks = [w > 0.0 for w in weights]
    degree = weights[0] + weights[1] + weights[2] + weights[3]

    span_all = chunk * LANES
    owner = (lax.broadcasted_iota(jnp.int32, (1, span_all), 1) // slots) % per_half
    across = [jnp.where(owner % side == j, 1.0, 0.0).astype(jnp.bfloat16) for j in range(side)]
    along = owner // side == lax.broadcasted_iota(jnp.int32, (16, span_all), 0)

    def arrived(ref, sem):
        return pltpu.make_async_remote_copy(
            src_ref=ref,
            dst_ref=ref,
            send_sem=feat_send.at[0],
            recv_sem=sem,
            device_id=near_place(1),
            device_id_type=MESH,
        )

    def absorb(kind, p, w, h, role):
        first_slot = p * plane
        slots_of = pl.ds(first_slot, plane)
        sem = 8 + h if kind >= 2 * halves else 2 * kind + p
        arrived(got.at[kind, slots_of], feat_recv.at[sem]).wait_recv()

        def some(g, _):
            mine = [first_slot + g * chunk + u for u in range(chunk)]
            x = jnp.concatenate([got[kind, u] for u in mine], axis=1)
            target = jnp.concatenate(
                [got_extra[role, u].astype(jnp.float32)[h : h + 1] for u in mine], axis=1
            )
            live = jnp.where(along & (target < UNUSED), 1.0, 0.0)
            marked = live * target
            left = jnp.concatenate(
                [x * live[i : i + 1].astype(jnp.bfloat16) for i in range(tall)]
                + [marked.astype(jnp.bfloat16)],
                axis=0,
            )
            right = jnp.concatenate([x * mask for mask in across], axis=0)
            found = lax.dot_general(
                left, right, (((1,), (1,)), ((), ())), preferred_element_type=jnp.float32
            )
            acc[w, h * LANES : (h + 1) * LANES, :] += found[:LANES]
            gather[w, h * tall : (h + 1) * tall, :] += found[LANES : LANES + tall]
            return 0

        if plane == chunk:
            some(0, 0)
        else:
            lax.fori_loop(0, plane // chunk, some, 0)

    def far_copy(source, target, e, arrival):
        return pltpu.make_async_remote_copy(
            src_ref=source,
            dst_ref=target,
            send_sem=far_send.at[e],
            recv_sem=far_recv.at[arrival],
            device_id=partner,
            device_id_type=MESH,
        )

    tiles = feat // SUBLANES
    middle = tiles // 2
    in_block = lax.broadcasted_iota(jnp.int32, (SUBLANES, LANES), 1) % feat
    lane_block = lax.broadcasted_iota(jnp.int32, (1, LANES), 1) // feat

    def pack(h):
        found = []
        for i in range(0, tall, 2):
            rows = [
                [
                    acc[1, pl.ds(h * LANES + (i + k) * feat + r * SUBLANES, SUBLANES), :]
                    for r in range(tiles)
                ]
                for k in range(2)
            ]
            found = found + [rows[0][0], rows[1][0]]
            for k in range(2):
                for r in range(1, middle):
                    turned = pltpu.roll(rows[k][tiles - r], r * SUBLANES, 1)
                    found.append(jnp.where(in_block >= r * SUBLANES, rows[k][r], turned))
            turned = pltpu.roll(rows[1][middle], middle * SUBLANES, 1)
            found.append(jnp.where(in_block >= middle * SUBLANES, rows[0][middle], turned))
        packed = jnp.concatenate(found, axis=0)
        acc_sent[h * packed.shape[0] : (h + 1) * packed.shape[0], :] = packed

    def unpack_far(h):
        upper, above = [], []
        each = tiles + 1
        for i in range(0, tall, 2):
            start = (h * tall // 2 + i // 2) * each
            given = [
                acc_far[pl.ds((start + r) * SUBLANES, SUBLANES), :] for r in range(each)
            ]
            for k in range(2):
                rows = [given[k]] + [None] * (tiles - 1)
                for r in range(1, middle):
                    both = given[2 + k * (middle - 1) + r - 1]
                    rows[r] = both
                    rows[tiles - r] = pltpu.roll(both, LANES - r * SUBLANES, 1)
                last_tile = given[each - 1]
                rows[middle] = (
                    pltpu.roll(last_tile, LANES - middle * SUBLANES, 1) if k else last_tile
                )
                for r in range(tiles):
                    upper.append(jnp.where(in_block >= r * SUBLANES, rows[r], 0.0))
                    above.append(jnp.where(in_block >= (r + 1) * SUBLANES, rows[r], 0.0))
        turned = jnp.concatenate(above, axis=0).T
        below = []
        for i in range(tall):
            mine = jnp.zeros((feat, LANES), jnp.float32)
            for j in range(side):
                band = turned[j * feat : (j + 1) * feat]
                if i != j:
                    band = pltpu.roll(band, (j - i) % side * feat, 1)
                mine = jnp.where(lane_block == j, band, mine)
            below.append(mine)
        rows = slice(h * LANES, (h + 1) * LANES)
        acc[0, rows, :] += jnp.concatenate(upper, axis=0) + jnp.concatenate(below, axis=0)

    def far_moments(h):
        half = acc_sent.shape[0] // halves
        rows = pl.ds(h * half, half)
        return far_copy(acc_sent.at[rows], acc_far.at[rows], 0, 1 + h)

    far_gather = far_copy(gather.at[1], gather_far, 1, 0)
    all_far_moments = far_copy(acc_sent, acc_far, 0, 1)

    def extras_arrived(role, p, count_of, e):
        arrived(got_extra.at[role, pl.ds(p * plane, count_of)], extra_recv.at[e]).wait_recv()

    extras_arrived(0, 0, plane, 0)

    extras_arrived(0, 1, plane, 1)

    for h in range(halves):
        absorb(h, 0, 1, h, 0)

        if h in DIRECT:

            @pl.when(relays == 1)
            def _():
                absorb(h, 1, 1, h, 0)

        else:
            absorb(h, 1, 1, h, 0)

        if h == 0:

            @pl.when(first_wing)
            def _():
                pl.semaphore_wait(ready, 1)

        if h + 1 == halves:
            far_gather.start()
        pack(h)

        @pl.when(last_wing)
        def _():
            far_moments(h).start()

        if h + 1 < halves or not HOLD_BACK:

            @pl.when(first_wing)
            def _():
                far_moments(h).start()

    def absorb_direct():
        @pl.when(takes == 1)
        def _():
            extras_arrived(2, 1, plane, 2)
            for h in DIRECT:
                absorb(2 * halves + h, 1, 0, h, 2)

    if not DIRECT_LAST:
        absorb_direct()
    extras_arrived(1, 0, near, 3)
    for h in range(halves):
        for p in range(2):
            absorb(halves + h, p, 0, h, 1)
        if HOLD_BACK and h == 0:

            @pl.when(first_wing)
            def _():
                far_moments(halves - 1).start()

    if DIRECT_LAST:
        absorb_direct()

    def unpack(ref, rows):
        for e in range(side):
            turned = rows if e == 0 else pltpu.roll(rows, LANES - e * feat, 1)
            ref[pl.ds(e, bricks // side, stride=side), :] = turned

    found_gather = gather[0]
    if wings > 1:
        far_gather.wait_recv()
        found_gather = found_gather + gather_far[...]
    unpack(g_ref, found_gather)

    eye = lax.broadcasted_iota(jnp.int32, (1, feat, LANES), 1) == lax.broadcasted_iota(
        jnp.int32, (1, feat, LANES), 2
    )
    chunks = bricks // CHUNK
    in_feat = lax.broadcasted_iota(jnp.int32, (bricks, LANES), 1) < feat

    def at(t):
        return pl.ds(pl.multiple_of(t * CHUNK, CHUNK), CHUNK)

    def block(ref, t):
        rows = pl.ds(pl.multiple_of(t * CHUNK * feat, CHUNK * feat), CHUNK * feat)
        return ref[rows, :].reshape(CHUNK, feat, LANES)

    def as_column(rows):
        return jnp.sum(jnp.where(eye, rows[:, None, :], 0.0), axis=2, keepdims=True)

    def gathered(t):
        return as_column(g_ref[at(t), :])

    def moments_times(step, part_of):
        for t in part_of:
            z_column = as_column(z_ref[step, at(t), :]).reshape(CHUNK // side, side, feat, 1)
            spread_column = z_column[:, 0]
            for e in range(1, side):
                spread_column = jnp.where(lane_block == e, z_column[:, e], spread_column)
            rows = CHUNK // side * feat
            packed = acc[0, t * rows : (t + 1) * rows, :].reshape(CHUNK // side, feat, LANES)
            mz_ref[t * (CHUNK // side) : (t + 1) * (CHUNK // side), :] = jnp.sum(
                packed * spread_column, axis=1
            )

    here = [ix > 0, ix < gx - 1, iy > 0, iy < gy - 1]
    beside = [(ix - 1, iy), (ix + 1, iy), (ix, iy - 1), (ix, iy + 1)]

    def halo_copy(step, k):
        if k < 2:
            source = z_ref.at[step, pl.ds(k * (bricks - BY), BY)]
            target = halo.at[step, k ^ 1, pl.ds(0, BY)]
        else:
            source = y_send.at[step, k - 2]
            target = halo.at[step, k ^ 1]
        return pltpu.make_async_remote_copy(
            src_ref=source,
            dst_ref=target,
            send_sem=halo_send.at[k],
            recv_sem=halo_recv.at[step % 2, k ^ 1],
            device_id=beside[k],
            device_id_type=MESH,
        )

    def halo_arrived(step, k):
        return pltpu.make_async_remote_copy(
            src_ref=halo.at[step, k, pl.ds(0, BY if k < 2 else BX)],
            dst_ref=halo.at[step, k, pl.ds(0, BY if k < 2 else BX)],
            send_sem=halo_send.at[k],
            recv_sem=halo_recv.at[step % 2, k],
            device_id=beside[k],
            device_id_type=MESH,
        )

    def send_halos(step, ks):
        for k in ks:

            @pl.when(here[k])
            def _():
                halo_copy(step, k).start()

    def produce(step, make):
        for t in (0, chunks - 1):
            z_ref[step, at(t), :] = make(t)
        send_halos(step, (0, 1))
        for t in range(1, chunks - 1):
            z_ref[step, at(t), :] = make(t)
        for e in range(2):
            y_send[step, e] = z_ref[step, pl.ds(e * (BY - 1), BX, stride=BY), :]
        send_halos(step, (2, 3))

    produce(0, lambda t: jnp.sum(block(square, t) * gathered(t), axis=1))

    def part_copy(j):
        a, b = divmod(j, gy)
        return pltpu.make_async_remote_copy(
            src_ref=part,
            dst_ref=parts.at[j],
            send_sem=part_send.at[0],
            recv_sem=part_recv.at[0],
            device_id=(all_rows_at[a], across_at[b]),
            device_id_type=MESH,
        )

    def sent(ref, sem):
        pltpu.make_async_remote_copy(
            src_ref=ref,
            dst_ref=ref,
            send_sem=sem,
            recv_sem=part_recv.at[0],
            device_id=near_place(1),
            device_id_type=MESH,
        ).wait_send()

    def fold(values):
        total = jnp.sum(values, axis=0, keepdims=True)
        width = total.shape[1]
        return sum(total[:, c : c + LANES] for c in range(0, width, LANES))

    def next_basis(step, t):
        if step == 0:
            return jnp.sum(voxel[at(t)] * gathered(t), axis=1)
        back = jnp.sum(voxel[at(t)] * as_column(mid_ref[at(t), :]), axis=1)
        shifted = (reg_ref[at(t), :] - SHIFTS[step - 1]) * basis[step - 1, at(t), :]
        return SCALE * (back + shifted)

    def operate(step):
        def widen(t, _):
            made = next_basis(step, t)
            basis[step, at(t), :] = made
            if step + 1 < ITERS:
                weighted = reg_ref[at(t), :] * made
                column = jnp.sum(voxel[at(t)] * weighted[:, None, :], axis=2, keepdims=True)
                q_ref[at(t), :] = jnp.sum(jnp.where(eye, column, 0.0), axis=1)
            return 0

        lax.fori_loop(0, chunks, widen, 0)
        each = chunks // halves
        for h in range(halves):
            if step == 0:
                far_moments(h).wait_recv()
                unpack_far(h)
            moments_times(step, range(h * each, (h + 1) * each))
        unpack(my_ref, mz_ref[...])
        z = z_ref[step]
        ym_ref[1:bricks, :] = z[: bricks - 1]
        yp_ref[0 : bricks - 1, :] = z[1:]
        found = []
        if step + 1 == ITERS:
            found = [fold(basis[a] * basis[b]) for a, b in early]
            final = (reg_ref[...] - SHIFTS[step]) * basis[step]
            found = found + [fold(basis[a] * final) for a, b in late]
        for k in range(4):

            @pl.when(here[k])
            def _():
                halo_arrived(step, k).wait_recv()
                halo_copy(step, k).wait_send()

        xm = jnp.concatenate([halo[step, 0][:BY], z[: bricks - BY]], axis=0)
        xp = jnp.concatenate([z[BY:], halo[step, 1][:BY]], axis=0)
        ym_ref[pl.ds(0, BX, stride=BY), :] = halo[step, 2]
        yp_ref[pl.ds(BY - 1, BX, stride=BY), :] = halo[step, 3]
        near = jnp.where(masks[0], xm, 0.0) + jnp.where(masks[1], xp, 0.0)
        near = near + jnp.where(masks[2], ym_ref[...], 0.0) + jnp.where(masks[3], yp_ref[...], 0.0)
        mid = jnp.where(in_feat, my_ref[...] + coupling_weight * (degree * z - near), 0.0)
        mid_ref[...] = mid

        if step + 1 < ITERS:

            def advance(t):
                back = jnp.sum(block(square, t) * as_column(mid_ref[at(t), :]), axis=1)
                shifted = q_ref[at(t), :] - SHIFTS[step] * z_ref[step, at(t), :]
                return SCALE * (back + shifted)

            produce(step + 1, advance)
        else:
            for e, (a, b) in enumerate(late):
                e += len(early)
                found[e] = SCALE * (found[e] + fold(z_ref[a] * mid))
        return found

    early = [(a, b) for a in range(ITERS) for b in range(a, ITERS)]
    late = [(a, ITERS) for a in range(ITERS)]
    pairs = early + late
    rows = []
    for step in range(ITERS):
        rows = operate(step)
    rows = rows + [jnp.zeros_like(rows[0])] * (-len(rows) % 8)
    sums = jnp.sum(jnp.concatenate(rows, axis=0), axis=1, keepdims=True)
    entry = lax.broadcasted_iota(jnp.int32, (len(rows), LANES), 1)
    diagonal = entry == lax.broadcasted_iota(jnp.int32, (len(rows), LANES), 0)
    mine = jnp.sum(jnp.where(diagonal, sums, 0.0), axis=0, keepdims=True)
    part[...] = mine
    parts[0] = mine

    for j in part_order:
        part_copy(j).start()

    def last(t, _):
        basis[ITERS, at(t), :] = next_basis(ITERS, t)
        return 0

    lax.fori_loop(0, chunks, last, 0)

    sent(got.at[pl.ds(0, 2 * halves), pl.ds(1, near - 1)], feat_send.at[0])
    sent(got_extra.at[pl.ds(0, 2), pl.ds(1, near - 1)], extra_send.at[0])

    @pl.when(gives == 1)
    def _():
        sent(got_extra.at[2, pl.ds(plane, plane)], extra_send.at[1])

    if wings > 1:
        far_gather.wait_send()
        all_far_moments.wait_send()
    others = parts.at[pl.ds(1, count - 1)]
    sent(others, part_send.at[0])
    arrived(others, part_recv.at[0]).wait_recv()
    total = jnp.sum(parts[...], axis=0)
    spread_total = jnp.sum(
        jnp.where(diagonal, jnp.broadcast_to(total, diagonal.shape), 0.0), axis=1, keepdims=True
    )
    gram = {}
    for e, (a, b) in enumerate(pairs):
        gram[a, b] = gram[b, a] = spread_total[e : e + 1]

    def inner(left, right):
        terms = [
            left[a] * right[b] * gram[a, b] for a in range(len(left)) for b in range(len(right))
        ]
        return functools.reduce(lambda p, q: p + q, terms)

    def apply(coefficients):
        size = len(coefficients)
        out = [SHIFTS[k] * coefficients[k] for k in range(size)]
        out.append(coefficients[-1] * (1.0 / SCALE))
        for k in range(1, size):
            out[k] = out[k] + coefficients[k - 1] * (1.0 / SCALE)
        return out

    one = jnp.ones((1, 1), jnp.float32)
    res, direction, answer = [one], [one], []
    norm_now = gram[0, 0]
    for step in range(ITERS):
        before_answer, before_res = answer, res
        image = apply(direction)
        alpha = norm_now / inner(direction, image)
        padded = answer + [jnp.zeros_like(one)] * (len(direction) - len(answer))
        answer = [p + alpha * d for p, d in zip(padded, direction)]
        res = [p - alpha * w for p, w in zip(res + [jnp.zeros_like(one)], image)]
        if step + 1 < ITERS:
            norm_next = inner(res, res)
            ratio = norm_next / norm_now
            direction = [
                p + ratio * d for p, d in zip(res, direction + [jnp.zeros_like(one)])
            ]
            norm_now = norm_next
    def combine(coefficients):
        return functools.reduce(
            lambda p, q: p + q, [c * basis[k] for k, c in enumerate(coefficients)]
        )

    answer_ref[...] = combine(before_answer)
    res_ref[...] = combine(before_res)
    direction_ref[...] = combine(direction)
    image_ref[...] = combine(image)
    alpha_ref[...] = jnp.broadcast_to(alpha, alpha_ref.shape)


def shards(gx, gy, point_feats, point_targets, point_lists, brick_adjacency, voxel_feats, voxel_reg):
    feat = point_feats.shape[0]
    brick_total, slots = point_lists.shape
    bricks, _, vox = voxel_feats.shape
    count = gx * gy
    cols = bricks * slots
    wings = WINGS
    halves = cols // LANES
    kept = bricks * feat * (feat + SUBLANES) // 2 // LANES
    near = count // wings
    vmem = pl.BlockSpec(memory_space=pltpu.VMEM)
    hbm = pl.BlockSpec(memory_space=pltpu.HBM)
    f32 = jnp.float32
    answer, res, direction, image, alpha = pl.pallas_call(
        functools.partial(kernel, gx, gy),
        out_shape=(pltpu.VMEM((bricks, vox), f32),) * 4 + (pltpu.VMEM((1, vox), f32),),
        in_specs=[hbm] * 6,
        out_specs=(vmem,) * 5,
        scratch_shapes=[
            pltpu.VMEM((3 * halves, near, feat, LANES), jnp.bfloat16),
            pltpu.VMEM((3, near, halves, LANES), jnp.bfloat16),
            pltpu.VMEM((near, wings, cols // LANES, LANES), jnp.bfloat16),
            pltpu.VMEM((kept, LANES), f32),
            pltpu.VMEM((kept, LANES), f32),
            pltpu.VMEM((bricks * feat // LANES, LANES), f32),
            pltpu.VMEM((count * cols // LANES, LANES), f32),
            pltpu.VMEM((bricks, feat, vox), f32),
            pltpu.VMEM((wings, bricks * feat * feat // LANES, LANES), f32),
            pltpu.VMEM((wings, bricks * feat // LANES, LANES), f32),
            pltpu.VMEM((bricks * feat // LANES, LANES), f32),
            pltpu.VMEM((bricks, LANES), f32),
            pltpu.VMEM((bricks * feat, LANES), f32),
            pltpu.VMEM((ITERS + 1, bricks, vox), f32),
            pltpu.VMEM((ITERS, bricks, LANES), f32),
            pltpu.VMEM((bricks, LANES), f32),
            pltpu.VMEM((bricks, LANES), f32),
            pltpu.VMEM((bricks, LANES), f32),
            pltpu.VMEM((bricks, LANES), f32),
            pltpu.VMEM((bricks, LANES), f32),
            pltpu.VMEM((ITERS, 2, BX, LANES), f32),
            pltpu.VMEM((ITERS, 4, 8, LANES), f32),
            pltpu.VMEM((1, LANES), f32),
            pltpu.VMEM((count, 1, LANES), f32),
            pltpu.VMEM((count * cols // LANES, LANES), point_targets.dtype),
            pltpu.VMEM((slots, brick_total), jnp.int32),
            pltpu.VMEM((4, bricks), jnp.int32),
            pltpu.VMEM((bricks, vox), f32),
            pltpu.SemaphoreType.DMA,
            pltpu.SemaphoreType.DMA((4,)),
            pltpu.SemaphoreType.DMA((1,)),
            pltpu.SemaphoreType.DMA((5 * halves,)),
            pltpu.SemaphoreType.DMA((2,)),
            pltpu.SemaphoreType.DMA((4,)),
            pltpu.SemaphoreType.DMA((2,)),
            pltpu.SemaphoreType.DMA((1 + halves,)),
            pltpu.SemaphoreType.DMA((4,)),
            pltpu.SemaphoreType.DMA((2, 4)),
            pltpu.SemaphoreType.DMA((1,)),
            pltpu.SemaphoreType.DMA((1,)),
            pltpu.SemaphoreType.REGULAR,
        ],
        compiler_params=pltpu.CompilerParams(collective_id=0, has_side_effects=True, vmem_limit_bytes=16 * 1024 * 1024),
    )(
        *(
            pltpu.with_memory_space_constraint(x, pltpu.HBM)
            for x in (
                point_feats,
                point_targets.reshape(-1, LANES),
                point_lists.T,
                brick_adjacency.T,
                voxel_feats,
                voxel_reg,
            )
        )
    )
    return answer + alpha * direction, res - alpha * image


def solution(mesh):
    placed = (
        P(None, ("gx", "gy")),
        P(("gx", "gy")),
        P(("gx", "gy"), None),
        P(("gx", "gy"), None),
        P(("gx", "gy"), None, None),
        P(("gx", "gy"), None),
    )
    return jax.shard_map(
        functools.partial(shards, mesh.shape["gx"], mesh.shape["gy"]),
        mesh=mesh,
        in_specs=placed,
        out_specs=(P(("gx", "gy"), None), P(("gx", "gy"), None)),
        check_vma=False,
    )
```

```python
import functools
import math

import jax
import jax.numpy as jnp
from jax import lax
from jax.experimental import pallas as pl
from jax.experimental.pallas import tpu as pltpu
from jax.sharding import PartitionSpec as P

BX = 8
BY = 4
ITERS = 3
LANES = 128
SUBLANES = 8
CHUNK = 8
MESH = pl.DeviceIdType.MESH
STRIDE = 11
SCALE = 2.0**-8
WINGS = 2
HOLD_BACK = True
DIRECT_LAST = True
DIRECT = (0,)
UNUSED = 256.0
SHIFTS = (8.0, 1.0, 4.0)

coupling_weight = 1.0


def kernel(
    gx,
    gy,
    feats_hbm,
    target_hbm,
    lists_hbm,
    adjacency_hbm,
    voxel_hbm,
    reg_hbm,
    answer_ref,
    res_ref,
    direction_ref,
    image_ref,
    alpha_ref,
    got,
    got_extra,
    extra,
    acc_sent,
    acc_far,
    gather_far,
    flat,
    voxel,
    acc,
    gather,
    mz_ref,
    g_ref,
    square,
    basis,
    z_ref,
    q_ref,
    my_ref,
    mid_ref,
    ym_ref,
    yp_ref,
    y_send,
    halo,
    part,
    parts,
    target_ref,
    lists_ref,
    adjacency_ref,
    reg_ref,
    feats_ref,
    feats_sem,
    voxel_sem,
    input_sem,
    feat_send,
    feat_recv,
    extra_send,
    extra_recv,
    far_send,
    far_recv,
    halo_send,
    halo_recv,
    part_send,
    part_recv,
    ready,
):
    count = gx * gy
    ix, iy = lax.axis_index("gx"), lax.axis_index("gy")
    me = ix * gy + iy
    feat = got.shape[2]
    total_bricks, slots = lists_ref.shape[1], lists_ref.shape[0]
    near = got.shape[1]
    wings = WINGS
    wing = me // near
    plane = near // 2
    chunk = math.gcd(plane, CHUNK)
    bricks = reg_ref.shape[0]
    cols = bricks * slots
    halves = cols // LANES
    per_half = LANES // slots
    side = LANES // feat
    tall = per_half // side

    half_gx = gx // wings
    deep = half_gx // 2
    first_x = wing * half_gx
    layer = ix // deep % 2
    inner = (layer + wing) % 2
    gives = inner * wing
    takes = inner * (1 - wing)
    relays = 1 - wing * (1 - inner)
    rows_at = [
        [first_x + (layer + p) % 2 * deep + (ix % deep + a) % deep for a in range(deep)]
        for p in range(2)
    ]
    across_at = [(iy + b) % gy for b in range(gy)]
    all_rows_at = [(ix + a) % gx for a in range(gx)]
    step_by = STRIDE if math.gcd(STRIDE, plane) == 1 else 1
    offsets = [
        (j // plane,) + divmod(j % plane * step_by % plane, gy) for j in range(near)
    ]
    part_order = list(range(count - 1, 0, -1))

    def near_x(j):
        p, a, _ = offsets[j]
        return rows_at[p][a]

    def near_y(j):
        return across_at[offsets[j][2]]

    def near_index(j):
        return (near_x(j) - first_x) * gy + near_y(j)

    def near_place(j):
        return (near_x(j), near_y(j))

    def far_place(j):
        return ((near_x(j) + half_gx) % gx, near_y(j))

    def columns(j, w, h):
        start = ((near_x(j) + w * half_gx) % gx * gy + near_y(j)) * cols + h * LANES
        return pl.ds(pl.multiple_of(start, LANES), LANES)

    barrier = pltpu.get_barrier_semaphore()

    partner = ((ix + half_gx) % gx, iy)
    first_wing = wing == 0
    last_wing = wing == wings - 1

    def greet(j):
        pl.semaphore_signal(barrier, inc=1, device_id=near_place(j), device_id_type=MESH)

    inputs = [
        pltpu.make_async_copy(source, target, input_sem.at[e])
        for e, (source, target) in enumerate(
            [
                (lists_hbm, lists_ref),
                (target_hbm, target_ref),
                (reg_hbm, reg_ref),
                (adjacency_hbm, adjacency_ref),
            ]
        )
    ]
    inputs[0].start()
    inputs[1].start()
    feats_in = pltpu.make_async_copy(feats_hbm, feats_ref, feats_sem)
    feats_in.start()
    for j in range(1, near):
        greet(j)
    if wings > 1:

        @pl.when(first_wing)
        def _():
            pl.semaphore_signal(barrier, inc=1, device_id=partner, device_id_type=MESH)

        @pl.when(takes == 1)
        def _():
            for j in range(plane, near):
                pl.semaphore_signal(
                    barrier, inc=1, device_id=far_place(j), device_id_type=MESH
                )

    inputs[2].start()
    inputs[3].start()
    voxel_copy = pltpu.make_async_copy(voxel_hbm, voxel, voxel_sem)
    voxel_copy.start()
    for h in range(halves):
        for w in range(wings):
            kind = h + (1 - w) * halves
            pltpu.make_async_copy(
                feats_hbm.at[:, columns(0, w, h)], got.at[kind, 0], feat_recv.at[2 * kind]
            ).start()
    halo[...] = jnp.zeros_like(halo)
    acc[...] = jnp.zeros_like(acc)
    gather[...] = jnp.zeros_like(gather)

    def feat_copy(w, h, j):
        flip = gives if w and offsets[j][0] and h in DIRECT else 0
        kind = h + (1 - w) * halves
        return pltpu.make_async_remote_copy(
            src_ref=feats_ref.at[:, columns(j, w, h)],
            dst_ref=got.at[kind + flip * 2 * halves, j],
            send_sem=feat_send.at[0],
            recv_sem=feat_recv.at[2 * kind + offsets[j][0] + flip * (4 * halves - h - 1)],
            device_id=((near_x(j) + flip * half_gx) % gx, near_y(j)),
            device_id_type=MESH,
        )

    def extra_copy(w, j):
        return pltpu.make_async_remote_copy(
            src_ref=extra.at[near_index(j), w],
            dst_ref=got_extra.at[1 - w, j],
            send_sem=extra_send.at[0],
            recv_sem=extra_recv.at[offsets[j][0] if w else 3],
            device_id=near_place(j),
            device_id_type=MESH,
        )

    def direct_extra_copy(j):
        return pltpu.make_async_remote_copy(
            src_ref=extra.at[near_index(j), 1],
            dst_ref=got_extra.at[2, j],
            send_sem=extra_send.at[1],
            recv_sem=extra_recv.at[2],
            device_id=far_place(j),
            device_id_type=MESH,
        )

    groups = total_bricks // LANES
    wide = slots * LANES
    inputs[0].wait()
    listed = lists_ref[...]
    offset = listed - slots * lax.broadcasted_iota(jnp.int32, listed.shape, 1)
    offset = jnp.where(listed >= 0, offset, -1)
    hits = jnp.concatenate(
        [
            jnp.max(jnp.where(offset == d, 1.0, 0.0), axis=0, keepdims=True)
            for d in range(slots)
        ],
        axis=0,
    )
    hits = jnp.concatenate(
        [hits[:, g * LANES : (g + 1) * LANES] for g in range(groups)], axis=0
    ).astype(jnp.bfloat16)
    spread = jnp.where(
        lax.broadcasted_iota(jnp.int32, (LANES, wide), 1) // slots
        == lax.broadcasted_iota(jnp.int32, (LANES, wide), 0),
        1.0,
        0.0,
    ).astype(jnp.bfloat16)
    spread_hits = jnp.dot(hits, spread, preferred_element_type=jnp.float32)
    same = (
        lax.broadcasted_iota(jnp.int32, (slots, wide), 1) % slots
        == lax.broadcasted_iota(jnp.int32, (slots, wide), 0)
    )
    live_rows = jnp.sum(
        jnp.where(same[None], spread_hits.reshape(groups, slots, wide), 0.0), axis=1
    )
    for l in range(slots):
        flat[pl.ds(l, groups, stride=slots), :] = live_rows[:, l * LANES : (l + 1) * LANES]
    inputs[1].wait()
    marked_targets = jnp.where(flat[...] > 0.0, target_ref[...].astype(jnp.float32), UNUSED)
    for k in range(count):
        from_me = (k // near + wings - wing) % wings if wings > 1 else 0
        for h in range(halves):
            row = k * halves + h
            extra[k % near, from_me, h : h + 1] = marked_targets[row : row + 1].astype(jnp.bfloat16)
    for w in range(wings):
        pltpu.make_async_copy(
            extra.at[me % near, w], got_extra.at[1 - w, 0], extra_recv.at[0 if w else 3]
        ).start()

    pl.semaphore_wait(barrier, near - 1 + wing + gives * plane)
    if wings > 1:

        @pl.when(last_wing)
        def _():
            pl.semaphore_signal(ready, inc=1, device_id=partner, device_id_type=MESH)

    for j in range(1, near):
        extra_copy(1, j).start()

    @pl.when(gives == 1)
    def _():
        for j in range(plane, near):
            direct_extra_copy(j).start()

    feats_in.wait()
    for h in range(halves):
        for j in range(1, near):
            feat_copy(1, h, j).start()
    for j in range(1, near):
        extra_copy(0, j).start()
    for h in range(halves):
        for j in range(1, near):
            feat_copy(0, h, j).start()
    voxel_copy.wait()
    inputs[2].wait()
    inputs[3].wait()
    square[...] = jnp.zeros_like(square)

    def squares(t, _):
        for u in range(4):
            b = t * 4 + u
            rows = pl.ds(pl.multiple_of(b * feat, feat), feat)
            square[rows, 0:feat] = lax.dot_general(
                voxel[b],
                voxel[b],
                (((1,), (1,)), ((), ())),
                precision=lax.Precision.HIGHEST,
                preferred_element_type=jnp.float32,
            )
        return 0

    lax.fori_loop(0, bricks // 4, squares, 0)

    linked = jnp.where(adjacency_ref[...] >= 0, 1.0, 0.0)
    same_brick = lax.broadcasted_iota(jnp.int32, (bricks, bricks), 0) == lax.broadcasted_iota(
        jnp.int32, (bricks, bricks), 1
    )
    weights = [
        jnp.sum(jnp.where(same_brick, linked[k : k + 1], 0.0), axis=1, keepdims=True)
        for k in range(4)
    ]
    masks = [w > 0.0 for w in weights]
    degree = weights[0] + weights[1] + weights[2] + weights[3]

    span_all = chunk * LANES
    owner = (lax.broadcasted_iota(jnp.int32, (1, span_all), 1) // slots) % per_half
    across = [jnp.where(owner % side == j, 1.0, 0.0).astype(jnp.bfloat16) for j in range(side)]
    along = owner // side == lax.broadcasted_iota(jnp.int32, (16, span_all), 0)

    def arrived(ref, sem):
        return pltpu.make_async_remote_copy(
            src_ref=ref,
            dst_ref=ref,
            send_sem=feat_send.at[0],
            recv_sem=sem,
            device_id=near_place(1),
            device_id_type=MESH,
        )

    def absorb(kind, p, w, h, role):
        first_slot = p * plane
        slots_of = pl.ds(first_slot, plane)
        sem = 8 + h if kind >= 2 * halves else 2 * kind + p
        arrived(got.at[kind, slots_of], feat_recv.at[sem]).wait_recv()

        def some(g, _):
            mine = [first_slot + g * chunk + u for u in range(chunk)]
            x = jnp.concatenate([got[kind, u] for u in mine], axis=1)
            target = jnp.concatenate(
                [got_extra[role, u].astype(jnp.float32)[h : h + 1] for u in mine], axis=1
            )
            live = jnp.where(along & (target < UNUSED), 1.0, 0.0)
            marked = live * target
            left = jnp.concatenate(
                [x * live[i : i + 1].astype(jnp.bfloat16) for i in range(tall)]
                + [marked.astype(jnp.bfloat16)],
                axis=0,
            )
            right = jnp.concatenate([x * mask for mask in across], axis=0)
            found = lax.dot_general(
                left, right, (((1,), (1,)), ((), ())), preferred_element_type=jnp.float32
            )
            acc[w, h * LANES : (h + 1) * LANES, :] += found[:LANES]
            gather[w, h * tall : (h + 1) * tall, :] += found[LANES : LANES + tall]
            return 0

        if plane == chunk:
            some(0, 0)
        else:
            lax.fori_loop(0, plane // chunk, some, 0)

    def far_copy(source, target, e, arrival):
        return pltpu.make_async_remote_copy(
            src_ref=source,
            dst_ref=target,
            send_sem=far_send.at[e],
            recv_sem=far_recv.at[arrival],
            device_id=partner,
            device_id_type=MESH,
        )

    tiles = feat // SUBLANES
    middle = tiles // 2
    in_block = lax.broadcasted_iota(jnp.int32, (SUBLANES, LANES), 1) % feat
    lane_block = lax.broadcasted_iota(jnp.int32, (1, LANES), 1) // feat

    def pack(h):
        found = []
        for i in range(0, tall, 2):
            rows = [
                [
                    acc[1, pl.ds(h * LANES + (i + k) * feat + r * SUBLANES, SUBLANES), :]
                    for r in range(tiles)
                ]
                for k in range(2)
            ]
            found = found + [rows[0][0], rows[1][0]]
            for k in range(2):
                for r in range(1, middle):
                    turned = pltpu.roll(rows[k][tiles - r], r * SUBLANES, 1)
                    found.append(jnp.where(in_block >= r * SUBLANES, rows[k][r], turned))
            turned = pltpu.roll(rows[1][middle], middle * SUBLANES, 1)
            found.append(jnp.where(in_block >= middle * SUBLANES, rows[0][middle], turned))
        packed = jnp.concatenate(found, axis=0)
        acc_sent[h * packed.shape[0] : (h + 1) * packed.shape[0], :] = packed

    def unpack_far(h):
        upper, above = [], []
        each = tiles + 1
        for i in range(0, tall, 2):
            start = (h * tall // 2 + i // 2) * each
            given = [
                acc_far[pl.ds((start + r) * SUBLANES, SUBLANES), :] for r in range(each)
            ]
            for k in range(2):
                rows = [given[k]] + [None] * (tiles - 1)
                for r in range(1, middle):
                    both = given[2 + k * (middle - 1) + r - 1]
                    rows[r] = both
                    rows[tiles - r] = pltpu.roll(both, LANES - r * SUBLANES, 1)
                last_tile = given[each - 1]
                rows[middle] = (
                    pltpu.roll(last_tile, LANES - middle * SUBLANES, 1) if k else last_tile
                )
                for r in range(tiles):
                    upper.append(jnp.where(in_block >= r * SUBLANES, rows[r], 0.0))
                    above.append(jnp.where(in_block >= (r + 1) * SUBLANES, rows[r], 0.0))
        turned = jnp.concatenate(above, axis=0).T
        below = []
        for i in range(tall):
            mine = jnp.zeros((feat, LANES), jnp.float32)
            for j in range(side):
                band = turned[j * feat : (j + 1) * feat]
                if i != j:
                    band = pltpu.roll(band, (j - i) % side * feat, 1)
                mine = jnp.where(lane_block == j, band, mine)
            below.append(mine)
        rows = slice(h * LANES, (h + 1) * LANES)
        acc[0, rows, :] += jnp.concatenate(upper, axis=0) + jnp.concatenate(below, axis=0)

    def far_moments(h):
        half = acc_sent.shape[0] // halves
        rows = pl.ds(h * half, half)
        return far_copy(acc_sent.at[rows], acc_far.at[rows], 0, 1 + h)

    far_gather = far_copy(gather.at[1], gather_far, 1, 0)
    all_far_moments = far_copy(acc_sent, acc_far, 0, 1)

    def extras_arrived(role, p, count_of, e):
        arrived(got_extra.at[role, pl.ds(p * plane, count_of)], extra_recv.at[e]).wait_recv()

    extras_arrived(0, 0, plane, 0)

    extras_arrived(0, 1, plane, 1)

    for h in range(halves):
        absorb(h, 0, 1, h, 0)

        if h in DIRECT:

            @pl.when(relays == 1)
            def _():
                absorb(h, 1, 1, h, 0)

        else:
            absorb(h, 1, 1, h, 0)

        if h == 0:

            @pl.when(first_wing)
            def _():
                pl.semaphore_wait(ready, 1)

        if h + 1 == halves:
            far_gather.start()
        pack(h)

        @pl.when(last_wing)
        def _():
            far_moments(h).start()

        if h + 1 < halves or not HOLD_BACK:

            @pl.when(first_wing)
            def _():
                far_moments(h).start()

    def absorb_direct():
        @pl.when(takes == 1)
        def _():
            extras_arrived(2, 1, plane, 2)
            for h in DIRECT:
                absorb(2 * halves + h, 1, 0, h, 2)

    if not DIRECT_LAST:
        absorb_direct()
    extras_arrived(1, 0, near, 3)
    for h in range(halves):
        for p in range(2):
            absorb(halves + h, p, 0, h, 1)
        if HOLD_BACK and h == 0:

            @pl.when(first_wing)
            def _():
                far_moments(halves - 1).start()

    if DIRECT_LAST:
        absorb_direct()

    def unpack(ref, rows):
        for e in range(side):
            turned = rows if e == 0 else pltpu.roll(rows, LANES - e * feat, 1)
            ref[pl.ds(e, bricks // side, stride=side), :] = turned

    found_gather = gather[0]
    if wings > 1:
        far_gather.wait_recv()
        found_gather = found_gather + gather_far[...]
    unpack(g_ref, found_gather)

    eye = lax.broadcasted_iota(jnp.int32, (1, feat, LANES), 1) == lax.broadcasted_iota(
        jnp.int32, (1, feat, LANES), 2
    )
    chunks = bricks // CHUNK
    in_feat = lax.broadcasted_iota(jnp.int32, (bricks, LANES), 1) < feat

    def at(t):
        return pl.ds(pl.multiple_of(t * CHUNK, CHUNK), CHUNK)

    def block(ref, t):
        rows = pl.ds(pl.multiple_of(t * CHUNK * feat, CHUNK * feat), CHUNK * feat)
        return ref[rows, :].reshape(CHUNK, feat, LANES)

    def as_column(rows):
        return jnp.sum(jnp.where(eye, rows[:, None, :], 0.0), axis=2, keepdims=True)

    def gathered(t):
        return as_column(g_ref[at(t), :])

    def moments_times(step, part_of):
        for t in part_of:
            z_column = as_column(z_ref[step, at(t), :]).reshape(CHUNK // side, side, feat, 1)
            spread_column = z_column[:, 0]
            for e in range(1, side):
                spread_column = jnp.where(lane_block == e, z_column[:, e], spread_column)
            rows = CHUNK // side * feat
            packed = acc[0, t * rows : (t + 1) * rows, :].reshape(CHUNK // side, feat, LANES)
            mz_ref[t * (CHUNK // side) : (t + 1) * (CHUNK // side), :] = jnp.sum(
                packed * spread_column, axis=1
            )

    here = [ix > 0, ix < gx - 1, iy > 0, iy < gy - 1]
    beside = [(ix - 1, iy), (ix + 1, iy), (ix, iy - 1), (ix, iy + 1)]

    def halo_copy(step, k):
        if k < 2:
            source = z_ref.at[step, pl.ds(k * (bricks - BY), BY)]
            target = halo.at[step, k ^ 1, pl.ds(0, BY)]
        else:
            source = y_send.at[step, k - 2]
            target = halo.at[step, k ^ 1]
        return pltpu.make_async_remote_copy(
            src_ref=source,
            dst_ref=target,
            send_sem=halo_send.at[k],
            recv_sem=halo_recv.at[step % 2, k ^ 1],
            device_id=beside[k],
            device_id_type=MESH,
        )

    def halo_arrived(step, k):
        return pltpu.make_async_remote_copy(
            src_ref=halo.at[step, k, pl.ds(0, BY if k < 2 else BX)],
            dst_ref=halo.at[step, k, pl.ds(0, BY if k < 2 else BX)],
            send_sem=halo_send.at[k],
            recv_sem=halo_recv.at[step % 2, k],
            device_id=beside[k],
            device_id_type=MESH,
        )

    def send_halos(step, ks):
        for k in ks:

            @pl.when(here[k])
            def _():
                halo_copy(step, k).start()

    def produce(step, make):
        for t in (0, chunks - 1):
            z_ref[step, at(t), :] = make(t)
        send_halos(step, (0, 1))
        for t in range(1, chunks - 1):
            z_ref[step, at(t), :] = make(t)
        for e in range(2):
            y_send[step, e] = z_ref[step, pl.ds(e * (BY - 1), BX, stride=BY), :]
        send_halos(step, (2, 3))

    produce(0, lambda t: jnp.sum(block(square, t) * gathered(t), axis=1))

    def part_copy(j):
        a, b = divmod(j, gy)
        return pltpu.make_async_remote_copy(
            src_ref=part,
            dst_ref=parts.at[j],
            send_sem=part_send.at[0],
            recv_sem=part_recv.at[0],
            device_id=(all_rows_at[a], across_at[b]),
            device_id_type=MESH,
        )

    def sent(ref, sem):
        pltpu.make_async_remote_copy(
            src_ref=ref,
            dst_ref=ref,
            send_sem=sem,
            recv_sem=part_recv.at[0],
            device_id=near_place(1),
            device_id_type=MESH,
        ).wait_send()

    def fold(values):
        total = jnp.sum(values, axis=0, keepdims=True)
        width = total.shape[1]
        return sum(total[:, c : c + LANES] for c in range(0, width, LANES))

    def next_basis(step, t):
        if step == 0:
            return jnp.sum(voxel[at(t)] * gathered(t), axis=1)
        back = jnp.sum(voxel[at(t)] * as_column(mid_ref[at(t), :]), axis=1)
        shifted = (reg_ref[at(t), :] - SHIFTS[step - 1]) * basis[step - 1, at(t), :]
        return SCALE * (back + shifted)

    def operate(step):
        def widen(t, _):
            made = next_basis(step, t)
            basis[step, at(t), :] = made
            if step + 1 < ITERS:
                weighted = reg_ref[at(t), :] * made
                column = jnp.sum(voxel[at(t)] * weighted[:, None, :], axis=2, keepdims=True)
                q_ref[at(t), :] = jnp.sum(jnp.where(eye, column, 0.0), axis=1)
            return 0

        lax.fori_loop(0, chunks, widen, 0)
        each = chunks // halves
        for h in range(halves):
            if step == 0:
                far_moments(h).wait_recv()
                unpack_far(h)
            moments_times(step, range(h * each, (h + 1) * each))
        unpack(my_ref, mz_ref[...])
        z = z_ref[step]
        ym_ref[1:bricks, :] = z[: bricks - 1]
        yp_ref[0 : bricks - 1, :] = z[1:]
        found = []
        if step + 1 == ITERS:
            found = [fold(basis[a] * basis[b]) for a, b in early]
            final = (reg_ref[...] - SHIFTS[step]) * basis[step]
            found = found + [fold(basis[a] * final) for a, b in late]
        for k in range(4):

            @pl.when(here[k])
            def _():
                halo_arrived(step, k).wait_recv()
                halo_copy(step, k).wait_send()

        xm = jnp.concatenate([halo[step, 0][:BY], z[: bricks - BY]], axis=0)
        xp = jnp.concatenate([z[BY:], halo[step, 1][:BY]], axis=0)
        ym_ref[pl.ds(0, BX, stride=BY), :] = halo[step, 2]
        yp_ref[pl.ds(BY - 1, BX, stride=BY), :] = halo[step, 3]
        near = jnp.where(masks[0], xm, 0.0) + jnp.where(masks[1], xp, 0.0)
        near = near + jnp.where(masks[2], ym_ref[...], 0.0) + jnp.where(masks[3], yp_ref[...], 0.0)
        mid = jnp.where(in_feat, my_ref[...] + coupling_weight * (degree * z - near), 0.0)
        mid_ref[...] = mid

        if step + 1 < ITERS:

            def advance(t):
                back = jnp.sum(block(square, t) * as_column(mid_ref[at(t), :]), axis=1)
                shifted = q_ref[at(t), :] - SHIFTS[step] * z_ref[step, at(t), :]
                return SCALE * (back + shifted)

            produce(step + 1, advance)
        else:
            for e, (a, b) in enumerate(late):
                e += len(early)
                found[e] = SCALE * (found[e] + fold(z_ref[a] * mid))
        return found

    early = [(a, b) for a in range(ITERS) for b in range(a, ITERS)]
    late = [(a, ITERS) for a in range(ITERS)]
    pairs = early + late
    rows = []
    for step in range(ITERS):
        rows = operate(step)
    rows = rows + [jnp.zeros_like(rows[0])] * (-len(rows) % 8)
    sums = jnp.sum(jnp.concatenate(rows, axis=0), axis=1, keepdims=True)
    entry = lax.broadcasted_iota(jnp.int32, (len(rows), LANES), 1)
    diagonal = entry == lax.broadcasted_iota(jnp.int32, (len(rows), LANES), 0)
    mine = jnp.sum(jnp.where(diagonal, sums, 0.0), axis=0, keepdims=True)
    part[...] = mine
    parts[0] = mine

    for j in part_order:
        part_copy(j).start()

    def last(t, _):
        basis[ITERS, at(t), :] = next_basis(ITERS, t)
        return 0

    lax.fori_loop(0, chunks, last, 0)

    sent(got.at[pl.ds(0, 2 * halves), pl.ds(1, near - 1)], feat_send.at[0])
    sent(got_extra.at[pl.ds(0, 2), pl.ds(1, near - 1)], extra_send.at[0])

    @pl.when(gives == 1)
    def _():
        sent(got_extra.at[2, pl.ds(plane, plane)], extra_send.at[1])

    if wings > 1:
        far_gather.wait_send()
        all_far_moments.wait_send()
    others = parts.at[pl.ds(1, count - 1)]
    sent(others, part_send.at[0])
    arrived(others, part_recv.at[0]).wait_recv()
    total = jnp.sum(parts[...], axis=0)
    spread_total = jnp.sum(
        jnp.where(diagonal, jnp.broadcast_to(total, diagonal.shape), 0.0), axis=1, keepdims=True
    )
    gram = {}
    for e, (a, b) in enumerate(pairs):
        gram[a, b] = gram[b, a] = spread_total[e : e + 1]

    def inner(left, right):
        terms = [
            left[a] * right[b] * gram[a, b] for a in range(len(left)) for b in range(len(right))
        ]
        return functools.reduce(lambda p, q: p + q, terms)

    def apply(coefficients):
        size = len(coefficients)
        out = [SHIFTS[k] * coefficients[k] for k in range(size)]
        out.append(coefficients[-1] * (1.0 / SCALE))
        for k in range(1, size):
            out[k] = out[k] + coefficients[k - 1] * (1.0 / SCALE)
        return out

    one = jnp.ones((1, 1), jnp.float32)
    res, direction, answer = [one], [one], []
    norm_now = gram[0, 0]
    for step in range(ITERS):
        before_answer, before_res = answer, res
        image = apply(direction)
        alpha = norm_now / inner(direction, image)
        padded = answer + [jnp.zeros_like(one)] * (len(direction) - len(answer))
        answer = [p + alpha * d for p, d in zip(padded, direction)]
        res = [p - alpha * w for p, w in zip(res + [jnp.zeros_like(one)], image)]
        if step + 1 < ITERS:
            norm_next = inner(res, res)
            ratio = norm_next / norm_now
            direction = [
                p + ratio * d for p, d in zip(res, direction + [jnp.zeros_like(one)])
            ]
            norm_now = norm_next
    def combine(coefficients):
        return functools.reduce(
            lambda p, q: p + q, [c * basis[k] for k, c in enumerate(coefficients)]
        )

    answer_ref[...] = combine(before_answer)
    res_ref[...] = combine(before_res)
    direction_ref[...] = combine(direction)
    image_ref[...] = combine(image)
    alpha_ref[...] = jnp.broadcast_to(alpha, alpha_ref.shape)


def shards(gx, gy, point_feats, point_targets, point_lists, brick_adjacency, voxel_feats, voxel_reg):
    feat = point_feats.shape[0]
    brick_total, slots = point_lists.shape
    bricks, _, vox = voxel_feats.shape
    count = gx * gy
    cols = bricks * slots
    wings = WINGS
    halves = cols // LANES
    kept = bricks * feat * (feat + SUBLANES) // 2 // LANES
    near = count // wings
    vmem = pl.BlockSpec(memory_space=pltpu.VMEM)
    hbm = pl.BlockSpec(memory_space=pltpu.HBM)
    f32 = jnp.float32
    answer, res, direction, image, alpha = pl.pallas_call(
        functools.partial(kernel, gx, gy),
        out_shape=(pltpu.VMEM((bricks, vox), f32),) * 4 + (pltpu.VMEM((1, vox), f32),),
        in_specs=[hbm] * 6,
        out_specs=(vmem,) * 5,
        scratch_shapes=[
            pltpu.VMEM((3 * halves, near, feat, LANES), jnp.bfloat16),
            pltpu.VMEM((3, near, halves, LANES), jnp.bfloat16),
            pltpu.VMEM((near, wings, cols // LANES, LANES), jnp.bfloat16),
            pltpu.VMEM((kept, LANES), f32),
            pltpu.VMEM((kept, LANES), f32),
            pltpu.VMEM((bricks * feat // LANES, LANES), f32),
            pltpu.VMEM((count * cols // LANES, LANES), f32),
            pltpu.VMEM((bricks, feat, vox), f32),
            pltpu.VMEM((wings, bricks * feat * feat // LANES, LANES), f32),
            pltpu.VMEM((wings, bricks * feat // LANES, LANES), f32),
            pltpu.VMEM((bricks * feat // LANES, LANES), f32),
            pltpu.VMEM((bricks, LANES), f32),
            pltpu.VMEM((bricks * feat, LANES), f32),
            pltpu.VMEM((ITERS + 1, bricks, vox), f32),
            pltpu.VMEM((ITERS, bricks, LANES), f32),
            pltpu.VMEM((bricks, LANES), f32),
            pltpu.VMEM((bricks, LANES), f32),
            pltpu.VMEM((bricks, LANES), f32),
            pltpu.VMEM((bricks, LANES), f32),
            pltpu.VMEM((bricks, LANES), f32),
            pltpu.VMEM((ITERS, 2, BX, LANES), f32),
            pltpu.VMEM((ITERS, 4, 8, LANES), f32),
            pltpu.VMEM((1, LANES), f32),
            pltpu.VMEM((count, 1, LANES), f32),
            pltpu.VMEM((count * cols // LANES, LANES), point_targets.dtype),
            pltpu.VMEM((slots, brick_total), jnp.int32),
            pltpu.VMEM((4, bricks), jnp.int32),
            pltpu.VMEM((bricks, vox), f32),
            pltpu.VMEM(point_feats.shape, point_feats.dtype),
            pltpu.SemaphoreType.DMA,
            pltpu.SemaphoreType.DMA,
            pltpu.SemaphoreType.DMA((4,)),
            pltpu.SemaphoreType.DMA((1,)),
            pltpu.SemaphoreType.DMA((5 * halves,)),
            pltpu.SemaphoreType.DMA((2,)),
            pltpu.SemaphoreType.DMA((4,)),
            pltpu.SemaphoreType.DMA((2,)),
            pltpu.SemaphoreType.DMA((1 + halves,)),
            pltpu.SemaphoreType.DMA((4,)),
            pltpu.SemaphoreType.DMA((2, 4)),
            pltpu.SemaphoreType.DMA((1,)),
            pltpu.SemaphoreType.DMA((1,)),
            pltpu.SemaphoreType.REGULAR,
        ],
        compiler_params=pltpu.CompilerParams(collective_id=0, has_side_effects=True, vmem_limit_bytes=16 * 1024 * 1024),
    )(
        *(
            pltpu.with_memory_space_constraint(x, pltpu.HBM)
            for x in (
                point_feats,
                point_targets.reshape(-1, LANES),
                point_lists.T,
                brick_adjacency.T,
                voxel_feats,
                voxel_reg,
            )
        )
    )
    return answer + alpha * direction, res - alpha * image


def solution(mesh):
    placed = (
        P(None, ("gx", "gy")),
        P(("gx", "gy")),
        P(("gx", "gy"), None),
        P(("gx", "gy"), None),
        P(("gx", "gy"), None, None),
        P(("gx", "gy"), None),
    )
    return jax.shard_map(
        functools.partial(shards, mesh.shape["gx"], mesh.shape["gy"]),
        mesh=mesh,
        in_specs=placed,
        out_specs=(P(("gx", "gy"), None), P(("gx", "gy"), None)),
        check_vma=False,
    )
```
